32 devices in a mesh: edge: 4 (over y, x), tile: 8 (over z, core).
Axes of the slice: x: 2, y: 2, z: 4, core: 2. Of those that a mesh axis runs over, the one named last changes fastest.
Arguments:
- features: bfloat16 [96, 48, 64, 128], P('edge', 'tile'), may hold values from -6 to 6
- hidden_state: bfloat16 [32, 48, 64, 128], P('edge', 'tile'), may hold values from -1 to 1
- edge_source: int32 [32], P('edge'), may hold values from 0 to 23
- edge_owner: int32 [32, 1], P('edge'), may hold values from 0 to 3; in each aligned block of 8 rows (0 to 7, 8 to 15, ...) at most 4 rows name the same one
- edge_target: int32 [32], P('edge'), may hold values from 0 to 23
- edge_counts: int32 [4], P('edge'), may hold values from 4 to 8, as said below
- corr_weight: bfloat16 [49, 128], replicated, may hold values from -0.875 to 0.875
- gate_weight: bfloat16 [3, 3, 256, 256], replicated, may hold values from -0.125 to 0.125
- candidate_weight: bfloat16 [3, 3, 256, 128], replicated, may hold values from -0.125 to 0.125
- jacobian_weight: bfloat16 [128, 24], replicated, may hold values from -0.5 to 0.5
- confidence_weight: bfloat16 [128, 2], replicated, may hold values from -3 to 3
Outputs:
- hidden_next: bfloat16 [32, 48, 64, 128], P('edge', 'tile')
- camera_hessian: float32 [576, 576], P('tile', 'edge')
- pose_diagonal: float32 [96, 36], P('edge')
The draws below stay inside these ranges and needn't reach their ends.
Inputs may be any that keep to these rules, and one draw needn't show every extreme that they name: `edge_owner`: in the rows of one index of edge at most 4 edges name the same owner, a bound that some block reaches. `edge_counts`: edges past a device's count are unused; some index of edge uses all 8.
All inputs are finite; a program needn't handle non-finite values.
Results may differ from the reference program's by a relative error of at most 0.015.
Values may be sent and summed in bfloat16 or wider, within the bound.
A program may use at most 128 MiB of HBM per device.

```python
import math
import jax
import jax.numpy as jnp
import numpy as np
from jax import lax

MAPH = 48
MAPW = 64
CH = 128
HID = 128
WINDOW = 7
FRAMES_DEV = 24
EDGES_DEV = 8
MOST = 4
FRAMES = 96
EDGES = 32
N_EDGE = 4


def draw_edge_counts(key, part):
    devices = EDGES // EDGES_DEV
    first_key, second_key = jax.random.split(jax.random.fold_in(key, 17))
    counts = jax.random.randint(first_key, (devices,), EDGES_DEV // 2, EDGES_DEV + 1)
    fullest = jax.random.randint(second_key, (), 0, devices)
    return jnp.where(jnp.arange(devices) == fullest, EDGES_DEV, counts).astype(jnp.int32)


def plant(entries, key, least, top_value):
    spot = [jax.random.randint(jax.random.fold_in(key, axis), (), 0, length) for axis, length in enumerate(entries.shape)]
    main_axis = entries.shape.index(max(entries.shape))
    beside = spot[:main_axis] + [(spot[main_axis] + 1) % entries.shape[main_axis]] + spot[main_axis + 1:]
    return entries.at[tuple(spot)].set(least).at[tuple(beside)].set(top_value)


def block_levels(rng, extent, shards, low, top_value):
    factor_of = 1.0
    for position, shards_of in shards:
        draws = jax.random.uniform(jax.random.fold_in(jax.random.fold_in(rng, 6), position), (shards_of,), jnp.float32, low / len(shards), top_value / len(shards))
        factor_of = factor_of * jnp.repeat(jnp.exp(draws), extent[position] // shards_of).reshape((-1,) + (1,) * (len(extent) - 1 - position))
    return factor_of


def routed_block(rng, own, number, rows, amount, top, reach, lean):
    ranking = jax.random.permutation(rng, amount)
    crowded, usual = shares(amount, rows * top, reach, lean, True), shares(amount, rows * top, reach, lean, False)
    places = jnp.arange(amount)

    def named(lengths, rotation):
        used = int((lengths > 0).sum())
        fixed = max(1, used // 4)
        passed = fixed + (places - fixed + rotation * (used - fixed)) % max(1, amount - fixed)
        return jnp.zeros((amount,), jnp.int32).at[ranking[jnp.where(places < fixed, places, passed)]].set(jnp.asarray(lengths, jnp.int32))

    lengths = jnp.where(number % 4 == 0, named(crowded, number // 4), named(usual, number - number // 4 - 1))
    mixed = jax.random.permutation(jax.random.fold_in(own, 3), amount)
    source_of, taker = mixed[0:amount // 2 * 2:2], mixed[1:amount // 2 * 2:2]
    margin = jnp.minimum(lengths[source_of] - 1, reach - lengths[taker]) // 2
    margin = jnp.where((source_of == ranking[0]) | (taker == ranking[0]) | (lengths[taker] == 0), 0, jnp.maximum(margin, 0))
    passed = jax.random.randint(jax.random.fold_in(own, 4), (amount // 2,), 0, 1 << 20) % (margin + 1)
    lengths = lengths.at[source_of].add(-passed).at[taker].add(passed)
    labels = jnp.searchsorted(jnp.cumsum(lengths), jnp.arange(rows * top), side="right").astype(jnp.int32)
    table = labels.reshape(top, rows).T
    table = table[jax.random.permutation(jax.random.fold_in(own, 1), rows)]
    rotation = jax.random.randint(jax.random.fold_in(own, 2), (rows, 1), 0, top)
    return jnp.take_along_axis(table, (jnp.arange(top)[None, :] + rotation) % top, axis=1)


def shares(count, total, bound, slope, full):
    loads = [(1 << 20) // math.isqrt(standing ** slope) + 1 for standing in range(1, count + 1)]
    largest = bound if full else min(bound, max(-(-total // count), total * loads[0] // sum(loads)))
    least = 1 if total - largest >= count - 1 else 0
    holding, surplus = [largest] + [least] * (count - 1), total - largest - least * (count - 1)
    while surplus > 0:
        candidates = [i for i in range(1, count) if holding[i] < largest] or [i for i in range(1, count) if holding[i] < bound]
        whole, left = sum([loads[i] for i in candidates]), surplus
        for i in candidates:
            more = min(bound - holding[i], max(1, left * loads[i] // whole), surplus)
            holding[i] = holding[i] + more
            surplus = surplus - more
    return np.array(holding)


def noise(own_key, dims, spread, most, shards=(), kind=jnp.bfloat16):
    loudness = block_levels(own_key, dims, shards, -0.22, 0.18) if shards else 1.0
    array = jax.random.normal(own_key, dims, jnp.float32) * spread * loudness
    return jnp.minimum(jnp.maximum(array, -most), most).astype(kind)


def setup_inputs(seed: int = 0) -> dict:
    seeds = jax.random.split(jax.random.key(seed), 12)
    features = noise(seeds[0], (FRAMES, MAPH, MAPW, CH), 1.0, 6.0, ((0, 4), (1, 8)))
    hidden_state = jnp.clip(jax.random.uniform(seeds[1], (EDGES, MAPH, MAPW, HID), jnp.float32, -1.0, 1.0) * block_levels(seeds[1], (EDGES, MAPH, MAPW, HID), ((0, 4), (1, 8)), -0.4, 0.0), -1.0, 1.0).astype(jnp.bfloat16)
    edge_source = plant(jax.random.randint(seeds[2], (EDGES,), 0, FRAMES_DEV), jax.random.fold_in(seeds[2], 1), 0, FRAMES_DEV - 1).astype(jnp.int32)
    edge_owner_keys = jax.random.split(jax.random.fold_in(seeds[3], 1), EDGES // EDGES_DEV)
    edge_owner_turns = jax.random.permutation(jax.random.fold_in(seeds[3], 3), EDGES // EDGES_DEV)
    edge_owner = jax.vmap(lambda own, number: routed_block(jax.random.fold_in(seeds[3], 2), own, number, EDGES_DEV, N_EDGE, 1, MOST, 1))(edge_owner_keys, edge_owner_turns).reshape((EDGES, 1))
    edge_target = plant(jax.random.randint(seeds[4], (EDGES,), 0, FRAMES_DEV), jax.random.fold_in(seeds[4], 1), 0, FRAMES_DEV - 1).astype(jnp.int32)
    edge_counts = draw_edge_counts(jax.random.fold_in(seeds[11], 71), 0)
    corr_weight = noise(seeds[6], (WINDOW * WINDOW, HID), (WINDOW * WINDOW) ** -0.5, 0.875)
    gate_weight = noise(seeds[7], (3, 3, 2 * HID, 2 * HID), (18 * HID) ** -0.5, 0.125)
    candidate_weight = noise(seeds[8], (3, 3, 2 * HID, HID), (18 * HID) ** -0.5, 0.125)
    jacobian_weight = noise(seeds[9], (HID, 24), HID ** -0.5, 0.5)
    confidence_weight = noise(seeds[10], (HID, 2), 0.5, 3.0)
    return dict(features=features, hidden_state=hidden_state, edge_source=edge_source, edge_owner=edge_owner, edge_target=edge_target, edge_counts=edge_counts, corr_weight=corr_weight, gate_weight=gate_weight, candidate_weight=candidate_weight, jacobian_weight=jacobian_weight, confidence_weight=confidence_weight)


def convolve(padded, weight):
    row_count = padded.shape[0] - 2
    col_count = padded.shape[1] - 2
    running = jnp.zeros((row_count, col_count, weight.shape[-1]), jnp.float32)
    for row_step in range(3):
        for col_step in range(3):
            window = padded[row_step:row_step + row_count, col_step:col_step + col_count].astype(jnp.float32)
            running = running + jnp.einsum('rwc,ck->rwk', window, weight[row_step, col_step].astype(jnp.float32))
    return running


def pad_map(values):
    return jnp.pad(values, ((1, 1), (1, 1), (0, 0)))


def window_corr(source_map, target_map):
    radius = WINDOW // 2
    padded = jnp.pad(target_map, ((radius, radius), (radius, radius), (0, 0)))
    columns = []
    for row_shift in range(WINDOW):
        for col_shift in range(WINDOW):
            moved = padded[row_shift:row_shift + MAPH, col_shift:col_shift + MAPW]
            columns.append(jnp.sum(source_map * moved, axis=-1))
    return jnp.stack(columns, axis=-1) * (CH ** -0.5)


def reference(features, hidden_state, edge_source, edge_owner, edge_target, edge_counts, corr_weight, gate_weight, candidate_weight, jacobian_weight, confidence_weight):
    edge_index = jnp.arange(EDGES, dtype=jnp.int32)
    device_of = edge_index // EDGES_DEV
    in_use = ((edge_index % EDGES_DEV) < edge_counts[device_of]).astype(jnp.float32)
    source_global = (device_of * FRAMES_DEV + edge_source).astype(jnp.int32)
    target_global = (edge_owner[:, 0] * FRAMES_DEV + edge_target).astype(jnp.int32)

    def edge_update(inputs):
        source_frame, target_frame, state, usage = inputs
        source_map = features[source_frame].astype(jnp.float32)
        target_map = features[target_frame].astype(jnp.float32)
        corr = window_corr(source_map, target_map).astype(jnp.bfloat16)
        motion = jax.nn.relu(jnp.einsum('rcd,dk->rck', corr.astype(jnp.float32), corr_weight.astype(jnp.float32))).astype(jnp.bfloat16)
        stacked = jnp.concatenate([state, motion], axis=-1)
        gates = jax.nn.sigmoid(convolve(pad_map(stacked), gate_weight))
        update = gates[..., :HID]
        reset = gates[..., HID:]
        state_float = state.astype(jnp.float32)
        reset_state = (reset * state_float).astype(jnp.bfloat16)
        mixed = jnp.concatenate([reset_state, motion], axis=-1)
        candidate = jnp.tanh(convolve(pad_map(mixed), candidate_weight))
        new_state = ((1.0 - update) * state_float + update * candidate).astype(jnp.bfloat16)
        new_float = new_state.astype(jnp.float32)
        jacobian = jnp.einsum('rwh,hk->krw', new_float, jacobian_weight.astype(jnp.float32)).reshape(2, 12, MAPH * MAPW)
        confidence = jax.nn.softplus(jnp.einsum('rwh,hk->krw', new_float, confidence_weight.astype(jnp.float32))).reshape(2, 1, MAPH * MAPW)
        normal_block = jnp.einsum('kap,kbp->ab', jacobian * confidence, jacobian, precision=lax.Precision.HIGHEST) / (MAPH * MAPW)
        normal_block = normal_block * usage
        kept = jnp.where(usage > 0, new_state, state)
        return kept, normal_block

    hidden_next, normal_blocks = lax.map(edge_update, (source_global, target_global, hidden_state, in_use))
    blocks4 = jnp.zeros((FRAMES, FRAMES, 6, 6), jnp.float32)
    blocks4 = blocks4.at[source_global, source_global].add(normal_blocks[:, :6, :6])
    blocks4 = blocks4.at[source_global, target_global].add(normal_blocks[:, :6, 6:])
    blocks4 = blocks4.at[target_global, source_global].add(normal_blocks[:, 6:, :6])
    blocks4 = blocks4.at[target_global, target_global].add(normal_blocks[:, 6:, 6:])
    frame_index = jnp.arange(FRAMES, dtype=jnp.int32)
    pose_diagonal = blocks4[frame_index, frame_index].reshape(FRAMES, 36)
    blocks4 = blocks4.at[frame_index, frame_index].set(jnp.zeros((FRAMES, 6, 6), jnp.float32))
    camera_hessian = blocks4.transpose(0, 2, 1, 3).reshape(6 * FRAMES, 6 * FRAMES)
    return hidden_next, camera_hessian, pose_diagonal
```

```python
import functools
import types

import jax
import jax.numpy as jnp
from jax import lax
from jax.experimental import pallas as pl
from jax.experimental.pallas import tpu as pltpu
from jax.sharding import PartitionSpec as P

MAPH = 48
WINDOW = 7
RADIUS = WINDOW // 2
NEAR = 2
FAR = RADIUS + NEAR
OWNER, TARGET, SOURCE, COUNT, PLACE, GROUP, REL, ASKS = 0, 8, 16, 24, 32, 40, 48, 64
MESH = pl.DeviceIdType.MESH
BF = jnp.bfloat16
F32 = jnp.float32


def nt(a, b):
    return lax.dot_general(a, b, (((1,), (1,)), ((), ())), preferred_element_type=F32)


def nn(a, b):
    return lax.dot_general(a, b, (((1,), (0,)), ((), ())), preferred_element_type=F32)


def iota(shape, dim):
    return lax.broadcasted_iota(jnp.int32, shape, dim)


def sixth(index):
    return jnp.floor((index.astype(F32) + 0.5) * (1.0 / 6.0))


def one_hot(cond):
    return cond.astype(F32).astype(BF)


def each(count, body):
    def step(i, carry):
        body(i)
        return carry

    lax.fori_loop(0, count, step, 0)


def reach(halo, rows):
    return [min(rows, halo - d * rows) for d in range((halo + rows - 1) // rows)]


def kernel(dims, names, *refs):
    n_edge, n_tile, edges, frames, rows, width, slots = dims
    r = types.SimpleNamespace(**dict(zip(names, refs)))
    band = rows * width
    per = edges // slots
    me = lax.axis_index("edge")
    tile = lax.axis_index("tile")
    texts = [getattr(r, f"text{s}") for s in range(slots)]

    loads = [
        pltpu.make_async_copy(r.feat_h, r.feat, r.l_in.at[0]),
        pltpu.make_async_copy(
            r.hidden_h, r.hext.at[:, pl.ds(NEAR * width, band)], r.l_in.at[1]
        ),
    ]
    fills = []
    for a in range(3):
        for b in range(3):
            at = pl.ds((a * 3 + b) * 128, 128)
            first, second = pl.ds(0, 128), pl.ds(128, 128)
            pairs = (
                (r.gate_w.at[a, b, first], r.wh.at[at]),
                (r.gate_w.at[a, b, second], r.wm.at[at, pl.ds(0, 256)]),
                (r.cand_w.at[a, b, second], r.wm.at[at, pl.ds(256, 128)]),
                (r.cand_w.at[a, b, first], r.wr.at[at]),
            )
            for source, target in pairs:
                fills.append(pltpu.make_async_copy(source, target, r.l_w.at[len(fills)]))
    for load in loads + fills:
        load.start()

    barrier = pltpu.get_barrier_semaphore()
    for rel in range(1, n_edge):
        pl.semaphore_signal(
            barrier, inc=1, device_id=((me + rel) % n_edge, tile), device_id_type=MESH
        )
    for rel in range(1, n_tile):
        pl.semaphore_signal(
            barrier, inc=1, device_id=(me, (tile + rel) % n_tile), device_id_type=MESH
        )

    owner = [r.own_s[0, OWNER + e] for e in range(edges)]
    rel_of = [(owner[e] - me + n_edge) % n_edge for e in range(edges)]
    rank, group = [], []
    for e in range(edges):
        before = jnp.int32(0)
        for k in range(e):
            before = before + (owner[k] == owner[e]).astype(jnp.int32)
        rank.append(jnp.minimum(before, slots - 1))
        group.append(jnp.where(rel_of[e] == 0, 0, rank[e] + 1))
    lane = iota((1, 128), 1)
    row = jnp.where(lane == COUNT, r.own_s[0, COUNT], 0)
    for e in range(edges):
        spot = jnp.int32(0)
        for k in range(edges):
            if k < e:
                spot = spot + (group[k] <= group[e]).astype(jnp.int32)
            elif k > e:
                spot = spot + (group[k] < group[e]).astype(jnp.int32)
        goal = r.own_s[0, TARGET + e]
        fields = (
            (OWNER, owner[e]),
            (TARGET, goal),
            (SOURCE, r.own_s[0, SOURCE + e]),
            (PLACE, jnp.int32(e)),
            (GROUP, group[e]),
            (REL, rel_of[e]),
        )
        for base, value in fields:
            row = jnp.where(lane == base + spot, value, row)
        row = jnp.where(lane == ASKS + rel_of[e] * slots + rank[e], goal, row)
    r.row_v[...] = row
    mine = pltpu.make_async_copy(r.row_v, r.row_s, r.l_row)
    mine.start()
    mine.wait()

    pl.semaphore_wait(barrier, n_edge + n_tile - 2)

    def remote(src, dst, send_sem, recv_sem, edge_id, tile_id):
        return pltpu.make_async_remote_copy(
            src_ref=src,
            dst_ref=dst,
            send_sem=send_sem,
            recv_sem=recv_sem,
            device_id=(edge_id, tile_id),
            device_id_type=MESH,
        )

    def meta_copy(rel):
        return remote(
            r.row_v, r.meta_all.at[me], r.s_meta.at[rel], r.r_meta.at[rel],
            (me + rel) % n_edge, tile,
        )

    for rel in range(1, n_edge):
        meta_copy(rel).start()

    class Halo:
        def __init__(self, halo, buf, source, sems):
            self.halo, self.buf, self.source, self.sems = halo, buf, source, sems
            self.counts = reach(halo, rows)

        def copies(self, e):
            for d, count in enumerate(self.counts):
                far, lines = d + 1, count * width
                s_up, r_up, s_dn, r_dn = self.sems
                up = remote(
                    self.source(e, 0, lines),
                    self.buf.at[e, pl.ds((self.halo + far * rows) * width, lines)],
                    s_up.at[d, e], r_up.at[d, e], me, tile - far,
                )
                dn = remote(
                    self.source(e, band - lines, lines),
                    self.buf.at[e, pl.ds((self.halo - d * rows - count) * width, lines)],
                    s_dn.at[d, e], r_dn.at[d, e], me, tile + far,
                )
                yield tile >= far, tile + far < n_tile, up, dn

        def start(self, e):
            for above, below, up, dn in self.copies(e):
                pl.when(above)(up.start)
                pl.when(below)(dn.start)

        def received(self, e):
            for above, below, up, dn in self.copies(e):
                pl.when(below)(up.wait_recv)
                pl.when(above)(dn.wait_recv)

        def sent(self, e):
            for above, below, up, dn in self.copies(e):
                pl.when(above)(up.wait_send)
                pl.when(below)(dn.wait_send)

        def clear(self):
            for d, count in enumerate(self.counts):
                far, lines = d + 1, count * width
                zero = jnp.zeros((lines, 128), BF)
                top = (self.halo - d * rows - count) * width
                low = (self.halo + far * rows) * width

                @pl.when(tile < far)
                def _():
                    def clear_top(e):
                        self.buf[e, pl.ds(top, lines)] = zero

                    each(edges, clear_top)

                @pl.when(tile + far >= n_tile)
                def _():
                    def clear_low(e):
                        self.buf[e, pl.ds(low, lines)] = zero

                    each(edges, clear_low)

            used = (rows + 2 * self.halo) * width
            spare = self.buf.shape[1] - used
            if spare:

                def clear_pad(e):
                    self.buf[e, pl.ds(used, spare)] = jnp.zeros((spare, 128), BF)

                each(edges, clear_pad)

    def inner(buf, halo):
        return lambda e, at, lines: buf.at[e, pl.ds(halo * width + at, lines)]

    hid = Halo(
        NEAR, r.hext, lambda e, at, lines: r.hidden_h.at[e, pl.ds(at, lines)],
        (r.s_hup, r.r_hup, r.s_hdn, r.r_hdn),
    )
    src = Halo(NEAR, r.sext, inner(r.sext, NEAR), (r.s_sup, r.r_sup, r.s_sdn, r.r_sdn))
    txt = Halo(FAR, r.text, inner(r.text, FAR), (r.s_tup, r.r_tup, r.s_tdn, r.r_tdn))

    each(edges, hid.start)
    r.meta_all[me] = r.row_v[...]
    for rel in range(1, n_edge):
        remote(
            r.row_v, r.meta_all.at[(me - rel + n_edge) % n_edge], r.s_meta.at[rel],
            r.r_meta.at[rel], (me + rel) % n_edge, tile,
        ).wait_recv()
    local = pltpu.make_async_copy(r.meta_all, r.meta_s, r.l_meta)
    local.start()
    loads[0].wait()
    local.wait()

    def feat_copy(rel, s):
        return remote(
            r.send.at[(rel - 1) * slots + s], texts[s].at[rel - 1],
            r.s_feat.at[rel, s], r.r_feat.at[rel, s], (me - rel + n_edge) % n_edge, tile,
        )

    for s in range(slots):
        for rel in range(1, n_edge):
            peer = (me - rel + n_edge) % n_edge
            r.send[(rel - 1) * slots + s] = r.feat[r.meta_s[peer, 0, ASKS + rel * slots + s]]
        for rel in range(1, n_edge):
            feat_copy(rel, s).start()

    def take_source(e):
        r.sext[e, pl.ds(NEAR * width, band)] = r.feat[r.row_s[0, SOURCE + e]]
        src.start(e)

    each(edges, take_source)
    for halo in (hid, src, txt):
        halo.clear()

    far_off = iota((width, 128), 0) - (iota((width, 128), 1) & (width - 1))
    scaled = jnp.where((far_off >= -RADIUS) & (far_off <= RADIUS), 128.0 ** (-0.5), 0.0)
    deep = 8 * width
    column = iota((deep, 128), 0) & 7
    r.fold[...] = one_hot(
        (iota((deep, 128), 1) & 63) == (((8 - column) & 7) << 3) + iota((deep, 128), 0) // width
    )
    spot = iota((128, 64), 0)
    turn = (spot & 63) >> 3
    across = jnp.where(turn > 4, 8 - turn, -turn)
    along = (spot & 7) - (spot >> 6)
    fits = (turn != 4) & (along >= 0) & (along < WINDOW)
    pick = (iota((128, 64), 1) == along * WINDOW + across + RADIUS) & fits
    lookup = jnp.concatenate(
        [r.corr_in[...].astype(F32), jnp.zeros((64 - WINDOW * WINDOW, 128), F32)], axis=0
    ).astype(BF)
    r.corr_w[...] = nn(one_hot(pick), lookup).astype(BF)

    place12 = iota((32, 64), 0)
    which = place12 >> 4
    within = place12 & 15
    name12 = iota((32, 64), 1)
    pick_j = (within < 12) & (name12 == which * 12 + within)
    padded_jac = jnp.concatenate(
        [r.jac_in[...].astype(F32), jnp.zeros((40, 128), F32)], axis=0
    ).astype(BF)
    conf_wide = r.conf_in[...].astype(F32)
    tall = iota((32, 128), 0)
    conf_rows = jnp.where(
        tall < 16,
        jnp.broadcast_to(conf_wide[0:1], (32, 128)),
        jnp.broadcast_to(conf_wide[1:2], (32, 128)),
    )
    r.head_w[...] = jnp.concatenate(
        [nn(one_hot(pick_j), padded_jac), jnp.where((tall & 15) < 12, conf_rows, 0.0)], axis=0
    ).astype(BF)

    def shifted(values, out_rows):
        parts = []
        for q, value in enumerate(values):
            lines = value.shape[0]
            column = iota((lines, 128), 0) & (width - 1)
            wide = value.astype(F32)
            left = jnp.where(column == 0, 0.0, pltpu.roll(wide, 1, 0)).astype(BF)
            right = jnp.where(column == width - 1, 0.0, pltpu.roll(wide, lines - 1, 0)).astype(BF)
            r.x3[q, 0:lines, 0:128] = left
            r.x3[q, 0:lines, 128:256] = value
            r.x3[q, 0:lines, 256:384] = right
        size = out_rows * width
        for q in range(len(values)):
            parts.append(
                jnp.concatenate(
                    [r.x3[q, a * width : a * width + size] for a in range(3)], axis=1
                )
            )
        return jnp.concatenate(parts, axis=0)

    wide_band = (rows + 2) * width

    def state_part(p):
        values = []
        for q in range(per):
            e = p * per + q
            values.append(r.hext[r.row_s[0, PLACE + e]])
        value = nn(shifted(values, rows + 2), r.wh[...])
        for q in range(per):
            r.gpre[p * per + q] = value[q * wide_band : (q + 1) * wide_band]

    loads[1].wait()
    for fill in fills:
        fill.wait()
    each(edges, hid.received)
    each(slots, state_part)
    each(edges, src.received)

    half = (iota((2 * width, 128), 1) >> 6) == iota((2 * width, 128), 0) // width
    pairs_of = (rows + 2 * NEAR + 1) // 2

    def motion_of(e, q):
        for k in range(pairs_of):
            at = 2 * k * width
            table = nt(r.sext[e, pl.ds(at, 2 * width)], r.text[e, pl.ds(at, deep)])
            lines = []
            for par in range(2):
                lines.append(
                    jnp.concatenate(
                        [
                            table[par * width : (par + 1) * width, g * 128 : (g + 1) * 128] * scaled
                            for g in range(deep // 128)
                        ],
                        axis=1,
                    )
                )
            banded = jnp.concatenate(lines, axis=0).astype(BF)
            folded = pltpu.roll(nn(banded, r.fold[...]), 0, 1, stride=8, stride_axis=0)
            value = nn(jnp.where(half, folded, 0.0).astype(BF), r.corr_w[...])
            count = min(2, rows + 2 * NEAR - 2 * k) * width
            r.mext[q, pl.ds(at, count)] = jnp.maximum(value, 0.0).astype(BF)[0:count]

    def update(p):
        for q in range(per):
            txt.received(p * per + q)
        for q in range(per):
            motion_of(p * per + q, q)
        both = nn(shifted([r.mext[q] for q in range(per)], rows + 2), r.wm[...])
        for q in range(per):
            e = p * per + q
            part = both[q * wide_band : (q + 1) * wide_band]
            r.cpre[q] = part[width : width + band, 256:384]
            before = r.gpre[e] + part[:, 0:256]
            r.upd[q] = 0.5 * jnp.tanh(0.5 * before[width : width + band, 0:128]) + 0.5
            reset = 0.5 * jnp.tanh(0.5 * before[:, 128:256]) + 0.5
            state = r.hext[r.row_s[0, PLACE + e], pl.ds(width, wide_band)].astype(F32)
            r.rext[q] = (reset * state).astype(BF)
        mixed = nn(shifted([r.rext[q] for q in range(per)], rows), r.wr[...])
        for q in range(per):
            e = p * per + q
            candidate = jnp.tanh(r.cpre[q] + mixed[q * band : (q + 1) * band])
            gate = r.upd[q]
            place = r.row_s[0, PLACE + e]
            state = r.hext[place, pl.ds(NEAR * width, band)]
            fresh = ((1.0 - gate) * state.astype(F32) + gate * candidate).astype(BF)
            used = (place < r.row_s[0, COUNT]).astype(F32)
            live = jnp.full((band, 128), used) > 0.5
            r.held[e] = jnp.where(live, fresh, state)
            heads = nt(r.head_w[...], fresh)
            jac = heads[0:32]
            weighted = jac * jax.nn.softplus(heads[32:64])
            at16 = pl.ds(pl.multiple_of(e * 16, 16), 16)
            r.jall[at16] = jnp.concatenate([jac[0:16], jac[16:32]], axis=1).astype(BF)
            r.wall[at16] = jnp.concatenate([weighted[0:16], weighted[16:32]], axis=1).astype(BF)

    def take_target(e, upto):
        value = r.feat[r.row_s[0, TARGET + e]]
        at = jnp.maximum(r.row_s[0, REL + e] - 1, 0)
        for s in range(upto + 1):
            value = jnp.where(r.row_s[0, GROUP + e] == s + 1, texts[s][at], value)
        r.text[e, pl.ds(FAR * width, band)] = value
        txt.start(e)

    def stage(p):
        for s in range(slots):

            @pl.when(p == s)
            def _():
                for rel in range(1, n_edge):
                    feat_copy(rel, s).wait_recv()
                for q in range(per):
                    take_target(s * per + q, s)

        pl.when(p > 0)(lambda: update(p - 1))

    each(slots + 1, stage)
    store = pltpu.make_async_copy(r.held, r.out_hidden, r.l_out)
    store.start()

    same = (iota((128, 128), 0) >> 4) == (iota((128, 128), 1) >> 4)
    square = jnp.where(same, nt(r.wall[...], r.jall[...]), 0.0)
    blocks = square[0:16]
    for e in range(1, edges):
        blocks = blocks + square[e * 16 : (e + 1) * 16]
    blocks = blocks * (1.0 / (MAPH * width))
    of = iota((16, 128), 1) >> 4
    for e in range(edges):
        used = (r.row_s[0, PLACE + e] < r.row_s[0, COUNT]).astype(jnp.int32)
        blocks = jnp.where((of == e) & (jnp.full((16, 128), used) == 0), 0.0, blocks)
    r.gpart[...] = blocks

    def tile_copy(rel):
        return remote(
            r.gpart, r.gtile.at[tile], r.s_gt.at[rel], r.r_gt.at[rel], me, (tile + rel) % n_tile
        )

    for rel in range(1, n_tile):
        tile_copy(rel).start()
    r.gtile[tile] = r.gpart[...]
    for rel in range(1, n_tile):
        remote(
            r.gpart, r.gtile.at[(tile - rel + n_tile) % n_tile], r.s_gt.at[rel], r.r_gt.at[rel],
            me, (tile + rel) % n_tile,
        ).wait_recv()
    total = r.gtile[0]
    for k in range(1, n_tile):
        total = total + r.gtile[k]
    r.gsum[...] = total

    def edge_copy(rel):
        return remote(
            r.gsum, r.gall.at[me], r.s_ge.at[rel], r.r_ge.at[rel], (me + rel) % n_edge, tile
        )

    for rel in range(1, n_edge):
        edge_copy(rel).start()
    r.gall[me] = total
    for rel in range(1, n_edge):
        remote(
            r.gsum, r.gall.at[(me - rel + n_edge) % n_edge], r.s_ge.at[rel], r.r_ge.at[rel],
            (me + rel) % n_edge, tile,
        ).wait_recv()

    store.wait()
    for rel in range(1, n_edge):
        meta_copy(rel).wait_send()
        edge_copy(rel).wait_send()
        for s in range(slots):
            feat_copy(rel, s).wait_send()
    for rel in range(1, n_tile):
        tile_copy(rel).wait_send()
    for halo in (hid, src, txt):
        each(edges, halo.sent)


def halves(value):
    high = value.astype(BF)
    return high, (value - high.astype(F32)).astype(BF)


def assemble(dims, meta_s, gall, hidden_h, out_hidden, out_cam, out_diag, held, sem):
    n_edge, n_tile, edges, frames, rows, width, slots = dims
    me = lax.axis_index("edge")
    tile = lax.axis_index("tile")
    fetch = pltpu.make_async_copy(hidden_h, held, sem.at[edges])
    fetch.start()
    cam_rows, cam_cols = out_cam.shape
    row_id = iota((cam_rows, 128), 0) + tile * cam_rows
    col_id = iota((cam_cols, 128), 0) + me * cam_cols
    same = (iota((128, 128), 0) >> 4) == (iota((128, 128), 1) >> 4)
    lane = iota((1, 128), 1)
    inner = lane & 15
    digit = jnp.where(inner < 6, inner, inner - 6)
    lefts, lows, rights = [], [], []
    for j in range(n_edge):
        spots = jnp.full((1, 128), -1, jnp.int32)
        for e in range(edges):
            source = (j * frames + meta_s[j, 0, SOURCE + e]) * 6
            target = (meta_s[j, 0, OWNER + e] * frames + meta_s[j, 0, TARGET + e]) * 6
            here = jnp.where(inner < 6, source, target) + digit
            spots = jnp.where(((lane >> 4) == e) & (inner < 12), here, spots)
        mine = (col_id == spots).astype(F32)
        left = jnp.concatenate([(row_id == spots).astype(F32), mine], axis=0).astype(BF)
        stack = jnp.where(same, jnp.concatenate([gall[j]] * 8, axis=0), 0.0)
        picked = nn(
            jnp.concatenate([left, left], axis=1), jnp.concatenate(halves(stack), axis=0)
        )
        high, low = halves(picked)
        lefts.append(high)
        lows.append(low)
        rights.append(mine.astype(BF))
    placed = nt(jnp.concatenate(lefts + lows, axis=1), jnp.concatenate(rights + rights, axis=1))
    fetch.wait()
    stores = [
        pltpu.make_async_copy(held.at[e], out_hidden.at[meta_s[me, 0, PLACE + e]], sem.at[e])
        for e in range(edges)
    ]
    for store in stores:
        store.start()
    cam = placed[0:cam_rows]
    row_frame = sixth(iota((cam_rows, cam_cols), 0) + tile * cam_rows)
    col_frame = sixth(iota((cam_rows, cam_cols), 1) + me * cam_cols)
    out_cam[...] = jnp.where(row_frame == col_frame, 0.0, cam)
    own = placed[cam_rows:]
    own_row = sixth(iota((cam_cols, cam_cols), 0))
    own_col = sixth(iota((cam_cols, cam_cols), 1))
    own = jnp.where(own_row == own_col, own, 0.0)
    wide_row = iota((cam_cols, 128), 0)
    wide_lane = iota((cam_cols, 128), 1)
    row_in = wide_row.astype(F32) - 6.0 * sixth(wide_row)
    lane_of = sixth(wide_lane)
    lane_in = wide_lane.astype(F32) - 6.0 * lane_of
    gather = one_hot(row_in == lane_in)
    high, low = halves(own)
    spread = jnp.where(row_in == lane_of, nn(high, gather) + nn(low, gather), 0.0)
    fold = one_hot(
        sixth(iota((frames, cam_cols), 1)) == iota((frames, cam_cols), 0).astype(F32)
    )
    high, low = halves(spread)
    out_diag[...] = (nn(fold, high) + nn(fold, low))[:, 0:36]
    for store in stores:
        store.wait()


def per_device(
    features,
    hidden_state,
    edge_source,
    edge_owner,
    edge_target,
    edge_counts,
    corr_weight,
    gate_weight,
    candidate_weight,
    jacobian_weight,
    confidence_weight,
):
    n_edge, n_tile = lax.axis_size("edge"), lax.axis_size("tile")
    edges = hidden_state.shape[0]
    frames, rows, width, chan = features.shape
    slots = max(2, (2 * edges + n_edge - 1) // n_edge)
    assert edges % slots == 0 and edges <= 8 and ASKS + n_edge * slots <= 128
    per = edges // slots
    band = rows * width

    fields = (
        (edge_owner[:, 0], OWNER), (edge_target, TARGET), (edge_source, SOURCE), (edge_counts, COUNT),
    )
    meta = jnp.zeros((1, 128), jnp.int32)
    for field, at in fields:
        meta = meta + jnp.pad(field, (at, 128 - at - field.shape[0]))[None, :]
    dims = (n_edge, n_tile, edges, frames, rows, width, slots)
    even = (rows + 2 * NEAR + 1) // 2 * 2
    dma = pltpu.SemaphoreType.DMA
    vmem = pl.BlockSpec(memory_space=pltpu.VMEM)
    smem = pl.BlockSpec(memory_space=pltpu.SMEM)
    hbm = pl.BlockSpec(memory_space=pl.ANY)

    inputs = (
        ("own_s", meta, smem),
        ("feat_h", features.reshape(frames, band, chan), hbm),
        ("hidden_h", hidden_state.reshape(edges, band, chan), hbm),
        ("corr_in", corr_weight, vmem),
        ("gate_w", gate_weight, hbm),
        ("cand_w", candidate_weight, hbm),
        ("jac_in", jacobian_weight.T, vmem),
        ("conf_in", confidence_weight.T, vmem),
    )
    outputs = (
        ("out_hidden", (edges, band, chan), BF, hbm),
        ("gall", (n_edge, 16, 128), F32, vmem),
        ("meta_all", (n_edge, 1, 128), jnp.int32, vmem),
    )
    near, far = len(reach(NEAR, rows)), len(reach(FAR, rows))
    scratch = {
        "row_v": pltpu.VMEM((1, 128), jnp.int32),
        "row_s": pltpu.SMEM((1, 128), jnp.int32),
        "meta_s": pltpu.SMEM((n_edge, 1, 128), jnp.int32),
        "feat": pltpu.VMEM((frames, band, chan), BF),
        "held": pltpu.VMEM((edges, band, chan), BF),
        "send": pltpu.VMEM(((n_edge - 1) * slots, band, chan), BF),
        "text": pltpu.VMEM((edges, (even + 2 * RADIUS) * width, chan), BF),
        "sext": pltpu.VMEM((edges, even * width, chan), BF),
        "hext": pltpu.VMEM((edges, (rows + 2 * NEAR) * width, chan), BF),
        "mext": pltpu.VMEM((per, (rows + 2 * NEAR) * width, chan), BF),
        "rext": pltpu.VMEM((per, (rows + 2) * width, chan), BF),
        "x3": pltpu.VMEM((per, (rows + 2 * NEAR) * width, 3 * chan), BF),
        "wh": pltpu.VMEM((9 * chan, 2 * chan), BF),
        "wm": pltpu.VMEM((9 * chan, 3 * chan), BF),
        "wr": pltpu.VMEM((9 * chan, chan), BF),
        "fold": pltpu.VMEM((8 * width, 128), BF),
        "corr_w": pltpu.VMEM((128, chan), BF),
        "head_w": pltpu.VMEM((64, chan), BF),
        "gpre": pltpu.VMEM((edges, (rows + 2) * width, 2 * chan), F32),
        "cpre": pltpu.VMEM((per, band, chan), F32),
        "upd": pltpu.VMEM((per, band, chan), F32),
        "jall": pltpu.VMEM((128, 2 * band), BF),
        "wall": pltpu.VMEM((128, 2 * band), BF),
        "gpart": pltpu.VMEM((16, 128), F32),
        "gtile": pltpu.VMEM((n_tile, 16, 128), F32),
        "gsum": pltpu.VMEM((16, 128), F32),
        "l_in": dma((2,)),
        "l_w": dma((36,)),
        "l_row": dma,
        "l_meta": dma,
        "l_out": dma,
        "s_meta": dma((n_edge,)),
        "r_meta": dma((n_edge,)),
        "s_feat": dma((n_edge, slots)),
        "r_feat": dma((n_edge, slots)),
        "s_gt": dma((n_tile,)),
        "r_gt": dma((n_tile,)),
        "s_ge": dma((n_edge,)),
        "r_ge": dma((n_edge,)),
    }
    for s in range(slots):
        scratch[f"text{s}"] = pltpu.VMEM((n_edge - 1, band, chan), BF)
    for key, count in (("h", near), ("s", near), ("t", far)):
        for name in (f"s_{key}up", f"r_{key}up", f"s_{key}dn", f"r_{key}dn"):
            scratch[name] = dma((count, edges))
    names = [i[0] for i in inputs] + [o[0] for o in outputs] + list(scratch)
    state, gall, meta_all = pl.pallas_call(
        functools.partial(kernel, dims, names),
        out_shape=tuple(jax.ShapeDtypeStruct(shape, kind) for _, shape, kind, _ in outputs),
        in_specs=[spec for _, _, spec in inputs],
        out_specs=tuple(spec for _, _, _, spec in outputs),
        scratch_shapes=list(scratch.values()),
        compiler_params=pltpu.CompilerParams(
            collective_id=0, has_side_effects=True, vmem_limit_bytes=56 * 1024 * 1024
        ),
    )(*[value for _, value, _ in inputs])
    hidden_next, cam, diag = pl.pallas_call(
        functools.partial(assemble, dims),
        out_shape=(
            jax.ShapeDtypeStruct((edges, band, chan), BF),
            jax.ShapeDtypeStruct((frames * n_edge * 6 // n_tile, frames * 6), F32),
            jax.ShapeDtypeStruct((frames, 36), F32),
        ),
        in_specs=[smem, vmem, hbm],
        out_specs=(hbm, vmem, vmem),
        scratch_shapes=[pltpu.VMEM((edges, band, chan), BF), dma((edges + 1,))],
    )(meta_all, gall, state)
    return hidden_next.reshape(hidden_state.shape), cam, diag


def solution(mesh):
    placed = (
        P("edge", "tile", None, None),
        P("edge", "tile", None, None),
        P("edge"),
        P("edge", None),
        P("edge"),
        P("edge"),
        P(),
        P(),
        P(),
        P(),
        P(),
    )
    return jax.shard_map(
        per_device,
        mesh=mesh,
        in_specs=placed,
        out_specs=(P("edge", "tile", None, None), P("tile", "edge"), P("edge", None)),
        check_vma=False,
    )
```

```python
import functools
import types

import jax
import jax.numpy as jnp
from jax import lax
from jax.experimental import pallas as pl
from jax.experimental.pallas import tpu as pltpu
from jax.sharding import PartitionSpec as P

MAPH = 48
WINDOW = 7
RADIUS = WINDOW // 2
NEAR = 2
FAR = RADIUS + NEAR
OWNER, TARGET, SOURCE, COUNT, PLACE, GROUP, REL, ASKS = 0, 8, 16, 24, 32, 40, 48, 64
MESH = pl.DeviceIdType.MESH
BF = jnp.bfloat16
F32 = jnp.float32


def nt(a, b):
    return lax.dot_general(a, b, (((1,), (1,)), ((), ())), preferred_element_type=F32)


def nn(a, b):
    return lax.dot_general(a, b, (((1,), (0,)), ((), ())), preferred_element_type=F32)


def iota(shape, dim):
    return lax.broadcasted_iota(jnp.int32, shape, dim)


def sixth(index):
    return jnp.floor((index.astype(F32) + 0.5) * (1.0 / 6.0))


def one_hot(cond):
    return cond.astype(F32).astype(BF)


def each(count, body):
    def step(i, carry):
        body(i)
        return carry

    lax.fori_loop(0, count, step, 0)


def reach(halo, rows):
    return [min(rows, halo - d * rows) for d in range((halo + rows - 1) // rows)]


def kernel(dims, names, *refs):
    n_edge, n_tile, edges, frames, rows, width, slots = dims
    r = types.SimpleNamespace(**dict(zip(names, refs)))
    band = rows * width
    per = edges // slots
    me = lax.axis_index("edge")
    tile = lax.axis_index("tile")
    texts = [getattr(r, f"text{s}") for s in range(slots)]

    loads = [
        pltpu.make_async_copy(r.feat_h, r.feat, r.l_in.at[0]),
        pltpu.make_async_copy(
            r.hidden_h, r.hext.at[:, pl.ds(NEAR * width, band)], r.l_in.at[1]
        ),
    ]
    fills = []
    for a in range(3):
        for b in range(3):
            at = pl.ds((a * 3 + b) * 128, 128)
            first, second = pl.ds(0, 128), pl.ds(128, 128)
            pairs = (
                (r.gate_w.at[a, b, first], r.wh.at[at]),
                (r.gate_w.at[a, b, second], r.wm.at[at]),
                (r.cand_w.at[a, b, first], r.wc.at[pl.ds(b * 128, 128), pl.ds(a * 128, 128)]),
                (r.cand_w.at[a, b, second], r.wc.at[pl.ds(384 + b * 128, 128), pl.ds(a * 128, 128)]),
            )
            for source, target in pairs:
                fills.append(pltpu.make_async_copy(source, target, r.l_w.at[len(fills)]))
    for load in loads + fills:
        load.start()

    barrier = pltpu.get_barrier_semaphore()
    for rel in range(1, n_edge):
        pl.semaphore_signal(
            barrier, inc=1, device_id=((me + rel) % n_edge, tile), device_id_type=MESH
        )
    for rel in range(1, n_tile):
        pl.semaphore_signal(
            barrier, inc=1, device_id=(me, (tile + rel) % n_tile), device_id_type=MESH
        )

    owner = [r.own_s[0, OWNER + e] for e in range(edges)]
    rel_of = [(owner[e] - me + n_edge) % n_edge for e in range(edges)]
    rank, group = [], []
    for e in range(edges):
        before = jnp.int32(0)
        for k in range(e):
            before = before + (owner[k] == owner[e]).astype(jnp.int32)
        rank.append(jnp.minimum(before, slots - 1))
        group.append(jnp.where(rel_of[e] == 0, 0, rank[e] + 1))
    lane = iota((1, 128), 1)
    row = jnp.where(lane == COUNT, r.own_s[0, COUNT], 0)
    for e in range(edges):
        spot = jnp.int32(0)
        for k in range(edges):
            if k < e:
                spot = spot + (group[k] <= group[e]).astype(jnp.int32)
            elif k > e:
                spot = spot + (group[k] < group[e]).astype(jnp.int32)
        goal = r.own_s[0, TARGET + e]
        fields = (
            (OWNER, owner[e]),
            (TARGET, goal),
            (SOURCE, r.own_s[0, SOURCE + e]),
            (PLACE, jnp.int32(e)),
            (GROUP, group[e]),
            (REL, rel_of[e]),
        )
        for base, value in fields:
            row = jnp.where(lane == base + spot, value, row)
        row = jnp.where(lane == ASKS + rel_of[e] * slots + rank[e], goal, row)
    r.row_v[...] = row
    mine = pltpu.make_async_copy(r.row_v, r.row_s, r.l_row)
    mine.start()
    mine.wait()

    pl.semaphore_wait(barrier, n_edge + n_tile - 2)

    def remote(src, dst, send_sem, recv_sem, edge_id, tile_id):
        return pltpu.make_async_remote_copy(
            src_ref=src,
            dst_ref=dst,
            send_sem=send_sem,
            recv_sem=recv_sem,
            device_id=(edge_id, tile_id),
            device_id_type=MESH,
        )

    def meta_copy(rel):
        return remote(
            r.row_v, r.meta_all.at[me], r.s_meta.at[rel], r.r_meta.at[rel],
            (me + rel) % n_edge, tile,
        )

    for rel in range(1, n_edge):
        meta_copy(rel).start()

    class Halo:
        def __init__(self, halo, buf, source, sems):
            self.halo, self.buf, self.source, self.sems = halo, buf, source, sems
            self.counts = reach(halo, rows)

        def copies(self, e):
            for d, count in enumerate(self.counts):
                far, lines = d + 1, count * width
                s_up, r_up, s_dn, r_dn = self.sems
                up = remote(
                    self.source(e, 0, lines),
                    self.buf.at[e, pl.ds((self.halo + far * rows) * width, lines)],
                    s_up.at[d, e], r_up.at[d, e], me, tile - far,
                )
                dn = remote(
                    self.source(e, band - lines, lines),
                    self.buf.at[e, pl.ds((self.halo - d * rows - count) * width, lines)],
                    s_dn.at[d, e], r_dn.at[d, e], me, tile + far,
                )
                yield tile >= far, tile + far < n_tile, up, dn

        def start(self, e):
            for above, below, up, dn in self.copies(e):
                pl.when(above)(up.start)
                pl.when(below)(dn.start)

        def received(self, e):
            for above, below, up, dn in self.copies(e):
                pl.when(below)(up.wait_recv)
                pl.when(above)(dn.wait_recv)

        def sent(self, e):
            for above, below, up, dn in self.copies(e):
                pl.when(above)(up.wait_send)
                pl.when(below)(dn.wait_send)

        def clear(self):
            for d, count in enumerate(self.counts):
                far, lines = d + 1, count * width
                zero = jnp.zeros((lines, 128), BF)
                top = (self.halo - d * rows - count) * width
                low = (self.halo + far * rows) * width

                @pl.when(tile < far)
                def _():
                    def clear_top(e):
                        self.buf[e, pl.ds(top, lines)] = zero

                    each(edges, clear_top)

                @pl.when(tile + far >= n_tile)
                def _():
                    def clear_low(e):
                        self.buf[e, pl.ds(low, lines)] = zero

                    each(edges, clear_low)

            used = (rows + 2 * self.halo) * width
            spare = self.buf.shape[1] - used
            if spare:

                def clear_pad(e):
                    self.buf[e, pl.ds(used, spare)] = jnp.zeros((spare, 128), BF)

                each(edges, clear_pad)

    def inner(buf, halo):
        return lambda e, at, lines: buf.at[e, pl.ds(halo * width + at, lines)]

    hid = Halo(
        NEAR, r.hext, lambda e, at, lines: r.hidden_h.at[e, pl.ds(at, lines)],
        (r.s_hup, r.r_hup, r.s_hdn, r.r_hdn),
    )
    src = Halo(NEAR, r.sext, inner(r.sext, NEAR), (r.s_sup, r.r_sup, r.s_sdn, r.r_sdn))
    txt = Halo(FAR, r.text, inner(r.text, FAR), (r.s_tup, r.r_tup, r.s_tdn, r.r_tdn))

    each(edges, hid.start)
    r.meta_all[me] = r.row_v[...]
    for rel in range(1, n_edge):
        remote(
            r.row_v, r.meta_all.at[(me - rel + n_edge) % n_edge], r.s_meta.at[rel],
            r.r_meta.at[rel], (me + rel) % n_edge, tile,
        ).wait_recv()
    local = pltpu.make_async_copy(r.meta_all, r.meta_s, r.l_meta)
    local.start()
    loads[0].wait()
    local.wait()

    def feat_copy(rel, s):
        return remote(
            r.send.at[(rel - 1) * slots + s], texts[s].at[rel - 1],
            r.s_feat.at[rel, s], r.r_feat.at[rel, s], (me - rel + n_edge) % n_edge, tile,
        )

    for s in range(slots):
        for rel in range(1, n_edge):
            peer = (me - rel + n_edge) % n_edge
            r.send[(rel - 1) * slots + s] = r.feat[r.meta_s[peer, 0, ASKS + rel * slots + s]]
        for rel in range(1, n_edge):
            feat_copy(rel, s).start()

    def take_source(e):
        r.sext[e, pl.ds(NEAR * width, band)] = r.feat[r.row_s[0, SOURCE + e]]
        src.start(e)

    each(edges, take_source)
    for halo in (hid, src, txt):
        halo.clear()

    spot = (iota((128, 64), 0) + 4) & 127
    along = ((spot >> 3) & 3) * 2 + (spot >> 6) - ((spot >> 5) & 1)
    across = WINDOW - 1 - (spot & 7)
    fits = (across >= 0) & (along >= 0) & (along < WINDOW)
    pick = (iota((128, 64), 1) == along * WINDOW + across) & fits
    lookup = jnp.concatenate(
        [r.corr_in[...].astype(F32), jnp.zeros((64 - WINDOW * WINDOW, 128), F32)], axis=0
    ).astype(BF)
    r.corr_w[...] = nn(one_hot(pick), lookup).astype(BF)

    place12 = iota((32, 64), 0)
    which = place12 >> 4
    within = place12 & 15
    name12 = iota((32, 64), 1)
    pick_j = (within < 12) & (name12 == which * 12 + within)
    padded_jac = jnp.concatenate(
        [r.jac_in[...].astype(F32), jnp.zeros((40, 128), F32)], axis=0
    ).astype(BF)
    conf_wide = r.conf_in[...].astype(F32)
    tall = iota((32, 128), 0)
    conf_rows = jnp.where(
        tall < 16,
        jnp.broadcast_to(conf_wide[0:1], (32, 128)),
        jnp.broadcast_to(conf_wide[1:2], (32, 128)),
    )
    r.head_w[...] = jnp.concatenate(
        [nn(one_hot(pick_j), padded_jac), jnp.where((tall & 15) < 12, conf_rows, 0.0)], axis=0
    ).astype(BF)

    def spread(value, out):
        lines = value.shape[0]
        column = iota((lines, 128), 0) & (width - 1)
        wide = value.astype(F32)
        left = jnp.where(column == 0, 0.0, pltpu.roll(wide, 1, 0)).astype(BF)
        right = jnp.where(column == width - 1, 0.0, pltpu.roll(wide, lines - 1, 0)).astype(BF)
        out[0:lines, 0:128] = left
        out[0:lines, 128:256] = value
        out[0:lines, 256:384] = right

    def windows(x3, out_rows):
        size = out_rows * width
        return jnp.concatenate(
            [
                jnp.concatenate([x3[q, a * width : a * width + size] for a in range(3)], axis=1)
                for q in range(per)
            ],
            axis=0,
        )

    wide_band = (rows + 2) * width

    def state_part(p):
        for q in range(per):
            spread(r.hext[r.row_s[0, PLACE + p * per + q]], r.x3.at[q])
        value = nn(windows(r.x3, rows + 2), r.wh[...])
        for q in range(per):
            r.gpre[p * per + q] = value[q * wide_band : (q + 1) * wide_band]

    loads[1].wait()
    for fill in fills:
        fill.wait()
    each(edges, hid.received)
    each(slots, state_part)
    each(edges, src.received)

    lane_w = (iota((width, 128), 1) + 4) & 127
    col_w = iota((width, 128), 0) + RADIUS - (lane_w & 7)
    in_map = (col_w >= 0) & (col_w < width) & ((lane_w & 7) < WINDOW)
    scaled = [
        jnp.where(in_map & (((lane_w >> 5) & 1) == par), 128.0 ** (-0.5), 0.0) for par in range(2)
    ]
    slot_w = (lane_w >> 3) & 3
    pairs_of = (rows + 2 * NEAR + 1) // 2
    quads_of = r.text.shape[1] // (4 * width)

    def motion_of(e, q):
        tables, starts = [], []
        for m in range(quads_of):
            first, last = max(0, 2 * m - 3), min(pairs_of - 1, 2 * m + 1)
            starts.append(first)
            tables.append(
                nt(
                    r.sext[e, pl.ds(2 * first * width, 2 * (last - first + 1) * width)],
                    r.text[e, pl.ds(4 * m * width, 4 * width)],
                )
            )
        lines = []
        for k in range(pairs_of):
            for par in range(2):
                found = None
                for g in range(4):
                    m, h = divmod(k + g, 2)
                    at = (2 * (k - starts[m]) + par) * width
                    piece = tables[m][at : at + width, h * 128 : (h + 1) * 128]
                    moved = pltpu.roll(
                        piece, width + 8 * g + 32 * par, 1, stride=1, stride_axis=0
                    )
                    found = moved if g == 0 else jnp.where(slot_w == g, moved, found)
                lines.append((found * scaled[par]).astype(BF))
        value = nn(jnp.concatenate(lines, axis=0), r.corr_w[...])
        r.mext[q] = jnp.maximum(value, 0.0).astype(BF)

    used_rows = (rows + 2 * NEAR) * width

    def update(p):
        for q in range(per):
            txt.received(p * per + q)
        for q in range(per):
            motion_of(p * per + q, q)
        for q in range(per):
            spread(r.mext[q, 0:used_rows], r.x3.at[q])
        both = nn(windows(r.x3, rows + 2), r.wm[...])
        for q in range(per):
            e = p * per + q
            before = r.gpre[e] + both[q * wide_band : (q + 1) * wide_band]
            r.upd[q] = 0.5 * jnp.tanh(0.5 * before[width : width + band, 0:128]) + 0.5
            reset = 0.5 * jnp.tanh(0.5 * before[:, 128:256]) + 0.5
            state = r.hext[r.row_s[0, PLACE + e], pl.ds(width, wide_band)].astype(F32)
            spread((reset * state).astype(BF), r.x3r.at[q])

        def inputs(first, count):
            first, count = first * width, count * width
            return jnp.concatenate(
                [
                    jnp.concatenate(
                        [
                            r.x3r[q, first : first + count],
                            r.x3[q, width + first : width + first + count],
                        ],
                        axis=1,
                    )
                    for q in range(per)
                ],
                axis=0,
            )

        upper = nn(inputs(0, rows + 1), r.wc[:, 0:256])
        lower = nn(inputs(2, rows), r.wc[:, 256:384])
        for q in range(per):
            e = p * per + q
            at = q * (rows + 1) * width
            mixed = upper[at : at + band, 0:128] + upper[at + width : at + width + band, 128:256]
            candidate = jnp.tanh(mixed + lower[q * band : (q + 1) * band])
            gate = r.upd[q]
            place = r.row_s[0, PLACE + e]
            state = r.hext[place, pl.ds(NEAR * width, band)]
            fresh = ((1.0 - gate) * state.astype(F32) + gate * candidate).astype(BF)
            used = (place < r.row_s[0, COUNT]).astype(F32)
            live = jnp.full((band, 128), used) > 0.5
            r.held[e] = jnp.where(live, fresh, state)
            heads = nt(r.head_w[...], fresh)
            jac = heads[0:32]
            weighted = jac * jax.nn.softplus(heads[32:64])
            at16 = pl.ds(pl.multiple_of(e * 16, 16), 16)
            r.jall[at16] = jnp.concatenate([jac[0:16], jac[16:32]], axis=1).astype(BF)
            r.wall[at16] = jnp.concatenate([weighted[0:16], weighted[16:32]], axis=1).astype(BF)

    flip_row, flip_col = iota((2 * width, 2 * width), 0), iota((2 * width, 2 * width), 1)
    flip = one_hot(
        (flip_row // width == flip_col // width)
        & ((flip_row & (width - 1)) + (flip_col & (width - 1)) == width - 1)
    )

    def take_target(e, upto):
        value = r.feat[r.row_s[0, TARGET + e]]
        at = jnp.maximum(r.row_s[0, REL + e] - 1, 0)
        for s in range(upto + 1):
            value = jnp.where(r.row_s[0, GROUP + e] == s + 1, texts[s][at], value)
        for first in range(0, band, 2 * width):
            count = min(2 * width, band - first)
            r.text[e, pl.ds(FAR * width + first, count)] = nn(
                flip[0:count, 0:count], value[first : first + count]
            ).astype(BF)
        txt.start(e)

    def stage(p):
        for s in range(slots):

            @pl.when(p == s)
            def _():
                for rel in range(1, n_edge):
                    feat_copy(rel, s).wait_recv()
                for q in range(per):
                    take_target(s * per + q, s)

        pl.when(p > 0)(lambda: update(p - 1))

    each(slots + 1, stage)
    store = pltpu.make_async_copy(r.held, r.out_hidden, r.l_out)
    store.start()

    same = (iota((128, 128), 0) >> 4) == (iota((128, 128), 1) >> 4)
    square = jnp.where(same, nt(r.wall[...], r.jall[...]), 0.0)
    blocks = square[0:16]
    for e in range(1, edges):
        blocks = blocks + square[e * 16 : (e + 1) * 16]
    blocks = blocks * (1.0 / (MAPH * width))
    of = iota((16, 128), 1) >> 4
    for e in range(edges):
        used = (r.row_s[0, PLACE + e] < r.row_s[0, COUNT]).astype(jnp.int32)
        blocks = jnp.where((of == e) & (jnp.full((16, 128), used) == 0), 0.0, blocks)
    r.gpart[...] = blocks

    def tile_copy(rel):
        return remote(
            r.gpart, r.gtile.at[tile], r.s_gt.at[rel], r.r_gt.at[rel], me, (tile + rel) % n_tile
        )

    for rel in range(1, n_tile):
        tile_copy(rel).start()
    r.gtile[tile] = r.gpart[...]
    for rel in range(1, n_tile):
        remote(
            r.gpart, r.gtile.at[(tile - rel + n_tile) % n_tile], r.s_gt.at[rel], r.r_gt.at[rel],
            me, (tile + rel) % n_tile,
        ).wait_recv()
    total = r.gtile[0]
    for k in range(1, n_tile):
        total = total + r.gtile[k]
    r.gsum[...] = total

    def edge_copy(rel):
        return remote(
            r.gsum, r.gall.at[me], r.s_ge.at[rel], r.r_ge.at[rel], (me + rel) % n_edge, tile
        )

    for rel in range(1, n_edge):
        edge_copy(rel).start()
    r.gall[me] = total
    for rel in range(1, n_edge):
        remote(
            r.gsum, r.gall.at[(me - rel + n_edge) % n_edge], r.s_ge.at[rel], r.r_ge.at[rel],
            (me + rel) % n_edge, tile,
        ).wait_recv()

    store.wait()
    for rel in range(1, n_edge):
        meta_copy(rel).wait_send()
        edge_copy(rel).wait_send()
        for s in range(slots):
            feat_copy(rel, s).wait_send()
    for rel in range(1, n_tile):
        tile_copy(rel).wait_send()
    for halo in (hid, src, txt):
        each(edges, halo.sent)


def halves(value):
    high = value.astype(BF)
    return high, (value - high.astype(F32)).astype(BF)


def assemble(dims, meta_s, gall, hidden_h, out_hidden, out_cam, out_diag, held, sem):
    n_edge, n_tile, edges, frames, rows, width, slots = dims
    me = lax.axis_index("edge")
    tile = lax.axis_index("tile")
    fetch = pltpu.make_async_copy(hidden_h, held, sem.at[edges])
    fetch.start()
    cam_rows, cam_cols = out_cam.shape
    row_id = iota((cam_rows, 128), 0) + tile * cam_rows
    col_id = iota((cam_cols, 128), 0) + me * cam_cols
    same = (iota((128, 128), 0) >> 4) == (iota((128, 128), 1) >> 4)
    lane = iota((1, 128), 1)
    inner = lane & 15
    digit = jnp.where(inner < 6, inner, inner - 6)
    lefts, lows, rights = [], [], []
    for j in range(n_edge):
        spots = jnp.full((1, 128), -1, jnp.int32)
        for e in range(edges):
            source = (j * frames + meta_s[j, 0, SOURCE + e]) * 6
            target = (meta_s[j, 0, OWNER + e] * frames + meta_s[j, 0, TARGET + e]) * 6
            here = jnp.where(inner < 6, source, target) + digit
            spots = jnp.where(((lane >> 4) == e) & (inner < 12), here, spots)
        mine = (col_id == spots).astype(F32)
        left = jnp.concatenate([(row_id == spots).astype(F32), mine], axis=0).astype(BF)
        stack = jnp.where(same, jnp.concatenate([gall[j]] * 8, axis=0), 0.0)
        picked = nn(
            jnp.concatenate([left, left], axis=1), jnp.concatenate(halves(stack), axis=0)
        )
        high, low = halves(picked)
        lefts.append(high)
        lows.append(low)
        rights.append(mine.astype(BF))
    placed = nt(jnp.concatenate(lefts + lows, axis=1), jnp.concatenate(rights + rights, axis=1))
    fetch.wait()
    stores = [
        pltpu.make_async_copy(held.at[e], out_hidden.at[meta_s[me, 0, PLACE + e]], sem.at[e])
        for e in range(edges)
    ]
    for store in stores:
        store.start()
    cam = placed[0:cam_rows]
    row_frame = sixth(iota((cam_rows, cam_cols), 0) + tile * cam_rows)
    col_frame = sixth(iota((cam_rows, cam_cols), 1) + me * cam_cols)
    out_cam[...] = jnp.where(row_frame == col_frame, 0.0, cam)
    own = placed[cam_rows:]
    own_row = sixth(iota((cam_cols, cam_cols), 0))
    own_col = sixth(iota((cam_cols, cam_cols), 1))
    own = jnp.where(own_row == own_col, own, 0.0)
    wide_row = iota((cam_cols, 128), 0)
    wide_lane = iota((cam_cols, 128), 1)
    row_in = wide_row.astype(F32) - 6.0 * sixth(wide_row)
    lane_of = sixth(wide_lane)
    lane_in = wide_lane.astype(F32) - 6.0 * lane_of
    gather = one_hot(row_in == lane_in)
    high, low = halves(own)
    spread = jnp.where(row_in == lane_of, nn(high, gather) + nn(low, gather), 0.0)
    fold = one_hot(
        sixth(iota((frames, cam_cols), 1)) == iota((frames, cam_cols), 0).astype(F32)
    )
    high, low = halves(spread)
    out_diag[...] = (nn(fold, high) + nn(fold, low))[:, 0:36]
    for store in stores:
        store.wait()


def per_device(
    features,
    hidden_state,
    edge_source,
    edge_owner,
    edge_target,
    edge_counts,
    corr_weight,
    gate_weight,
    candidate_weight,
    jacobian_weight,
    confidence_weight,
):
    n_edge, n_tile = lax.axis_size("edge"), lax.axis_size("tile")
    edges = hidden_state.shape[0]
    frames, rows, width, chan = features.shape
    slots = max(2, (2 * edges + n_edge - 1) // n_edge)
    assert edges % slots == 0 and edges <= 8 and ASKS + n_edge * slots <= 128
    per = edges // slots
    band = rows * width

    fields = (
        (edge_owner[:, 0], OWNER), (edge_target, TARGET), (edge_source, SOURCE), (edge_counts, COUNT),
    )
    meta = jnp.zeros((1, 128), jnp.int32)
    for field, at in fields:
        meta = meta + jnp.pad(field, (at, 128 - at - field.shape[0]))[None, :]
    dims = (n_edge, n_tile, edges, frames, rows, width, slots)
    even = (rows + 2 * NEAR + 1) // 2 * 2
    dma = pltpu.SemaphoreType.DMA
    vmem = pl.BlockSpec(memory_space=pltpu.VMEM)
    smem = pl.BlockSpec(memory_space=pltpu.SMEM)
    hbm = pl.BlockSpec(memory_space=pl.ANY)

    inputs = (
        ("own_s", meta, smem),
        ("feat_h", features.reshape(frames, band, chan), hbm),
        ("hidden_h", hidden_state.reshape(edges, band, chan), hbm),
        ("corr_in", corr_weight, vmem),
        ("gate_w", gate_weight, hbm),
        ("cand_w", candidate_weight, hbm),
        ("jac_in", jacobian_weight.T, vmem),
        ("conf_in", confidence_weight.T, vmem),
    )
    outputs = (
        ("out_hidden", (edges, band, chan), BF, hbm),
        ("gall", (n_edge, 16, 128), F32, vmem),
        ("meta_all", (n_edge, 1, 128), jnp.int32, vmem),
    )
    near, far = len(reach(NEAR, rows)), len(reach(FAR, rows))
    scratch = {
        "row_v": pltpu.VMEM((1, 128), jnp.int32),
        "row_s": pltpu.SMEM((1, 128), jnp.int32),
        "meta_s": pltpu.SMEM((n_edge, 1, 128), jnp.int32),
        "feat": pltpu.VMEM((frames, band, chan), BF),
        "held": pltpu.VMEM((edges, band, chan), BF),
        "send": pltpu.VMEM(((n_edge - 1) * slots, band, chan), BF),
        "text": pltpu.VMEM((edges, (even + 2 * RADIUS + 3) // 4 * 4 * width, chan), BF),
        "sext": pltpu.VMEM((edges, even * width, chan), BF),
        "hext": pltpu.VMEM((edges, (rows + 2 * NEAR) * width, chan), BF),
        "mext": pltpu.VMEM((per, even * width, chan), BF),
        "x3": pltpu.VMEM((per, (rows + 2 * NEAR) * width, 3 * chan), BF),
        "x3r": pltpu.VMEM((per, (rows + 2) * width, 3 * chan), BF),
        "wh": pltpu.VMEM((9 * chan, 2 * chan), BF),
        "wm": pltpu.VMEM((9 * chan, 2 * chan), BF),
        "wc": pltpu.VMEM((6 * chan, 3 * chan), BF),
        "corr_w": pltpu.VMEM((128, chan), BF),
        "head_w": pltpu.VMEM((64, chan), BF),
        "gpre": pltpu.VMEM((edges, (rows + 2) * width, 2 * chan), F32),
        "upd": pltpu.VMEM((per, band, chan), F32),
        "jall": pltpu.VMEM((128, 2 * band), BF),
        "wall": pltpu.VMEM((128, 2 * band), BF),
        "gpart": pltpu.VMEM((16, 128), F32),
        "gtile": pltpu.VMEM((n_tile, 16, 128), F32),
        "gsum": pltpu.VMEM((16, 128), F32),
        "l_in": dma((2,)),
        "l_w": dma((36,)),
        "l_row": dma,
        "l_meta": dma,
        "l_out": dma,
        "s_meta": dma((n_edge,)),
        "r_meta": dma((n_edge,)),
        "s_feat": dma((n_edge, slots)),
        "r_feat": dma((n_edge, slots)),
        "s_gt": dma((n_tile,)),
        "r_gt": dma((n_tile,)),
        "s_ge": dma((n_edge,)),
        "r_ge": dma((n_edge,)),
    }
    for s in range(slots):
        scratch[f"text{s}"] = pltpu.VMEM((n_edge - 1, band, chan), BF)
    for key, count in (("h", near), ("s", near), ("t", far)):
        for name in (f"s_{key}up", f"r_{key}up", f"s_{key}dn", f"r_{key}dn"):
            scratch[name] = dma((count, edges))
    names = [i[0] for i in inputs] + [o[0] for o in outputs] + list(scratch)
    state, gall, meta_all = pl.pallas_call(
        functools.partial(kernel, dims, names),
        out_shape=tuple(jax.ShapeDtypeStruct(shape, kind) for _, shape, kind, _ in outputs),
        in_specs=[spec for _, _, spec in inputs],
        out_specs=tuple(spec for _, _, _, spec in outputs),
        scratch_shapes=list(scratch.values()),
        compiler_params=pltpu.CompilerParams(
            collective_id=0, has_side_effects=True, vmem_limit_bytes=56 * 1024 * 1024
        ),
    )(*[value for _, value, _ in inputs])
    hidden_next, cam, diag = pl.pallas_call(
        functools.partial(assemble, dims),
        out_shape=(
            jax.ShapeDtypeStruct((edges, band, chan), BF),
            jax.ShapeDtypeStruct((frames * n_edge * 6 // n_tile, frames * 6), F32),
            jax.ShapeDtypeStruct((frames, 36), F32),
        ),
        in_specs=[smem, vmem, hbm],
        out_specs=(hbm, vmem, vmem),
        scratch_shapes=[pltpu.VMEM((edges, band, chan), BF), dma((edges + 1,))],
    )(meta_all, gall, state)
    return hidden_next.reshape(hidden_state.shape), cam, diag


def solution(mesh):
    placed = (
        P("edge", "tile", None, None),
        P("edge", "tile", None, None),
        P("edge"),
        P("edge", None),
        P("edge"),
        P("edge"),
        P(),
        P(),
        P(),
        P(),
        P(),
    )
    return jax.shard_map(
        per_device,
        mesh=mesh,
        in_specs=placed,
        out_specs=(P("edge", "tile", None, None), P("tile", "edge"), P("edge", None)),
        check_vma=False,
    )
```

```python
import functools
import types

import jax
import jax.numpy as jnp
from jax import lax
from jax.experimental import pallas as pl
from jax.experimental.pallas import tpu as pltpu
from jax.sharding import PartitionSpec as P

MAPH = 48
WINDOW = 7
RADIUS = WINDOW // 2
NEAR = 2
FAR = RADIUS + NEAR
OWNER, TARGET, SOURCE, COUNT, PLACE, GROUP, REL, ASKS = 0, 8, 16, 24, 32, 40, 48, 64
MESH = pl.DeviceIdType.MESH
BF = jnp.bfloat16
F32 = jnp.float32


def nt(a, b):
    return lax.dot_general(a, b, (((1,), (1,)), ((), ())), preferred_element_type=F32)


def nn(a, b):
    return lax.dot_general(a, b, (((1,), (0,)), ((), ())), preferred_element_type=F32)


def iota(shape, dim):
    return lax.broadcasted_iota(jnp.int32, shape, dim)


def sixth(index):
    return jnp.floor((index.astype(F32) + 0.5) * (1.0 / 6.0))


def one_hot(cond):
    return cond.astype(F32).astype(BF)


def each(count, body):
    def step(i, carry):
        body(i)
        return carry

    lax.fori_loop(0, count, step, 0)


def reach(halo, rows):
    return [min(rows, halo - d * rows) for d in range((halo + rows - 1) // rows)]


def kernel(dims, names, *refs):
    n_edge, n_tile, edges, frames, rows, width, slots = dims
    r = types.SimpleNamespace(**dict(zip(names, refs)))
    band = rows * width
    per = edges // slots
    me = lax.axis_index("edge")
    tile = lax.axis_index("tile")
    texts = [getattr(r, f"text{s}") for s in range(slots)]

    loads = [
        pltpu.make_async_copy(r.feat_h, r.feat, r.l_in.at[0]),
        pltpu.make_async_copy(
            r.hidden_h, r.hext.at[:, pl.ds(NEAR * width, band)], r.l_in.at[1]
        ),
    ]
    fills = []
    for a in range(3):
        for b in range(3):
            at = pl.ds((a * 3 + b) * 128, 128)
            first, second = pl.ds(0, 128), pl.ds(128, 128)
            pairs = (
                (r.gate_w.at[a, b, first], r.wh.at[at]),
                (r.gate_w.at[a, b, second], r.wm.at[at]),
                (r.cand_w.at[a, b, first], r.wc.at[pl.ds(a * 128, 128), pl.ds(b * 128, 128)]),
                (r.cand_w.at[a, b, second], r.wc.at[pl.ds(384 + a * 128, 128), pl.ds(b * 128, 128)]),
            )
            for source, target in pairs:
                fills.append(pltpu.make_async_copy(source, target, r.l_w.at[len(fills)]))
    for load in loads + fills:
        load.start()

    barrier = pltpu.get_barrier_semaphore()
    for rel in range(1, n_edge):
        pl.semaphore_signal(
            barrier, inc=1, device_id=((me + rel) % n_edge, tile), device_id_type=MESH
        )
    for rel in range(1, n_tile):
        pl.semaphore_signal(
            barrier, inc=1, device_id=(me, (tile + rel) % n_tile), device_id_type=MESH
        )

    owner = [r.own_s[0, OWNER + e] for e in range(edges)]
    rel_of = [(owner[e] - me + n_edge) % n_edge for e in range(edges)]
    rank, group = [], []
    for e in range(edges):
        before = jnp.int32(0)
        for k in range(e):
            before = before + (owner[k] == owner[e]).astype(jnp.int32)
        rank.append(jnp.minimum(before, slots - 1))
        group.append(jnp.where(rel_of[e] == 0, 0, rank[e] + 1))
    lane = iota((1, 128), 1)
    row = jnp.where(lane == COUNT, r.own_s[0, COUNT], 0)
    for e in range(edges):
        spot = jnp.int32(0)
        for k in range(edges):
            if k < e:
                spot = spot + (group[k] <= group[e]).astype(jnp.int32)
            elif k > e:
                spot = spot + (group[k] < group[e]).astype(jnp.int32)
        goal = r.own_s[0, TARGET + e]
        fields = (
            (OWNER, owner[e]),
            (TARGET, goal),
            (SOURCE, r.own_s[0, SOURCE + e]),
            (PLACE, jnp.int32(e)),
            (GROUP, group[e]),
            (REL, rel_of[e]),
        )
        for base, value in fields:
            row = jnp.where(lane == base + spot, value, row)
        row = jnp.where(lane == ASKS + rel_of[e] * slots + rank[e], goal, row)
    r.row_v[...] = row
    mine = pltpu.make_async_copy(r.row_v, r.row_s, r.l_row)
    mine.start()
    mine.wait()

    pl.semaphore_wait(barrier, n_edge + n_tile - 2)

    def remote(src, dst, send_sem, recv_sem, edge_id, tile_id):
        return pltpu.make_async_remote_copy(
            src_ref=src,
            dst_ref=dst,
            send_sem=send_sem,
            recv_sem=recv_sem,
            device_id=(edge_id, tile_id),
            device_id_type=MESH,
        )

    def meta_copy(rel):
        return remote(
            r.row_v, r.meta_all.at[me], r.s_meta.at[rel], r.r_meta.at[rel],
            (me + rel) % n_edge, tile,
        )

    for rel in range(1, n_edge):
        meta_copy(rel).start()

    class Halo:
        def __init__(self, halo, buf, source, sems):
            self.halo, self.buf, self.source, self.sems = halo, buf, source, sems
            self.counts = reach(halo, rows)

        def copies(self, e):
            for d, count in enumerate(self.counts):
                far, lines = d + 1, count * width
                s_up, r_up, s_dn, r_dn = self.sems
                up = remote(
                    self.source(e, 0, lines),
                    self.buf.at[e, pl.ds((self.halo + far * rows) * width, lines)],
                    s_up.at[d, e], r_up.at[d, e], me, tile - far,
                )
                dn = remote(
                    self.source(e, band - lines, lines),
                    self.buf.at[e, pl.ds((self.halo - d * rows - count) * width, lines)],
                    s_dn.at[d, e], r_dn.at[d, e], me, tile + far,
                )
                yield tile >= far, tile + far < n_tile, up, dn

        def start(self, e):
            for above, below, up, dn in self.copies(e):
                pl.when(above)(up.start)
                pl.when(below)(dn.start)

        def received(self, e):
            for above, below, up, dn in self.copies(e):
                pl.when(below)(up.wait_recv)
                pl.when(above)(dn.wait_recv)

        def sent(self, e):
            for above, below, up, dn in self.copies(e):
                pl.when(above)(up.wait_send)
                pl.when(below)(dn.wait_send)

        def clear(self):
            for d, count in enumerate(self.counts):
                far, lines = d + 1, count * width
                zero = jnp.zeros((lines, 128), BF)
                top = (self.halo - d * rows - count) * width
                low = (self.halo + far * rows) * width

                @pl.when(tile < far)
                def _():
                    def clear_top(e):
                        self.buf[e, pl.ds(top, lines)] = zero

                    each(edges, clear_top)

                @pl.when(tile + far >= n_tile)
                def _():
                    def clear_low(e):
                        self.buf[e, pl.ds(low, lines)] = zero

                    each(edges, clear_low)

            used = (rows + 2 * self.halo) * width
            spare = self.buf.shape[1] - used
            if spare:

                def clear_pad(e):
                    self.buf[e, pl.ds(used, spare)] = jnp.zeros((spare, 128), BF)

                each(edges, clear_pad)

    def inner(buf, halo):
        return lambda e, at, lines: buf.at[e, pl.ds(halo * width + at, lines)]

    hid = Halo(
        NEAR, r.hext, lambda e, at, lines: r.hidden_h.at[e, pl.ds(at, lines)],
        (r.s_hup, r.r_hup, r.s_hdn, r.r_hdn),
    )
    src = Halo(NEAR, r.sext, inner(r.sext, NEAR), (r.s_sup, r.r_sup, r.s_sdn, r.r_sdn))
    txt = Halo(FAR, r.text, inner(r.text, FAR), (r.s_tup, r.r_tup, r.s_tdn, r.r_tdn))

    each(edges, hid.start)
    r.meta_all[me] = r.row_v[...]
    for rel in range(1, n_edge):
        remote(
            r.row_v, r.meta_all.at[(me - rel + n_edge) % n_edge], r.s_meta.at[rel],
            r.r_meta.at[rel], (me + rel) % n_edge, tile,
        ).wait_recv()
    local = pltpu.make_async_copy(r.meta_all, r.meta_s, r.l_meta)
    local.start()
    loads[0].wait()
    local.wait()

    def feat_copy(rel, s):
        return remote(
            r.send.at[(rel - 1) * slots + s], texts[s].at[rel - 1],
            r.s_feat.at[rel, s], r.r_feat.at[rel, s], (me - rel + n_edge) % n_edge, tile,
        )

    for s in range(slots):
        for rel in range(1, n_edge):
            peer = (me - rel + n_edge) % n_edge
            r.send[(rel - 1) * slots + s] = r.feat[r.meta_s[peer, 0, ASKS + rel * slots + s]]
        for rel in range(1, n_edge):
            feat_copy(rel, s).start()

    def take_source(e):
        r.sext[e, pl.ds(NEAR * width, band)] = r.feat[r.row_s[0, SOURCE + e]]
        src.start(e)

    each(edges, take_source)
    for halo in (hid, src, txt):
        halo.clear()

    spot = (iota((128, 64), 0) + 4) & 127
    along = ((spot >> 3) & 3) * 2 + (spot >> 6) - ((spot >> 5) & 1)
    across = WINDOW - 1 - (spot & 7)
    fits = (across >= 0) & (along >= 0) & (along < WINDOW)
    pick = (iota((128, 64), 1) == along * WINDOW + across) & fits
    lookup = jnp.concatenate(
        [r.corr_in[...].astype(F32), jnp.zeros((64 - WINDOW * WINDOW, 128), F32)], axis=0
    ).astype(BF)
    r.corr_w[...] = nn(one_hot(pick), lookup).astype(BF)

    place12 = iota((32, 64), 0)
    which = place12 >> 4
    within = place12 & 15
    name12 = iota((32, 64), 1)
    pick_j = (within < 12) & (name12 == which * 12 + within)
    padded_jac = jnp.concatenate(
        [r.jac_in[...].astype(F32), jnp.zeros((40, 128), F32)], axis=0
    ).astype(BF)
    conf_wide = r.conf_in[...].astype(F32)
    tall = iota((32, 128), 0)
    conf_rows = jnp.where(
        tall < 16,
        jnp.broadcast_to(conf_wide[0:1], (32, 128)),
        jnp.broadcast_to(conf_wide[1:2], (32, 128)),
    )
    r.head_w[...] = jnp.concatenate(
        [nn(one_hot(pick_j), padded_jac), jnp.where((tall & 15) < 12, conf_rows, 0.0)], axis=0
    ).astype(BF)

    def nudge(wide, by):
        lines = wide.shape[0]
        column = iota((lines, 128), 0) & (width - 1)
        edge = 0 if by == 1 else width - 1
        return jnp.where(column == edge, 0.0, pltpu.roll(wide, by % lines, 0))

    def spread(value, out):
        lines = value.shape[0]
        wide = value.astype(F32)
        out[0:lines, 0:128] = nudge(wide, 1).astype(BF)
        out[0:lines, 128:256] = value.astype(BF)
        out[0:lines, 256:384] = nudge(wide, -1).astype(BF)

    def windows(x3, q, out_rows):
        size = out_rows * width
        return jnp.concatenate([x3[q, a * width : a * width + size] for a in range(3)], axis=1)

    wide_band = (rows + 2) * width

    def state_part(p):
        for q in range(per):
            e = p * per + q
            spread(r.hext[r.row_s[0, PLACE + e]], r.x3.at[q])
            r.gpre[e] = nn(windows(r.x3, q, rows + 2), r.wh[...])

    loads[1].wait()
    for fill in fills:
        fill.wait()
    each(edges, hid.received)
    each(slots, state_part)
    each(edges, src.received)

    lane_w = (iota((width, 128), 1) + 4) & 127
    col_w = iota((width, 128), 0) + RADIUS - (lane_w & 7)
    in_map = (col_w >= 0) & (col_w < width) & ((lane_w & 7) < WINDOW)
    scaled = [
        jnp.where(in_map & (((lane_w >> 5) & 1) == par), 128.0 ** (-0.5), 0.0) for par in range(2)
    ]
    slot_w = (lane_w >> 3) & 3
    pairs_of = (rows + 2 * NEAR + 1) // 2
    quads_of = r.text.shape[1] // (4 * width)
    used_rows = (rows + 2 * NEAR) * width

    def motion_of(e, q):
        tables, starts = [], []
        for m in range(quads_of):
            first, last = max(0, 2 * m - 3), min(pairs_of - 1, 2 * m + 1)
            starts.append(first)
            tables.append(
                nt(
                    r.sext[e, pl.ds(2 * first * width, 2 * (last - first + 1) * width)],
                    r.text[e, pl.ds(4 * m * width, 4 * width)],
                )
            )
        lines = []
        for k in range(pairs_of):
            for par in range(2):
                found = None
                for g in range(4):
                    m, h = divmod(k + g, 2)
                    at = (2 * (k - starts[m]) + par) * width
                    piece = tables[m][at : at + width, h * 128 : (h + 1) * 128]
                    moved = pltpu.roll(
                        piece, width + 8 * g + 32 * par, 1, stride=1, stride_axis=0
                    )
                    found = moved if g == 0 else jnp.where(slot_w == g, moved, found)
                lines.append((found * scaled[par]).astype(BF))
        value = nn(jnp.concatenate(lines, axis=0), r.corr_w[...])
        spread(jnp.maximum(value[0:used_rows], 0.0), r.x3.at[q])

    def update(p):
        for q in range(per):
            txt.received(p * per + q)
            motion_of(p * per + q, q)
        for q in range(per):
            e = p * per + q
            before = r.gpre[e] + nn(windows(r.x3, q, rows + 2), r.wm[...])
            r.upd[q] = 0.5 * jnp.tanh(0.5 * before[width : width + band, 0:128]) + 0.5
            reset = 0.5 * jnp.tanh(0.5 * before[:, 128:256]) + 0.5
            state = r.hext[r.row_s[0, PLACE + e], pl.ds(width, wide_band)].astype(F32)
            r.rext[q] = (reset * state).astype(BF)
        for q in range(per):
            e = p * per + q
            part = nn(
                jnp.concatenate(
                    [r.rext[q, a * width : a * width + band] for a in range(3)]
                    + [
                        r.x3[q, (a + 1) * width : (a + 1) * width + band, 128:256]
                        for a in range(3)
                    ],
                    axis=1,
                ),
                r.wc[...],
            )
            candidate = jnp.tanh(
                nudge(part[:, 0:128], 1) + part[:, 128:256] + nudge(part[:, 256:384], -1)
            )
            gate = r.upd[q]
            place = r.row_s[0, PLACE + e]
            state = r.hext[place, pl.ds(NEAR * width, band)]
            fresh = ((1.0 - gate) * state.astype(F32) + gate * candidate).astype(BF)
            used = (place < r.row_s[0, COUNT]).astype(F32)
            live = jnp.full((band, 128), used) > 0.5
            r.held[e] = jnp.where(live, fresh, state)
            heads = nt(r.head_w[...], fresh)
            jac = heads[0:32]
            weighted = jac * jax.nn.softplus(heads[32:64])
            at16 = pl.ds(pl.multiple_of(e * 16, 16), 16)
            r.jall[at16] = jnp.concatenate([jac[0:16], jac[16:32]], axis=1).astype(BF)
            r.wall[at16] = jnp.concatenate([weighted[0:16], weighted[16:32]], axis=1).astype(BF)

    flip_row, flip_col = iota((2 * width, 2 * width), 0), iota((2 * width, 2 * width), 1)
    flip = one_hot(
        (flip_row // width == flip_col // width)
        & ((flip_row & (width - 1)) + (flip_col & (width - 1)) == width - 1)
    )

    def take_target(e, upto):
        value = r.feat[r.row_s[0, TARGET + e]]
        at = jnp.maximum(r.row_s[0, REL + e] - 1, 0)
        for s in range(upto + 1):
            value = jnp.where(r.row_s[0, GROUP + e] == s + 1, texts[s][at], value)
        for first in range(0, band, 2 * width):
            count = min(2 * width, band - first)
            r.text[e, pl.ds(FAR * width + first, count)] = nn(
                flip[0:count, 0:count], value[first : first + count]
            ).astype(BF)
        txt.start(e)

    def stage(p):
        for s in range(slots):

            @pl.when(p == s)
            def _():
                for rel in range(1, n_edge):
                    feat_copy(rel, s).wait_recv()
                for q in range(per):
                    take_target(s * per + q, s)

        pl.when(p > 0)(lambda: update(p - 1))

    each(slots + 1, stage)
    store = pltpu.make_async_copy(r.held, r.out_hidden, r.l_out)
    store.start()

    same = (iota((128, 128), 0) >> 4) == (iota((128, 128), 1) >> 4)
    square = jnp.where(same, nt(r.wall[...], r.jall[...]), 0.0)
    blocks = square[0:16]
    for e in range(1, edges):
        blocks = blocks + square[e * 16 : (e + 1) * 16]
    blocks = blocks * (1.0 / (MAPH * width))
    of = iota((16, 128), 1) >> 4
    for e in range(edges):
        used = (r.row_s[0, PLACE + e] < r.row_s[0, COUNT]).astype(jnp.int32)
        blocks = jnp.where((of == e) & (jnp.full((16, 128), used) == 0), 0.0, blocks)
    r.gpart[...] = blocks

    def tile_copy(rel):
        return remote(
            r.gpart, r.gtile.at[tile], r.s_gt.at[rel], r.r_gt.at[rel], me, (tile + rel) % n_tile
        )

    for rel in range(1, n_tile):
        tile_copy(rel).start()
    r.gtile[tile] = r.gpart[...]
    for rel in range(1, n_tile):
        remote(
            r.gpart, r.gtile.at[(tile - rel + n_tile) % n_tile], r.s_gt.at[rel], r.r_gt.at[rel],
            me, (tile + rel) % n_tile,
        ).wait_recv()
    total = r.gtile[0]
    for k in range(1, n_tile):
        total = total + r.gtile[k]
    r.gsum[...] = total

    def edge_copy(rel):
        return remote(
            r.gsum, r.gall.at[me], r.s_ge.at[rel], r.r_ge.at[rel], (me + rel) % n_edge, tile
        )

    for rel in range(1, n_edge):
        edge_copy(rel).start()
    r.gall[me] = total
    for rel in range(1, n_edge):
        remote(
            r.gsum, r.gall.at[(me - rel + n_edge) % n_edge], r.s_ge.at[rel], r.r_ge.at[rel],
            (me + rel) % n_edge, tile,
        ).wait_recv()

    store.wait()
    for rel in range(1, n_edge):
        meta_copy(rel).wait_send()
        edge_copy(rel).wait_send()
        for s in range(slots):
            feat_copy(rel, s).wait_send()
    for rel in range(1, n_tile):
        tile_copy(rel).wait_send()
    for halo in (hid, src, txt):
        each(edges, halo.sent)


def halves(value):
    high = value.astype(BF)
    return high, (value - high.astype(F32)).astype(BF)


def assemble(dims, meta_s, gall, hidden_h, out_hidden, out_cam, out_diag, held, sem):
    n_edge, n_tile, edges, frames, rows, width, slots = dims
    me = lax.axis_index("edge")
    tile = lax.axis_index("tile")
    fetch = pltpu.make_async_copy(hidden_h, held, sem.at[edges])
    fetch.start()
    cam_rows, cam_cols = out_cam.shape
    row_id = iota((cam_rows, 128), 0) + tile * cam_rows
    col_id = iota((cam_cols, 128), 0) + me * cam_cols
    same = (iota((128, 128), 0) >> 4) == (iota((128, 128), 1) >> 4)
    lane = iota((1, 128), 1)
    inner = lane & 15
    digit = jnp.where(inner < 6, inner, inner - 6)
    lefts, lows, rights = [], [], []
    for j in range(n_edge):
        spots = jnp.full((1, 128), -1, jnp.int32)
        for e in range(edges):
            source = (j * frames + meta_s[j, 0, SOURCE + e]) * 6
            target = (meta_s[j, 0, OWNER + e] * frames + meta_s[j, 0, TARGET + e]) * 6
            here = jnp.where(inner < 6, source, target) + digit
            spots = jnp.where(((lane >> 4) == e) & (inner < 12), here, spots)
        mine = (col_id == spots).astype(F32)
        left = jnp.concatenate([(row_id == spots).astype(F32), mine], axis=0).astype(BF)
        stack = jnp.where(same, jnp.concatenate([gall[j]] * 8, axis=0), 0.0)
        picked = nn(
            jnp.concatenate([left, left], axis=1), jnp.concatenate(halves(stack), axis=0)
        )
        high, low = halves(picked)
        lefts.append(high)
        lows.append(low)
        rights.append(mine.astype(BF))
    placed = nt(jnp.concatenate(lefts + lows, axis=1), jnp.concatenate(rights + rights, axis=1))
    fetch.wait()
    stores = [
        pltpu.make_async_copy(held.at[e], out_hidden.at[meta_s[me, 0, PLACE + e]], sem.at[e])
        for e in range(edges)
    ]
    for store in stores:
        store.start()
    cam = placed[0:cam_rows]
    row_frame = sixth(iota((cam_rows, cam_cols), 0) + tile * cam_rows)
    col_frame = sixth(iota((cam_rows, cam_cols), 1) + me * cam_cols)
    out_cam[...] = jnp.where(row_frame == col_frame, 0.0, cam)
    own = placed[cam_rows:]
    own_row = sixth(iota((cam_cols, cam_cols), 0))
    own_col = sixth(iota((cam_cols, cam_cols), 1))
    own = jnp.where(own_row == own_col, own, 0.0)
    wide_row = iota((cam_cols, 128), 0)
    wide_lane = iota((cam_cols, 128), 1)
    row_in = wide_row.astype(F32) - 6.0 * sixth(wide_row)
    lane_of = sixth(wide_lane)
    lane_in = wide_lane.astype(F32) - 6.0 * lane_of
    gather = one_hot(row_in == lane_in)
    high, low = halves(own)
    spread = jnp.where(row_in == lane_of, nn(high, gather) + nn(low, gather), 0.0)
    fold = one_hot(
        sixth(iota((frames, cam_cols), 1)) == iota((frames, cam_cols), 0).astype(F32)
    )
    high, low = halves(spread)
    out_diag[...] = (nn(fold, high) + nn(fold, low))[:, 0:36]
    for store in stores:
        store.wait()


def per_device(
    features,
    hidden_state,
    edge_source,
    edge_owner,
    edge_target,
    edge_counts,
    corr_weight,
    gate_weight,
    candidate_weight,
    jacobian_weight,
    confidence_weight,
):
    n_edge, n_tile = lax.axis_size("edge"), lax.axis_size("tile")
    edges = hidden_state.shape[0]
    frames, rows, width, chan = features.shape
    slots = max(2, (2 * edges + n_edge - 1) // n_edge)
    assert edges % slots == 0 and edges <= 8 and ASKS + n_edge * slots <= 128
    per = edges // slots
    band = rows * width

    fields = (
        (edge_owner[:, 0], OWNER), (edge_target, TARGET), (edge_source, SOURCE), (edge_counts, COUNT),
    )
    meta = jnp.zeros((1, 128), jnp.int32)
    for field, at in fields:
        meta = meta + jnp.pad(field, (at, 128 - at - field.shape[0]))[None, :]
    dims = (n_edge, n_tile, edges, frames, rows, width, slots)
    even = (rows + 2 * NEAR + 1) // 2 * 2
    dma = pltpu.SemaphoreType.DMA
    vmem = pl.BlockSpec(memory_space=pltpu.VMEM)
    smem = pl.BlockSpec(memory_space=pltpu.SMEM)
    hbm = pl.BlockSpec(memory_space=pl.ANY)

    inputs = (
        ("own_s", meta, smem),
        ("feat_h", features.reshape(frames, band, chan), hbm),
        ("hidden_h", hidden_state.reshape(edges, band, chan), hbm),
        ("corr_in", corr_weight, vmem),
        ("gate_w", gate_weight, hbm),
        ("cand_w", candidate_weight, hbm),
        ("jac_in", jacobian_weight.T, vmem),
        ("conf_in", confidence_weight.T, vmem),
    )
    outputs = (
        ("out_hidden", (edges, band, chan), BF, hbm),
        ("gall", (n_edge, 16, 128), F32, vmem),
        ("meta_all", (n_edge, 1, 128), jnp.int32, vmem),
    )
    near, far = len(reach(NEAR, rows)), len(reach(FAR, rows))
    scratch = {
        "row_v": pltpu.VMEM((1, 128), jnp.int32),
        "row_s": pltpu.SMEM((1, 128), jnp.int32),
        "meta_s": pltpu.SMEM((n_edge, 1, 128), jnp.int32),
        "feat": pltpu.VMEM((frames, band, chan), BF),
        "held": pltpu.VMEM((edges, band, chan), BF),
        "send": pltpu.VMEM(((n_edge - 1) * slots, band, chan), BF),
        "text": pltpu.VMEM((edges, (even + 2 * RADIUS + 3) // 4 * 4 * width, chan), BF),
        "sext": pltpu.VMEM((edges, even * width, chan), BF),
        "hext": pltpu.VMEM((edges, (rows + 2 * NEAR) * width, chan), BF),
        "rext": pltpu.VMEM((per, (rows + 2) * width, chan), BF),
        "x3": pltpu.VMEM((per, (rows + 2 * NEAR) * width, 3 * chan), BF),
        "wh": pltpu.VMEM((9 * chan, 2 * chan), BF),
        "wm": pltpu.VMEM((9 * chan, 2 * chan), BF),
        "wc": pltpu.VMEM((6 * chan, 3 * chan), BF),
        "corr_w": pltpu.VMEM((128, chan), BF),
        "head_w": pltpu.VMEM((64, chan), BF),
        "gpre": pltpu.VMEM((edges, (rows + 2) * width, 2 * chan), F32),
        "upd": pltpu.VMEM((per, band, chan), F32),
        "jall": pltpu.VMEM((128, 2 * band), BF),
        "wall": pltpu.VMEM((128, 2 * band), BF),
        "gpart": pltpu.VMEM((16, 128), F32),
        "gtile": pltpu.VMEM((n_tile, 16, 128), F32),
        "gsum": pltpu.VMEM((16, 128), F32),
        "l_in": dma((2,)),
        "l_w": dma((36,)),
        "l_row": dma,
        "l_meta": dma,
        "l_out": dma,
        "s_meta": dma((n_edge,)),
        "r_meta": dma((n_edge,)),
        "s_feat": dma((n_edge, slots)),
        "r_feat": dma((n_edge, slots)),
        "s_gt": dma((n_tile,)),
        "r_gt": dma((n_tile,)),
        "s_ge": dma((n_edge,)),
        "r_ge": dma((n_edge,)),
    }
    for s in range(slots):
        scratch[f"text{s}"] = pltpu.VMEM((n_edge - 1, band, chan), BF)
    for key, count in (("h", near), ("s", near), ("t", far)):
        for name in (f"s_{key}up", f"r_{key}up", f"s_{key}dn", f"r_{key}dn"):
            scratch[name] = dma((count, edges))
    names = [i[0] for i in inputs] + [o[0] for o in outputs] + list(scratch)
    state, gall, meta_all = pl.pallas_call(
        functools.partial(kernel, dims, names),
        out_shape=tuple(jax.ShapeDtypeStruct(shape, kind) for _, shape, kind, _ in outputs),
        in_specs=[spec for _, _, spec in inputs],
        out_specs=tuple(spec for _, _, _, spec in outputs),
        scratch_shapes=list(scratch.values()),
        compiler_params=pltpu.CompilerParams(
            collective_id=0, has_side_effects=True, vmem_limit_bytes=56 * 1024 * 1024
        ),
    )(*[value for _, value, _ in inputs])
    hidden_next, cam, diag = pl.pallas_call(
        functools.partial(assemble, dims),
        out_shape=(
            jax.ShapeDtypeStruct((edges, band, chan), BF),
            jax.ShapeDtypeStruct((frames * n_edge * 6 // n_tile, frames * 6), F32),
            jax.ShapeDtypeStruct((frames, 36), F32),
        ),
        in_specs=[smem, vmem, hbm],
        out_specs=(hbm, vmem, vmem),
        scratch_shapes=[pltpu.VMEM((edges, band, chan), BF), dma((edges + 1,))],
    )(meta_all, gall, state)
    return hidden_next.reshape(hidden_state.shape), cam, diag


def solution(mesh):
    placed = (
        P("edge", "tile", None, None),
        P("edge", "tile", None, None),
        P("edge"),
        P("edge", None),
        P("edge"),
        P("edge"),
        P(),
        P(),
        P(),
        P(),
        P(),
    )
    return jax.shard_map(
        per_device,
        mesh=mesh,
        in_specs=placed,
        out_specs=(P("edge", "tile", None, None), P("tile", "edge"), P("edge", None)),
        check_vma=False,
    )
```

```python
import functools
import types

import jax
import jax.numpy as jnp
from jax import lax
from jax.experimental import pallas as pl
from jax.experimental.pallas import tpu as pltpu
from jax.sharding import PartitionSpec as P

MAPH = 48
WINDOW = 7
RADIUS = WINDOW // 2
NEAR = 2
FAR = RADIUS + NEAR
OWNER, TARGET, SOURCE, PLACE, GROUP, REL, ASKS = 0, 8, 16, 32, 40, 48, 64
MESH = pl.DeviceIdType.MESH
BF = jnp.bfloat16
F32 = jnp.float32


def nt(a, b):
    return lax.dot_general(a, b, (((1,), (1,)), ((), ())), preferred_element_type=F32)


def nn(a, b):
    return lax.dot_general(a, b, (((1,), (0,)), ((), ())), preferred_element_type=F32)


def iota(shape, dim):
    return lax.broadcasted_iota(jnp.int32, shape, dim)


def sixth(index):
    return jnp.floor((index.astype(F32) + 0.5) * (1.0 / 6.0))


def one_hot(cond):
    return cond.astype(F32).astype(BF)


def each(count, body):
    def step(i, carry):
        body(i)
        return carry

    lax.fori_loop(0, count, step, 0)


def reach(halo, rows):
    return [min(rows, halo - d * rows) for d in range((halo + rows - 1) // rows)]


def kernel(dims, names, *refs):
    n_edge, n_tile, edges, frames, rows, width, slots = dims
    r = types.SimpleNamespace(**dict(zip(names, refs)))
    band = rows * width
    per = edges // slots
    me = lax.axis_index("edge")
    tile = lax.axis_index("tile")
    texts = [getattr(r, f"text{s}") for s in range(slots)]

    ints = [
        pltpu.make_async_copy(r.owner_h, r.owner_s, r.l_ints.at[0]),
        pltpu.make_async_copy(r.target_h, r.target_s, r.l_ints.at[1]),
        pltpu.make_async_copy(r.source_h, r.source_s, r.l_ints.at[2]),
        pltpu.make_async_copy(r.count_h, r.count_s, r.l_ints.at[3]),
    ]
    loads = [
        pltpu.make_async_copy(r.feat_h, r.feat, r.l_in.at[0]),
        pltpu.make_async_copy(
            r.hidden_h, r.hext.at[:, pl.ds(NEAR * width, band)], r.l_in.at[1]
        ),
        pltpu.make_async_copy(r.corr_h, r.corr_in, r.l_in.at[2]),
        pltpu.make_async_copy(r.jac_h, r.jac_in, r.l_in.at[3]),
        pltpu.make_async_copy(r.conf_h, r.conf_in, r.l_in.at[4]),
    ]
    fills = []
    for a in range(3):
        for b in range(3):
            at = pl.ds((a * 3 + b) * 128, 128)
            first, second = pl.ds(0, 128), pl.ds(128, 128)
            pairs = (
                (r.gate_w.at[a, b, first], r.wh.at[at]),
                (r.gate_w.at[a, b, second], r.wm.at[at]),
                (r.cand_w.at[a, b, first], r.wc.at[pl.ds(a * 128, 128), pl.ds(b * 128, 128)]),
                (r.cand_w.at[a, b, second], r.wc.at[pl.ds(384 + a * 128, 128), pl.ds(b * 128, 128)]),
            )
            for source, target in pairs:
                fills.append(pltpu.make_async_copy(source, target, r.l_w.at[len(fills)]))
    for load in ints + loads + fills:
        load.start()

    barrier = pltpu.get_barrier_semaphore()
    for rel in range(1, n_edge):
        pl.semaphore_signal(
            barrier, inc=1, device_id=((me + rel) % n_edge, tile), device_id_type=MESH
        )
    for rel in range(1, n_tile):
        pl.semaphore_signal(
            barrier, inc=1, device_id=(me, (tile + rel) % n_tile), device_id_type=MESH
        )

    for load in ints:
        load.wait()
    owner = [r.owner_s[e] for e in range(edges)]
    rel_of = [(owner[e] - me + n_edge) % n_edge for e in range(edges)]
    rank, group = [], []
    for e in range(edges):
        before = jnp.int32(0)
        for k in range(e):
            before = before + (owner[k] == owner[e]).astype(jnp.int32)
        rank.append(jnp.minimum(before, slots - 1))
        group.append(jnp.where(rel_of[e] == 0, 0, rank[e] + 1))
    lane = iota((1, 128), 1)
    row = jnp.zeros((1, 128), jnp.int32)
    for e in range(edges):
        spot = jnp.int32(0)
        for k in range(edges):
            if k < e:
                spot = spot + (group[k] <= group[e]).astype(jnp.int32)
            elif k > e:
                spot = spot + (group[k] < group[e]).astype(jnp.int32)
        goal = r.target_s[e]
        fields = (
            (OWNER, owner[e]),
            (TARGET, goal),
            (SOURCE, r.source_s[e]),
            (PLACE, jnp.int32(e)),
            (GROUP, group[e]),
            (REL, rel_of[e]),
        )
        for base, value in fields:
            row = jnp.where(lane == base + spot, value, row)
        row = jnp.where(lane == ASKS + rel_of[e] * slots + rank[e], goal, row)
    r.row_v[...] = row
    mine = pltpu.make_async_copy(r.row_v, r.row_s, r.l_row)
    mine.start()

    pl.semaphore_wait(barrier, n_edge + n_tile - 2)

    def remote(src, dst, send_sem, recv_sem, edge_id, tile_id):
        return pltpu.make_async_remote_copy(
            src_ref=src,
            dst_ref=dst,
            send_sem=send_sem,
            recv_sem=recv_sem,
            device_id=(edge_id, tile_id),
            device_id_type=MESH,
        )

    def meta_copy(rel):
        return remote(
            r.row_v, r.meta_s.at[me], r.s_meta.at[rel], r.r_meta.at[rel],
            (me + rel) % n_edge, tile,
        )

    for rel in range(1, n_edge):
        meta_copy(rel).start()

    class Halo:
        def __init__(self, halo, buf, source, sems):
            self.halo, self.buf, self.source, self.sems = halo, buf, source, sems
            self.counts = reach(halo, rows)

        def copies(self, e):
            for d, count in enumerate(self.counts):
                far, lines = d + 1, count * width
                s_up, r_up, s_dn, r_dn = self.sems
                up = remote(
                    self.source(e, 0, lines),
                    self.buf.at[e, pl.ds((self.halo + far * rows) * width, lines)],
                    s_up.at[d, e], r_up.at[d, e], me, tile - far,
                )
                dn = remote(
                    self.source(e, band - lines, lines),
                    self.buf.at[e, pl.ds((self.halo - d * rows - count) * width, lines)],
                    s_dn.at[d, e], r_dn.at[d, e], me, tile + far,
                )
                yield tile >= far, tile + far < n_tile, up, dn

        def start(self, e):
            for above, below, up, dn in self.copies(e):
                pl.when(above)(up.start)
                pl.when(below)(dn.start)

        def received(self, e):
            for above, below, up, dn in self.copies(e):
                pl.when(below)(up.wait_recv)
                pl.when(above)(dn.wait_recv)

        def sent(self, e):
            for above, below, up, dn in self.copies(e):
                pl.when(above)(up.wait_send)
                pl.when(below)(dn.wait_send)

        def clear(self):
            for d, count in enumerate(self.counts):
                far, lines = d + 1, count * width
                zero = jnp.zeros((lines, 128), BF)
                top = (self.halo - d * rows - count) * width
                low = (self.halo + far * rows) * width

                @pl.when(tile < far)
                def _():
                    def clear_top(e):
                        self.buf[e, pl.ds(top, lines)] = zero

                    each(edges, clear_top)

                @pl.when(tile + far >= n_tile)
                def _():
                    def clear_low(e):
                        self.buf[e, pl.ds(low, lines)] = zero

                    each(edges, clear_low)

            used = (rows + 2 * self.halo) * width
            spare = self.buf.shape[1] - used
            if spare:

                def clear_pad(e):
                    self.buf[e, pl.ds(used, spare)] = jnp.zeros((spare, 128), BF)

                each(edges, clear_pad)

    def inner(buf, halo):
        return lambda e, at, lines: buf.at[e, pl.ds(halo * width + at, lines)]

    hid = Halo(
        NEAR, r.hext, lambda e, at, lines: r.hidden_h.at[e, pl.ds(at, lines)],
        (r.s_hup, r.r_hup, r.s_hdn, r.r_hdn),
    )
    src = Halo(NEAR, r.sext, inner(r.sext, NEAR), (r.s_sup, r.r_sup, r.s_sdn, r.r_sdn))
    txt = Halo(FAR, r.text, inner(r.text, FAR), (r.s_tup, r.r_tup, r.s_tdn, r.r_tdn))

    each(edges, hid.start)
    own_row = pltpu.make_async_copy(r.row_v, r.meta_s.at[me], r.l_own)
    own_row.start()
    for rel in range(1, n_edge):
        remote(
            r.row_v, r.meta_s.at[(me - rel + n_edge) % n_edge], r.s_meta.at[rel],
            r.r_meta.at[rel], (me + rel) % n_edge, tile,
        ).wait_recv()
    loads[0].wait()

    def feat_copy(rel, s):
        return remote(
            r.send.at[(rel - 1) * slots + s], texts[s].at[rel - 1],
            r.s_feat.at[rel, s], r.r_feat.at[rel, s], (me - rel + n_edge) % n_edge, tile,
        )

    for s in range(slots):
        for rel in range(1, n_edge):
            peer = (me - rel + n_edge) % n_edge
            r.send[(rel - 1) * slots + s] = r.feat[r.meta_s[peer, 0, ASKS + rel * slots + s]]
        for rel in range(1, n_edge):
            feat_copy(rel, s).start()

    mine.wait()
    own_row.wait()
    tables = pltpu.make_async_copy(r.meta_s, r.meta_all, r.l_meta)
    tables.start()

    def take_source(e):
        r.sext[e, pl.ds(NEAR * width, band)] = r.feat[r.row_s[0, SOURCE + e]]
        src.start(e)

    each(edges, take_source)
    for halo in (hid, src, txt):
        halo.clear()

    for load in loads[2:]:
        load.wait()

    spot = (iota((128, 64), 0) + 4) & 127
    along = ((spot >> 3) & 3) * 2 + (spot >> 6) - ((spot >> 5) & 1)
    across = WINDOW - 1 - (spot & 7)
    fits = (across >= 0) & (along >= 0) & (along < WINDOW)
    pick = (iota((128, 64), 1) == along * WINDOW + across) & fits
    lookup = jnp.concatenate(
        [r.corr_in[...].astype(F32), jnp.zeros((64 - WINDOW * WINDOW, 128), F32)], axis=0
    ).astype(BF)
    r.corr_w[...] = nn(one_hot(pick), lookup).astype(BF)

    place12 = iota((32, 64), 0)
    which = place12 >> 4
    within = place12 & 15
    name12 = iota((32, 64), 1)
    pick_j = (within < 12) & (name12 == which * 12 + within)
    padded_jac = jnp.concatenate(
        [r.jac_in[...].astype(F32), jnp.zeros((40, 128), F32)], axis=0
    ).astype(BF)
    conf_wide = r.conf_in[...].astype(F32)
    tall = iota((32, 128), 0)
    conf_rows = jnp.where(
        tall < 16,
        jnp.broadcast_to(conf_wide[0:1], (32, 128)),
        jnp.broadcast_to(conf_wide[1:2], (32, 128)),
    )
    r.head_w[...] = jnp.concatenate(
        [nn(one_hot(pick_j), padded_jac), jnp.where((tall & 15) < 12, conf_rows, 0.0)], axis=0
    ).astype(BF)

    def nudge(wide, by):
        lines = wide.shape[0]
        column = iota((lines, 128), 0) & (width - 1)
        edge = 0 if by == 1 else width - 1
        return jnp.where(column == edge, 0.0, pltpu.roll(wide, by % lines, 0))

    def spread(value, out):
        lines = value.shape[0]
        wide = value.astype(F32)
        out[0:lines, 0:128] = nudge(wide, 1).astype(BF)
        out[0:lines, 128:256] = value.astype(BF)
        out[0:lines, 256:384] = nudge(wide, -1).astype(BF)

    def windows(x3, q, out_rows):
        size = out_rows * width
        return jnp.concatenate([x3[q, a * width : a * width + size] for a in range(3)], axis=1)

    wide_band = (rows + 2) * width

    def state_part(p):
        for q in range(per):
            e = p * per + q
            spread(r.hext[r.row_s[0, PLACE + e]], r.x3.at[q])
            r.gpre[e] = nn(windows(r.x3, q, rows + 2), r.wh[...])

    loads[1].wait()
    for fill in fills:
        fill.wait()
    each(edges, hid.received)
    each(slots, state_part)
    each(edges, src.received)

    lane_w = (iota((width, 128), 1) + 4) & 127
    col_w = iota((width, 128), 0) + RADIUS - (lane_w & 7)
    in_map = (col_w >= 0) & (col_w < width) & ((lane_w & 7) < WINDOW)
    scaled = [
        jnp.where(in_map & (((lane_w >> 5) & 1) == par), 128.0 ** (-0.5), 0.0) for par in range(2)
    ]
    slot_w = (lane_w >> 3) & 3
    pairs_of = (rows + 2 * NEAR + 1) // 2
    quads_of = r.text.shape[1] // (4 * width)
    used_rows = (rows + 2 * NEAR) * width

    def motion_of(e, q):
        tables, starts = [], []
        for m in range(quads_of):
            first, last = max(0, 2 * m - 3), min(pairs_of - 1, 2 * m + 1)
            starts.append(first)
            tables.append(
                nt(
                    r.sext[e, pl.ds(2 * first * width, 2 * (last - first + 1) * width)],
                    r.text[e, pl.ds(4 * m * width, 4 * width)],
                )
            )
        lines = []
        for k in range(pairs_of):
            for par in range(2):
                found = None
                for g in range(4):
                    m, h = divmod(k + g, 2)
                    at = (2 * (k - starts[m]) + par) * width
                    piece = tables[m][at : at + width, h * 128 : (h + 1) * 128]
                    moved = pltpu.roll(
                        piece, width + 8 * g + 32 * par, 1, stride=1, stride_axis=0
                    )
                    found = moved if g == 0 else jnp.where(slot_w == g, moved, found)
                lines.append((found * scaled[par]).astype(BF))
        value = nn(jnp.concatenate(lines, axis=0), r.corr_w[...])
        spread(jnp.maximum(value[0:used_rows], 0.0), r.x3.at[q])

    def update(p):
        for q in range(per):
            txt.received(p * per + q)
            motion_of(p * per + q, q)
        for q in range(per):
            e = p * per + q
            before = r.gpre[e] + nn(windows(r.x3, q, rows + 2), r.wm[...])
            r.upd[q] = 0.5 * jnp.tanh(0.5 * before[width : width + band, 0:128]) + 0.5
            reset = 0.5 * jnp.tanh(0.5 * before[:, 128:256]) + 0.5
            state = r.hext[r.row_s[0, PLACE + e], pl.ds(width, wide_band)].astype(F32)
            r.rext[q] = (reset * state).astype(BF)
        for q in range(per):
            e = p * per + q
            part = nn(
                jnp.concatenate(
                    [r.rext[q, a * width : a * width + band] for a in range(3)]
                    + [
                        r.x3[q, (a + 1) * width : (a + 1) * width + band, 128:256]
                        for a in range(3)
                    ],
                    axis=1,
                ),
                r.wc[...],
            )
            candidate = jnp.tanh(
                nudge(part[:, 0:128], 1) + part[:, 128:256] + nudge(part[:, 256:384], -1)
            )
            gate = r.upd[q]
            place = r.row_s[0, PLACE + e]
            state = r.hext[place, pl.ds(NEAR * width, band)]
            fresh = ((1.0 - gate) * state.astype(F32) + gate * candidate).astype(BF)
            used = (place < r.count_s[0]).astype(F32)
            live = jnp.full((band, 128), used) > 0.5
            r.held[e] = jnp.where(live, fresh, state)
            heads = nt(r.head_w[...], fresh)
            jac = heads[0:32]
            weighted = jac * jax.nn.softplus(heads[32:64])
            at16 = pl.ds(pl.multiple_of(e * 16, 16), 16)
            r.jall[at16] = jnp.concatenate([jac[0:16], jac[16:32]], axis=1).astype(BF)
            r.wall[at16] = jnp.concatenate([weighted[0:16], weighted[16:32]], axis=1).astype(BF)

    flip_row, flip_col = iota((2 * width, 2 * width), 0), iota((2 * width, 2 * width), 1)
    flip = one_hot(
        (flip_row // width == flip_col // width)
        & ((flip_row & (width - 1)) + (flip_col & (width - 1)) == width - 1)
    )

    def take_target(e, upto):
        value = r.feat[r.row_s[0, TARGET + e]]
        at = jnp.maximum(r.row_s[0, REL + e] - 1, 0)
        for s in range(upto + 1):
            value = jnp.where(r.row_s[0, GROUP + e] == s + 1, texts[s][at], value)
        for first in range(0, band, 2 * width):
            count = min(2 * width, band - first)
            r.text[e, pl.ds(FAR * width + first, count)] = nn(
                flip[0:count, 0:count], value[first : first + count]
            ).astype(BF)
        txt.start(e)

    def stage(p):
        for s in range(slots):

            @pl.when(p == s)
            def _():
                for rel in range(1, n_edge):
                    feat_copy(rel, s).wait_recv()
                for q in range(per):
                    take_target(s * per + q, s)

        pl.when(p > 0)(lambda: update(p - 1))

    each(slots + 1, stage)
    store = pltpu.make_async_copy(r.held, r.out_hidden, r.l_out)
    store.start()

    same = (iota((128, 128), 0) >> 4) == (iota((128, 128), 1) >> 4)
    square = jnp.where(same, nt(r.wall[...], r.jall[...]), 0.0)
    blocks = square[0:16]
    for e in range(1, edges):
        blocks = blocks + square[e * 16 : (e + 1) * 16]
    blocks = blocks * (1.0 / (MAPH * width))
    of = iota((16, 128), 1) >> 4
    for e in range(edges):
        used = (r.row_s[0, PLACE + e] < r.count_s[0]).astype(jnp.int32)
        blocks = jnp.where((of == e) & (jnp.full((16, 128), used) == 0), 0.0, blocks)
    r.gpart[...] = blocks

    def tile_copy(rel):
        return remote(
            r.gpart, r.gtile.at[tile], r.s_gt.at[rel], r.r_gt.at[rel], me, (tile + rel) % n_tile
        )

    for rel in range(1, n_tile):
        tile_copy(rel).start()
    r.gtile[tile] = r.gpart[...]
    for rel in range(1, n_tile):
        remote(
            r.gpart, r.gtile.at[(tile - rel + n_tile) % n_tile], r.s_gt.at[rel], r.r_gt.at[rel],
            me, (tile + rel) % n_tile,
        ).wait_recv()
    total = r.gtile[0]
    for k in range(1, n_tile):
        total = total + r.gtile[k]
    r.gsum[...] = total

    def edge_copy(rel):
        return remote(
            r.gsum, r.gall.at[me], r.s_ge.at[rel], r.r_ge.at[rel], (me + rel) % n_edge, tile
        )

    for rel in range(1, n_edge):
        edge_copy(rel).start()
    r.gall[me] = total
    for rel in range(1, n_edge):
        remote(
            r.gsum, r.gall.at[(me - rel + n_edge) % n_edge], r.s_ge.at[rel], r.r_ge.at[rel],
            (me + rel) % n_edge, tile,
        ).wait_recv()

    store.wait()
    tables.wait()
    for rel in range(1, n_edge):
        meta_copy(rel).wait_send()
        edge_copy(rel).wait_send()
        for s in range(slots):
            feat_copy(rel, s).wait_send()
    for rel in range(1, n_tile):
        tile_copy(rel).wait_send()
    for halo in (hid, src, txt):
        each(edges, halo.sent)


def halves(value):
    high = value.astype(BF)
    return high, (value - high.astype(F32)).astype(BF)


def assemble(dims, meta_s, gall, hidden_h, out_hidden, out_cam, out_diag, held, sem):
    n_edge, n_tile, edges, frames, rows, width, slots = dims
    me = lax.axis_index("edge")
    tile = lax.axis_index("tile")
    fetch = pltpu.make_async_copy(hidden_h, held, sem.at[edges])
    fetch.start()
    cam_rows, cam_cols = out_cam.shape
    row_id = iota((cam_rows, 128), 0) + tile * cam_rows
    col_id = iota((cam_cols, 128), 0) + me * cam_cols
    same = (iota((128, 128), 0) >> 4) == (iota((128, 128), 1) >> 4)
    lane = iota((1, 128), 1)
    inner = lane & 15
    digit = jnp.where(inner < 6, inner, inner - 6)
    lefts, lows, rights = [], [], []
    for j in range(n_edge):
        spots = jnp.full((1, 128), -1, jnp.int32)
        for e in range(edges):
            source = (j * frames + meta_s[j, 0, SOURCE + e]) * 6
            target = (meta_s[j, 0, OWNER + e] * frames + meta_s[j, 0, TARGET + e]) * 6
            here = jnp.where(inner < 6, source, target) + digit
            spots = jnp.where(((lane >> 4) == e) & (inner < 12), here, spots)
        mine = (col_id == spots).astype(F32)
        left = jnp.concatenate([(row_id == spots).astype(F32), mine], axis=0).astype(BF)
        stack = jnp.where(same, jnp.concatenate([gall[j]] * 8, axis=0), 0.0)
        picked = nn(
            jnp.concatenate([left, left], axis=1), jnp.concatenate(halves(stack), axis=0)
        )
        high, low = halves(picked)
        lefts.append(high)
        lows.append(low)
        rights.append(mine.astype(BF))
    placed = nt(jnp.concatenate(lefts + lows, axis=1), jnp.concatenate(rights + rights, axis=1))
    fetch.wait()
    stores = [
        pltpu.make_async_copy(held.at[e], out_hidden.at[meta_s[me, 0, PLACE + e]], sem.at[e])
        for e in range(edges)
    ]
    for store in stores:
        store.start()
    cam = placed[0:cam_rows]
    row_frame = sixth(iota((cam_rows, cam_cols), 0) + tile * cam_rows)
    col_frame = sixth(iota((cam_rows, cam_cols), 1) + me * cam_cols)
    out_cam[...] = jnp.where(row_frame == col_frame, 0.0, cam)
    own = placed[cam_rows:]
    own_row = sixth(iota((cam_cols, cam_cols), 0))
    own_col = sixth(iota((cam_cols, cam_cols), 1))
    own = jnp.where(own_row == own_col, own, 0.0)
    wide_row = iota((cam_cols, 128), 0)
    wide_lane = iota((cam_cols, 128), 1)
    row_in = wide_row.astype(F32) - 6.0 * sixth(wide_row)
    lane_of = sixth(wide_lane)
    lane_in = wide_lane.astype(F32) - 6.0 * lane_of
    gather = one_hot(row_in == lane_in)
    high, low = halves(own)
    spread = jnp.where(row_in == lane_of, nn(high, gather) + nn(low, gather), 0.0)
    fold = one_hot(
        sixth(iota((frames, cam_cols), 1)) == iota((frames, cam_cols), 0).astype(F32)
    )
    high, low = halves(spread)
    out_diag[...] = (nn(fold, high) + nn(fold, low))[:, 0:36]
    for store in stores:
        store.wait()


def per_device(
    features,
    hidden_state,
    edge_source,
    edge_owner,
    edge_target,
    edge_counts,
    corr_weight,
    gate_weight,
    candidate_weight,
    jacobian_weight,
    confidence_weight,
):
    n_edge, n_tile = lax.axis_size("edge"), lax.axis_size("tile")
    edges = hidden_state.shape[0]
    frames, rows, width, chan = features.shape
    slots = max(2, (2 * edges + n_edge - 1) // n_edge)
    assert edges % slots == 0 and edges <= 8 and ASKS + n_edge * slots <= 128
    per = edges // slots
    band = rows * width

    dims = (n_edge, n_tile, edges, frames, rows, width, slots)
    even = (rows + 2 * NEAR + 1) // 2 * 2
    dma = pltpu.SemaphoreType.DMA
    vmem = pl.BlockSpec(memory_space=pltpu.VMEM)
    smem = pl.BlockSpec(memory_space=pltpu.SMEM)
    hbm = pl.BlockSpec(memory_space=pl.ANY)

    inputs = (
        ("owner_h", edge_owner[:, 0], hbm),
        ("target_h", edge_target, hbm),
        ("source_h", edge_source, hbm),
        ("count_h", edge_counts, hbm),
        ("feat_h", features.reshape(frames, band, chan), hbm),
        ("hidden_h", hidden_state.reshape(edges, band, chan), hbm),
        ("corr_h", corr_weight, hbm),
        ("gate_w", gate_weight, hbm),
        ("cand_w", candidate_weight, hbm),
        ("jac_h", jacobian_weight.T, hbm),
        ("conf_h", confidence_weight.T, hbm),
    )
    outputs = (
        ("out_hidden", (edges, band, chan), BF, hbm),
        ("gall", (n_edge, 16, 128), F32, vmem),
        ("meta_all", (n_edge, 1, 128), jnp.int32, hbm),
    )
    near, far = len(reach(NEAR, rows)), len(reach(FAR, rows))
    scratch = {
        "owner_s": pltpu.SMEM((edges,), jnp.int32),
        "target_s": pltpu.SMEM((edges,), jnp.int32),
        "source_s": pltpu.SMEM((edges,), jnp.int32),
        "count_s": pltpu.SMEM((1,), jnp.int32),
        "corr_in": pltpu.VMEM(corr_weight.shape, BF),
        "jac_in": pltpu.VMEM(jacobian_weight.shape[::-1], BF),
        "conf_in": pltpu.VMEM(confidence_weight.shape[::-1], BF),
        "row_v": pltpu.VMEM((1, 128), jnp.int32),
        "row_s": pltpu.SMEM((1, 128), jnp.int32),
        "meta_s": pltpu.SMEM((n_edge, 1, 128), jnp.int32),
        "feat": pltpu.VMEM((frames, band, chan), BF),
        "held": pltpu.VMEM((edges, band, chan), BF),
        "send": pltpu.VMEM(((n_edge - 1) * slots, band, chan), BF),
        "text": pltpu.VMEM((edges, (even + 2 * RADIUS + 3) // 4 * 4 * width, chan), BF),
        "sext": pltpu.VMEM((edges, even * width, chan), BF),
        "hext": pltpu.VMEM((edges, (rows + 2 * NEAR) * width, chan), BF),
        "rext": pltpu.VMEM((per, (rows + 2) * width, chan), BF),
        "x3": pltpu.VMEM((per, (rows + 2 * NEAR) * width, 3 * chan), BF),
        "wh": pltpu.VMEM((9 * chan, 2 * chan), BF),
        "wm": pltpu.VMEM((9 * chan, 2 * chan), BF),
        "wc": pltpu.VMEM((6 * chan, 3 * chan), BF),
        "corr_w": pltpu.VMEM((128, chan), BF),
        "head_w": pltpu.VMEM((64, chan), BF),
        "gpre": pltpu.VMEM((edges, (rows + 2) * width, 2 * chan), F32),
        "upd": pltpu.VMEM((per, band, chan), F32),
        "jall": pltpu.VMEM((128, 2 * band), BF),
        "wall": pltpu.VMEM((128, 2 * band), BF),
        "gpart": pltpu.VMEM((16, 128), F32),
        "gtile": pltpu.VMEM((n_tile, 16, 128), F32),
        "gsum": pltpu.VMEM((16, 128), F32),
        "l_in": dma((5,)),
        "l_w": dma((36,)),
        "l_ints": dma((4,)),
        "l_row": dma,
        "l_meta": dma,
        "l_own": dma,
        "l_out": dma,
        "s_meta": dma((n_edge,)),
        "r_meta": dma((n_edge,)),
        "s_feat": dma((n_edge, slots)),
        "r_feat": dma((n_edge, slots)),
        "s_gt": dma((n_tile,)),
        "r_gt": dma((n_tile,)),
        "s_ge": dma((n_edge,)),
        "r_ge": dma((n_edge,)),
    }
    for s in range(slots):
        scratch[f"text{s}"] = pltpu.VMEM((n_edge - 1, band, chan), BF)
    for key, count in (("h", near), ("s", near), ("t", far)):
        for name in (f"s_{key}up", f"r_{key}up", f"s_{key}dn", f"r_{key}dn"):
            scratch[name] = dma((count, edges))
    names = [i[0] for i in inputs] + [o[0] for o in outputs] + list(scratch)
    state, gall, meta_all = pl.pallas_call(
        functools.partial(kernel, dims, names),
        out_shape=tuple(jax.ShapeDtypeStruct(shape, kind) for _, shape, kind, _ in outputs),
        in_specs=[spec for _, _, spec in inputs],
        out_specs=tuple(spec for _, _, _, spec in outputs),
        scratch_shapes=list(scratch.values()),
        compiler_params=pltpu.CompilerParams(
            collective_id=0, has_side_effects=True, vmem_limit_bytes=56 * 1024 * 1024
        ),
    )(*[value for _, value, _ in inputs])
    hidden_next, cam, diag = pl.pallas_call(
        functools.partial(assemble, dims),
        out_shape=(
            jax.ShapeDtypeStruct((edges, band, chan), BF),
            jax.ShapeDtypeStruct((frames * n_edge * 6 // n_tile, frames * 6), F32),
            jax.ShapeDtypeStruct((frames, 36), F32),
        ),
        in_specs=[smem, vmem, hbm],
        out_specs=(hbm, vmem, vmem),
        scratch_shapes=[pltpu.VMEM((edges, band, chan), BF), dma((edges + 1,))],
    )(meta_all, gall, state)
    return hidden_next.reshape(hidden_state.shape), cam, diag


def solution(mesh):
    placed = (
        P("edge", "tile", None, None),
        P("edge", "tile", None, None),
        P("edge"),
        P("edge", None),
        P("edge"),
        P("edge"),
        P(),
        P(),
        P(),
        P(),
        P(),
    )
    return jax.shard_map(
        per_device,
        mesh=mesh,
        in_specs=placed,
        out_specs=(P("edge", "tile", None, None), P("tile", "edge"), P("edge", None)),
        check_vma=False,
    )
```

```python
import functools
import types

import jax
import jax.numpy as jnp
from jax import lax
from jax.experimental import pallas as pl
from jax.experimental.pallas import tpu as pltpu
from jax.sharding import PartitionSpec as P

MAPH = 48
WINDOW = 7
RADIUS = WINDOW // 2
NEAR = 2
FAR = RADIUS + NEAR
OWNER, TARGET, SOURCE, PLACE, GROUP, REL, ASKS = 0, 8, 16, 32, 40, 48, 64
MESH = pl.DeviceIdType.MESH
BF = jnp.bfloat16
F32 = jnp.float32


def nt(a, b):
    return lax.dot_general(a, b, (((1,), (1,)), ((), ())), preferred_element_type=F32)


def nn(a, b):
    return lax.dot_general(a, b, (((1,), (0,)), ((), ())), preferred_element_type=F32)


def iota(shape, dim):
    return lax.broadcasted_iota(jnp.int32, shape, dim)


def sixth(index):
    return jnp.floor((index.astype(F32) + 0.5) * (1.0 / 6.0))


def one_hot(cond):
    return cond.astype(F32).astype(BF)


def each(count, body):
    def step(i, carry):
        body(i)
        return carry

    lax.fori_loop(0, count, step, 0)


def reach(halo, rows):
    return [min(rows, halo - d * rows) for d in range((halo + rows - 1) // rows)]


def kernel(dims, names, *refs):
    n_edge, n_tile, edges, frames, rows, width, slots = dims
    r = types.SimpleNamespace(**dict(zip(names, refs)))
    band = rows * width
    per = edges // slots
    me = lax.axis_index("edge")
    tile = lax.axis_index("tile")
    texts = [getattr(r, f"text{s}") for s in range(slots)]

    ints = [
        pltpu.make_async_copy(r.owner_h, r.owner_s, r.l_ints.at[0]),
        pltpu.make_async_copy(r.target_h, r.target_s, r.l_ints.at[1]),
        pltpu.make_async_copy(r.source_h, r.source_s, r.l_ints.at[2]),
        pltpu.make_async_copy(r.count_h, r.count_s, r.l_ints.at[3]),
    ]
    loads = [
        pltpu.make_async_copy(r.feat_h, r.feat, r.l_in.at[0]),
        pltpu.make_async_copy(
            r.hidden_h, r.hext.at[:, pl.ds(NEAR * width, band)], r.l_in.at[1]
        ),
        pltpu.make_async_copy(r.corr_h, r.corr_in, r.l_in.at[2]),
        pltpu.make_async_copy(r.jac_h, r.jac_in, r.l_in.at[3]),
        pltpu.make_async_copy(r.conf_h, r.conf_in, r.l_in.at[4]),
    ]
    first, second = pl.ds(0, 128), pl.ds(128, 128)
    fills = [
        pltpu.make_async_copy(r.gate_w.at[:, :, first], r.wh, r.l_w.at[0]),
        pltpu.make_async_copy(r.gate_w.at[:, :, second], r.wm, r.l_w.at[1]),
    ]
    for part, at in enumerate((first, second)):
        for b in range(3):
            fills.append(
                pltpu.make_async_copy(
                    r.cand_w.at[:, b, at], r.wc.at[part, :, :, pl.ds(b * 128, 128)], r.l_w.at[2]
                )
            )
    filled = fills[:2] + [pltpu.make_async_copy(r.wc, r.wc, r.l_w.at[2])]
    for load in ints + loads + fills:
        load.start()

    barrier = pltpu.get_barrier_semaphore()
    for rel in range(1, n_edge):
        pl.semaphore_signal(
            barrier, inc=1, device_id=((me + rel) % n_edge, tile), device_id_type=MESH
        )
    for rel in range(1, n_tile):
        pl.semaphore_signal(
            barrier, inc=1, device_id=(me, (tile + rel) % n_tile), device_id_type=MESH
        )

    for load in ints:
        load.wait()
    owner = [r.owner_s[e] for e in range(edges)]
    rel_of = [(owner[e] - me + n_edge) % n_edge for e in range(edges)]
    rank, group = [], []
    for e in range(edges):
        before = jnp.int32(0)
        for k in range(e):
            before = before + (owner[k] == owner[e]).astype(jnp.int32)
        rank.append(jnp.minimum(before, slots - 1))
        group.append(jnp.where(rel_of[e] == 0, 0, rank[e] + 1))
    lane = iota((1, 128), 1)
    row = jnp.zeros((1, 128), jnp.int32)
    for e in range(edges):
        spot = jnp.int32(0)
        for k in range(edges):
            if k < e:
                spot = spot + (group[k] <= group[e]).astype(jnp.int32)
            elif k > e:
                spot = spot + (group[k] < group[e]).astype(jnp.int32)
        goal = r.target_s[e]
        fields = (
            (OWNER, owner[e]),
            (TARGET, goal),
            (SOURCE, r.source_s[e]),
            (PLACE, jnp.int32(e)),
            (GROUP, group[e]),
            (REL, rel_of[e]),
        )
        for base, value in fields:
            row = jnp.where(lane == base + spot, value, row)
        row = jnp.where(lane == ASKS + rel_of[e] * slots + rank[e], goal, row)
    r.row_v[...] = row
    mine = pltpu.make_async_copy(r.row_v, r.row_s, r.l_row)
    mine.start()

    pl.semaphore_wait(barrier, n_edge + n_tile - 2)

    def remote(src, dst, send_sem, recv_sem, edge_id, tile_id):
        return pltpu.make_async_remote_copy(
            src_ref=src,
            dst_ref=dst,
            send_sem=send_sem,
            recv_sem=recv_sem,
            device_id=(edge_id, tile_id),
            device_id_type=MESH,
        )

    def meta_copy(rel):
        return remote(
            r.row_v, r.meta_s.at[me], r.s_meta.at[rel - 1], r.r_meta.at[rel - 1],
            (me + rel) % n_edge, tile,
        )

    for rel in range(1, n_edge):
        meta_copy(rel).start()

    class Halo:
        def __init__(self, halo, lot, buf, source, sems):
            self.halo, self.lot, self.buf, self.source, self.sems = halo, lot, buf, source, sems
            self.counts = reach(halo, rows)

        def copies(self, i, lot):
            which = pl.ds(i * lot, lot)
            for d, count in enumerate(self.counts):
                far, lines = d + 1, count * width
                s_up, r_up, s_dn, r_dn = self.sems
                up = remote(
                    self.source(which, 0, lines),
                    self.buf.at[which, pl.ds((self.halo + far * rows) * width, lines)],
                    s_up.at[d], r_up.at[d, i], me, tile - far,
                )
                dn = remote(
                    self.source(which, band - lines, lines),
                    self.buf.at[which, pl.ds((self.halo - d * rows - count) * width, lines)],
                    s_dn.at[d], r_dn.at[d, i], me, tile + far,
                )
                yield tile >= far, tile + far < n_tile, up, dn

        def start(self, i):
            for above, below, up, dn in self.copies(i, self.lot):
                pl.when(above)(up.start)
                pl.when(below)(dn.start)

        def received(self, i):
            for above, below, up, dn in self.copies(i, self.lot):
                pl.when(below)(up.wait_recv)
                pl.when(above)(dn.wait_recv)

        def sent(self):
            for above, below, up, dn in self.copies(0, edges):
                pl.when(above)(up.wait_send)
                pl.when(below)(dn.wait_send)

        def clear(self):
            for d, count in enumerate(self.counts):
                far, lines = d + 1, count * width
                zero = jnp.zeros((lines, 128), BF)
                top = (self.halo - d * rows - count) * width
                low = (self.halo + far * rows) * width

                @pl.when(tile < far)
                def _():
                    def clear_top(e):
                        self.buf[e, pl.ds(top, lines)] = zero

                    each(edges, clear_top)

                @pl.when(tile + far >= n_tile)
                def _():
                    def clear_low(e):
                        self.buf[e, pl.ds(low, lines)] = zero

                    each(edges, clear_low)

            used = (rows + 2 * self.halo) * width
            spare = self.buf.shape[1] - used
            if spare:

                def clear_pad(e):
                    self.buf[e, pl.ds(used, spare)] = jnp.zeros((spare, 128), BF)

                each(edges, clear_pad)

    def inner(buf, halo):
        return lambda which, at, lines: buf.at[which, pl.ds(halo * width + at, lines)]

    hid = Halo(
        NEAR, edges, r.hext, lambda which, at, lines: r.hidden_h.at[which, pl.ds(at, lines)],
        (r.s_hup, r.r_hup, r.s_hdn, r.r_hdn),
    )
    src = Halo(
        NEAR, edges, r.sext, inner(r.sext, NEAR), (r.s_sup, r.r_sup, r.s_sdn, r.r_sdn)
    )
    txt = Halo(FAR, 1, r.text, inner(r.text, FAR), (r.s_tup, r.r_tup, r.s_tdn, r.r_tdn))

    hid.start(0)
    own_row = pltpu.make_async_copy(r.row_v, r.meta_s.at[me], r.l_own)
    own_row.start()
    for rel in range(1, n_edge):
        remote(
            r.row_v, r.meta_s.at[(me - rel + n_edge) % n_edge], r.s_meta.at[rel - 1],
            r.r_meta.at[rel - 1], (me + rel) % n_edge, tile,
        ).wait_recv()
    loads[0].wait()

    others = n_edge - 1

    def feat_copy(rel, s):
        return remote(
            r.send.at[s * others + rel - 1], texts[s].at[rel - 1],
            r.s_feat, r.r_feat.at[s], (me - rel + n_edge) % n_edge, tile,
        )

    def feat_group(s):
        return remote(
            r.send.at[pl.ds(s * others, others)], texts[s],
            r.s_feat, r.r_feat.at[s], (me + 1) % n_edge, tile,
        )

    for s in range(slots):
        for rel in range(1, n_edge):
            peer = (me - rel + n_edge) % n_edge
            r.send[s * others + rel - 1] = r.feat[r.meta_s[peer, 0, ASKS + rel * slots + s]]
        for rel in range(1, n_edge):
            feat_copy(rel, s).start()

    mine.wait()
    own_row.wait()
    tables = pltpu.make_async_copy(r.meta_s, r.meta_all, r.l_meta)
    tables.start()

    def take_source(e):
        r.sext[e, pl.ds(NEAR * width, band)] = r.feat[r.row_s[0, SOURCE + e]]

    each(edges, take_source)
    src.start(0)
    for halo in (hid, src, txt):
        halo.clear()

    for load in loads[2:]:
        load.wait()

    spot = (iota((128, 64), 0) + 4) & 127
    along = ((spot >> 3) & 3) * 2 + (spot >> 6) - ((spot >> 5) & 1)
    across = WINDOW - 1 - (spot & 7)
    fits = (across >= 0) & (along >= 0) & (along < WINDOW)
    pick = (iota((128, 64), 1) == along * WINDOW + across) & fits
    lookup = jnp.concatenate(
        [r.corr_in[...].astype(F32), jnp.zeros((64 - WINDOW * WINDOW, 128), F32)], axis=0
    ).astype(BF)
    r.corr_w[...] = nn(one_hot(pick), lookup).astype(BF)

    place12 = iota((32, 64), 0)
    which = place12 >> 4
    within = place12 & 15
    name12 = iota((32, 64), 1)
    pick_j = (within < 12) & (name12 == which * 12 + within)
    padded_jac = jnp.concatenate(
        [r.jac_in[...].astype(F32), jnp.zeros((40, 128), F32)], axis=0
    ).astype(BF)
    conf_wide = r.conf_in[...].astype(F32)
    tall = iota((32, 128), 0)
    conf_rows = jnp.where(
        tall < 16,
        jnp.broadcast_to(conf_wide[0:1], (32, 128)),
        jnp.broadcast_to(conf_wide[1:2], (32, 128)),
    )
    r.head_w[...] = jnp.concatenate(
        [nn(one_hot(pick_j), padded_jac), jnp.where((tall & 15) < 12, conf_rows, 0.0)], axis=0
    ).astype(BF)

    def nudge(wide, by):
        lines = wide.shape[0]
        column = iota((lines, 128), 0) & (width - 1)
        edge = 0 if by == 1 else width - 1
        return jnp.where(column == edge, 0.0, pltpu.roll(wide, by % lines, 0))

    def spread(value, out):
        lines = value.shape[0]
        wide = value.astype(F32)
        out[0:lines, 0:128] = nudge(wide, 1).astype(BF)
        out[0:lines, 128:256] = value.astype(BF)
        out[0:lines, 256:384] = nudge(wide, -1).astype(BF)

    def windows(x3, q, out_rows):
        size = out_rows * width
        return jnp.concatenate([x3[q, a * width : a * width + size] for a in range(3)], axis=1)

    wide_band = (rows + 2) * width

    def state_part(p):
        for q in range(per):
            e = p * per + q
            spread(r.hext[r.row_s[0, PLACE + e]], r.x3.at[q])
            r.gpre[e] = nn(windows(r.x3, q, rows + 2), r.wh[...].reshape(9 * 128, 256))

    loads[1].wait()
    for fill in filled:
        fill.wait()
    flip_row, flip_col = iota((2 * width, 2 * width), 0), iota((2 * width, 2 * width), 1)
    flip = one_hot(
        (flip_row // width == flip_col // width)
        & ((flip_row & (width - 1)) + (flip_col & (width - 1)) == width - 1)
    )

    def take_target(e, upto):
        value = r.feat[r.row_s[0, TARGET + e]]
        at = jnp.maximum(r.row_s[0, REL + e] - 1, 0)
        for s in range(upto + 1):
            value = jnp.where(r.row_s[0, GROUP + e] == s + 1, texts[s][at], value)
        for first in range(0, band, 2 * width):
            count = min(2 * width, band - first)
            r.text[e, pl.ds(FAR * width + first, count)] = nn(
                flip[0:count, 0:count], value[first : first + count]
            ).astype(BF)
        txt.start(e)

    def take(s):
        feat_group(s).wait_recv()
        for q in range(per):
            take_target(s * per + q, s)

    hid.received(0)
    each(slots // 2, state_part)
    take(0)
    each(slots - slots // 2, lambda p: state_part(p + slots // 2))
    src.received(0)

    lane_w = (iota((width, 128), 1) + 4) & 127
    col_w = iota((width, 128), 0) + RADIUS - (lane_w & 7)
    in_map = (col_w >= 0) & (col_w < width) & ((lane_w & 7) < WINDOW)
    scaled = [
        jnp.where(in_map & (((lane_w >> 5) & 1) == par), 128.0 ** (-0.5), 0.0) for par in range(2)
    ]
    slot_w = (lane_w >> 3) & 3
    pairs_of = (rows + 2 * NEAR + 1) // 2
    quads_of = r.text.shape[1] // (4 * width)
    used_rows = (rows + 2 * NEAR) * width

    def motion_of(e, q):
        tables, starts = [], []
        for m in range(quads_of):
            first, last = max(0, 2 * m - 3), min(pairs_of - 1, 2 * m + 1)
            starts.append(first)
            tables.append(
                nt(
                    r.sext[e, pl.ds(2 * first * width, 2 * (last - first + 1) * width)],
                    r.text[e, pl.ds(4 * m * width, 4 * width)],
                )
            )
        lines = []
        for k in range(pairs_of):
            for par in range(2):
                found = None
                for g in range(4):
                    m, h = divmod(k + g, 2)
                    at = (2 * (k - starts[m]) + par) * width
                    piece = tables[m][at : at + width, h * 128 : (h + 1) * 128]
                    moved = pltpu.roll(
                        piece, width + 8 * g + 32 * par, 1, stride=1, stride_axis=0
                    )
                    found = moved if g == 0 else jnp.where(slot_w == g, moved, found)
                lines.append((found * scaled[par]).astype(BF))
        value = nn(jnp.concatenate(lines, axis=0), r.corr_w[...])
        spread(jnp.maximum(value[0:used_rows], 0.0), r.x3.at[q])

    def update(p):
        for q in range(per):
            txt.received(p * per + q)
            motion_of(p * per + q, q)
        for q in range(per):
            e = p * per + q
            before = r.gpre[e] + nn(windows(r.x3, q, rows + 2), r.wm[...].reshape(9 * 128, 256))
            r.upd[q] = 0.5 * jnp.tanh(0.5 * before[width : width + band, 0:128]) + 0.5
            reset = 0.5 * jnp.tanh(0.5 * before[:, 128:256]) + 0.5
            state = r.hext[r.row_s[0, PLACE + e], pl.ds(width, wide_band)].astype(F32)
            r.rext[q] = (reset * state).astype(BF)
        for q in range(per):
            e = p * per + q
            part = nn(
                jnp.concatenate(
                    [r.rext[q, a * width : a * width + band] for a in range(3)]
                    + [
                        r.x3[q, (a + 1) * width : (a + 1) * width + band, 128:256]
                        for a in range(3)
                    ],
                    axis=1,
                ),
                r.wc[...].reshape(6 * 128, 384),
            )
            candidate = jnp.tanh(
                nudge(part[:, 0:128], 1) + part[:, 128:256] + nudge(part[:, 256:384], -1)
            )
            gate = r.upd[q]
            place = r.row_s[0, PLACE + e]
            state = r.hext[place, pl.ds(NEAR * width, band)]
            fresh = ((1.0 - gate) * state.astype(F32) + gate * candidate).astype(BF)
            used = (place < r.count_s[0]).astype(F32)
            live = jnp.full((band, 128), used) > 0.5
            r.held[e] = jnp.where(live, fresh, state)
            heads = nt(r.head_w[...], fresh)
            jac = heads[0:32]
            weighted = jac * jax.nn.softplus(heads[32:64])
            at16 = pl.ds(pl.multiple_of(e * 16, 16), 16)
            r.jall[at16] = jnp.concatenate([jac[0:16], jac[16:32]], axis=1).astype(BF)
            r.wall[at16] = jnp.concatenate([weighted[0:16], weighted[16:32]], axis=1).astype(BF)

    def stage(p):
        for s in range(1, slots):

            @pl.when(p == s - 1)
            def _():
                take(s)

        update(p)

    each(slots, stage)
    store = pltpu.make_async_copy(r.held, r.out_hidden, r.l_out)
    store.start()

    same = (iota((128, 128), 0) >> 4) == (iota((128, 128), 1) >> 4)
    square = jnp.where(same, nt(r.wall[...], r.jall[...]), 0.0)
    blocks = square[0:16]
    for e in range(1, edges):
        blocks = blocks + square[e * 16 : (e + 1) * 16]
    blocks = blocks * (1.0 / (MAPH * width))
    of = iota((16, 128), 1) >> 4
    for e in range(edges):
        used = (r.row_s[0, PLACE + e] < r.count_s[0]).astype(jnp.int32)
        blocks = jnp.where((of == e) & (jnp.full((16, 128), used) == 0), 0.0, blocks)
    r.gpart[...] = blocks

    def tile_copy(rel):
        return remote(
            r.gpart, r.gtile.at[tile], r.s_gt, r.r_gt, me, (tile + rel) % n_tile
        )

    def all_tiles():
        some = r.gtile.at[pl.ds(0, n_tile - 1)]
        return remote(some, some, r.s_gt, r.r_gt, me, (tile + 1) % n_tile)

    for rel in range(1, n_tile):
        tile_copy(rel).start()
    r.gtile[tile] = r.gpart[...]
    all_tiles().wait_recv()
    total = r.gtile[0]
    for k in range(1, n_tile):
        total = total + r.gtile[k]
    r.gsum[...] = total

    def edge_copy(rel):
        return remote(r.gsum, r.gall.at[me], r.s_ge, r.r_ge, (me + rel) % n_edge, tile)

    def all_edges():
        some = r.gall.at[pl.ds(0, others)]
        return remote(some, some, r.s_ge, r.r_ge, (me + 1) % n_edge, tile)

    for rel in range(1, n_edge):
        edge_copy(rel).start()
    r.gall[me] = total
    all_edges().wait_recv()

    store.wait()
    tables.wait()
    for rel in range(1, n_edge):
        meta_copy(rel).wait_send()
    for s in range(slots):
        feat_group(s).wait_send()
    all_tiles().wait_send()
    all_edges().wait_send()
    for halo in (hid, src, txt):
        halo.sent()


def halves(value):
    high = value.astype(BF)
    return high, (value - high.astype(F32)).astype(BF)


def assemble(dims, meta_s, gall, hidden_h, out_hidden, out_cam, out_diag, held, sem):
    n_edge, n_tile, edges, frames, rows, width, slots = dims
    me = lax.axis_index("edge")
    tile = lax.axis_index("tile")
    fetch = pltpu.make_async_copy(hidden_h, held, sem.at[0])
    fetch.start()
    cam_rows, cam_cols = out_cam.shape
    row_id = iota((cam_rows, 128), 0) + tile * cam_rows
    col_id = iota((cam_cols, 128), 0) + me * cam_cols
    same = (iota((128, 128), 0) >> 4) == (iota((128, 128), 1) >> 4)
    lane = iota((1, 128), 1)
    inner = lane & 15
    digit = jnp.where(inner < 6, inner, inner - 6)
    lefts, lows, rights = [], [], []
    for j in range(n_edge):
        spots = jnp.full((1, 128), -1, jnp.int32)
        for e in range(edges):
            source = (j * frames + meta_s[j, 0, SOURCE + e]) * 6
            target = (meta_s[j, 0, OWNER + e] * frames + meta_s[j, 0, TARGET + e]) * 6
            here = jnp.where(inner < 6, source, target) + digit
            spots = jnp.where(((lane >> 4) == e) & (inner < 12), here, spots)
        mine = (col_id == spots).astype(F32)
        left = jnp.concatenate([(row_id == spots).astype(F32), mine], axis=0).astype(BF)
        stack = jnp.where(same, jnp.concatenate([gall[j]] * 8, axis=0), 0.0)
        picked = nn(
            jnp.concatenate([left, left], axis=1), jnp.concatenate(halves(stack), axis=0)
        )
        high, low = halves(picked)
        lefts.append(high)
        lows.append(low)
        rights.append(mine.astype(BF))
    placed = nt(jnp.concatenate(lefts + lows, axis=1), jnp.concatenate(rights + rights, axis=1))
    fetch.wait()
    stores = [
        pltpu.make_async_copy(held.at[e], out_hidden.at[meta_s[me, 0, PLACE + e]], sem.at[1])
        for e in range(edges)
    ]
    for store in stores:
        store.start()
    cam = placed[0:cam_rows]
    row_frame = sixth(iota((cam_rows, cam_cols), 0) + tile * cam_rows)
    col_frame = sixth(iota((cam_rows, cam_cols), 1) + me * cam_cols)
    out_cam[...] = jnp.where(row_frame == col_frame, 0.0, cam)
    own = placed[cam_rows:]
    own_row = sixth(iota((cam_cols, cam_cols), 0))
    own_col = sixth(iota((cam_cols, cam_cols), 1))
    own = jnp.where(own_row == own_col, own, 0.0)
    wide_row = iota((cam_cols, 128), 0)
    wide_lane = iota((cam_cols, 128), 1)
    row_in = wide_row.astype(F32) - 6.0 * sixth(wide_row)
    lane_of = sixth(wide_lane)
    lane_in = wide_lane.astype(F32) - 6.0 * lane_of
    gather = one_hot(row_in == lane_in)
    high, low = halves(own)
    spread = jnp.where(row_in == lane_of, nn(high, gather) + nn(low, gather), 0.0)
    fold = one_hot(
        sixth(iota((frames, cam_cols), 1)) == iota((frames, cam_cols), 0).astype(F32)
    )
    high, low = halves(spread)
    out_diag[...] = (nn(fold, high) + nn(fold, low))[:, 0:36]
    pltpu.make_async_copy(held, out_hidden, sem.at[1]).wait()


def per_device(
    features,
    hidden_state,
    edge_source,
    edge_owner,
    edge_target,
    edge_counts,
    corr_weight,
    gate_weight,
    candidate_weight,
    jacobian_weight,
    confidence_weight,
):
    n_edge, n_tile = lax.axis_size("edge"), lax.axis_size("tile")
    edges = hidden_state.shape[0]
    frames, rows, width, chan = features.shape
    slots = max(2, (2 * edges + n_edge - 1) // n_edge)
    assert edges % slots == 0 and edges <= 8 and ASKS + n_edge * slots <= 128
    per = edges // slots
    band = rows * width

    dims = (n_edge, n_tile, edges, frames, rows, width, slots)
    even = (rows + 2 * NEAR + 1) // 2 * 2
    dma = pltpu.SemaphoreType.DMA
    vmem = pl.BlockSpec(memory_space=pltpu.VMEM)
    smem = pl.BlockSpec(memory_space=pltpu.SMEM)
    hbm = pl.BlockSpec(memory_space=pl.ANY)

    inputs = (
        ("owner_h", edge_owner[:, 0], hbm),
        ("target_h", edge_target, hbm),
        ("source_h", edge_source, hbm),
        ("count_h", edge_counts, hbm),
        ("feat_h", features.reshape(frames, band, chan), hbm),
        ("hidden_h", hidden_state.reshape(edges, band, chan), hbm),
        ("corr_h", corr_weight, hbm),
        ("gate_w", gate_weight, hbm),
        ("cand_w", candidate_weight, hbm),
        ("jac_h", jacobian_weight.T, hbm),
        ("conf_h", confidence_weight.T, hbm),
    )
    outputs = (
        ("out_hidden", (edges, band, chan), BF, hbm),
        ("gall", (n_edge, 16, 128), F32, vmem),
        ("meta_all", (n_edge, 1, 128), jnp.int32, hbm),
    )
    near, far = len(reach(NEAR, rows)), len(reach(FAR, rows))
    scratch = {
        "owner_s": pltpu.SMEM((edges,), jnp.int32),
        "target_s": pltpu.SMEM((edges,), jnp.int32),
        "source_s": pltpu.SMEM((edges,), jnp.int32),
        "count_s": pltpu.SMEM((1,), jnp.int32),
        "corr_in": pltpu.VMEM(corr_weight.shape, BF),
        "jac_in": pltpu.VMEM(jacobian_weight.shape[::-1], BF),
        "conf_in": pltpu.VMEM(confidence_weight.shape[::-1], BF),
        "row_v": pltpu.VMEM((1, 128), jnp.int32),
        "row_s": pltpu.SMEM((1, 128), jnp.int32),
        "meta_s": pltpu.SMEM((n_edge, 1, 128), jnp.int32),
        "feat": pltpu.VMEM((frames, band, chan), BF),
        "held": pltpu.VMEM((edges, band, chan), BF),
        "send": pltpu.VMEM(((n_edge - 1) * slots, band, chan), BF),
        "text": pltpu.VMEM((edges, (even + 2 * RADIUS + 3) // 4 * 4 * width, chan), BF),
        "sext": pltpu.VMEM((edges, even * width, chan), BF),
        "hext": pltpu.VMEM((edges, (rows + 2 * NEAR) * width, chan), BF),
        "rext": pltpu.VMEM((per, (rows + 2) * width, chan), BF),
        "x3": pltpu.VMEM((per, (rows + 2 * NEAR) * width, 3 * chan), BF),
        "wh": pltpu.VMEM((3, 3, chan, 2 * chan), BF),
        "wm": pltpu.VMEM((3, 3, chan, 2 * chan), BF),
        "wc": pltpu.VMEM((2, 3, chan, 3 * chan), BF),
        "corr_w": pltpu.VMEM((128, chan), BF),
        "head_w": pltpu.VMEM((64, chan), BF),
        "gpre": pltpu.VMEM((edges, (rows + 2) * width, 2 * chan), F32),
        "upd": pltpu.VMEM((per, band, chan), F32),
        "jall": pltpu.VMEM((128, 2 * band), BF),
        "wall": pltpu.VMEM((128, 2 * band), BF),
        "gpart": pltpu.VMEM((16, 128), F32),
        "gtile": pltpu.VMEM((n_tile, 16, 128), F32),
        "gsum": pltpu.VMEM((16, 128), F32),
        "l_in": dma((5,)),
        "l_w": dma((3,)),
        "l_ints": dma((4,)),
        "l_row": dma,
        "l_meta": dma,
        "l_own": dma,
        "l_out": dma,
        "s_meta": dma((n_edge - 1,)),
        "r_meta": dma((n_edge - 1,)),
        "s_feat": dma,
        "r_feat": dma((slots,)),
        "s_gt": dma,
        "r_gt": dma,
        "s_ge": dma,
        "r_ge": dma,
    }
    for s in range(slots):
        scratch[f"text{s}"] = pltpu.VMEM((n_edge - 1, band, chan), BF)
    for key, count, lots in (("h", near, 1), ("s", near, 1), ("t", far, edges)):
        for way in ("up", "dn"):
            scratch[f"s_{key}{way}"] = dma((count,))
            scratch[f"r_{key}{way}"] = dma((count, lots))
    names = [i[0] for i in inputs] + [o[0] for o in outputs] + list(scratch)
    state, gall, meta_all = pl.pallas_call(
        functools.partial(kernel, dims, names),
        out_shape=tuple(jax.ShapeDtypeStruct(shape, kind) for _, shape, kind, _ in outputs),
        in_specs=[spec for _, _, spec in inputs],
        out_specs=tuple(spec for _, _, _, spec in outputs),
        scratch_shapes=list(scratch.values()),
        compiler_params=pltpu.CompilerParams(
            collective_id=0, has_side_effects=True, vmem_limit_bytes=56 * 1024 * 1024
        ),
    )(*[value for _, value, _ in inputs])
    hidden_next, cam, diag = pl.pallas_call(
        functools.partial(assemble, dims),
        out_shape=(
            jax.ShapeDtypeStruct((edges, band, chan), BF),
            jax.ShapeDtypeStruct((frames * n_edge * 6 // n_tile, frames * 6), F32),
            jax.ShapeDtypeStruct((frames, 36), F32),
        ),
        in_specs=[smem, vmem, hbm],
        out_specs=(hbm, vmem, vmem),
        scratch_shapes=[pltpu.VMEM((edges, band, chan), BF), dma((2,))],
    )(meta_all, gall, state)
    return hidden_next.reshape(hidden_state.shape), cam, diag


def solution(mesh):
    placed = (
        P("edge", "tile", None, None),
        P("edge", "tile", None, None),
        P("edge"),
        P("edge", None),
        P("edge"),
        P("edge"),
        P(),
        P(),
        P(),
        P(),
        P(),
    )
    return jax.shard_map(
        per_device,
        mesh=mesh,
        in_specs=placed,
        out_specs=(P("edge", "tile", None, None), P("tile", "edge"), P("edge", None)),
        check_vma=False,
    )
```

```python
import functools
import types

import jax
import jax.numpy as jnp
from jax import lax
from jax.experimental import pallas as pl
from jax.experimental.pallas import tpu as pltpu
from jax.sharding import PartitionSpec as P

MAPH = 48
WINDOW = 7
RADIUS = WINDOW // 2
NEAR = 2
FAR = RADIUS + NEAR
OWNER, TARGET, SOURCE, SPOT, PLACE, GROUP, REL = 0, 8, 16, 24, 32, 40, 48
MESH = pl.DeviceIdType.MESH
BF = jnp.bfloat16
F32 = jnp.float32


def nt(a, b):
    return lax.dot_general(a, b, (((1,), (1,)), ((), ())), preferred_element_type=F32)


def nn(a, b):
    return lax.dot_general(a, b, (((1,), (0,)), ((), ())), preferred_element_type=F32)


def iota(shape, dim):
    return lax.broadcasted_iota(jnp.int32, shape, dim)


def sixth(index):
    return jnp.floor((index.astype(F32) + 0.5) * (1.0 / 6.0))


def one_hot(cond):
    return cond.astype(F32).astype(BF)


def each(count, body):
    def step(i, carry):
        body(i)
        return carry

    lax.fori_loop(0, count, step, 0)


def reach(halo, rows):
    return [min(rows, halo - d * rows) for d in range((halo + rows - 1) // rows)]


def kernel(dims, names, *refs):
    n_edge, n_tile, edges, frames, rows, width, slots = dims
    r = types.SimpleNamespace(**dict(zip(names, refs)))
    band = rows * width
    per = edges // slots
    me = lax.axis_index("edge")
    tile = lax.axis_index("tile")
    texts = [getattr(r, f"text{s}") for s in range(slots)]

    ints = [
        pltpu.make_async_copy(r.owner_h, r.owner_s, r.l_ints.at[0]),
        pltpu.make_async_copy(r.target_h, r.target_s, r.l_ints.at[1]),
        pltpu.make_async_copy(r.source_h, r.source_s, r.l_ints.at[2]),
        pltpu.make_async_copy(r.count_h, r.count_s, r.l_ints.at[3]),
    ]
    loads = [
        pltpu.make_async_copy(r.feat_h, r.feat, r.l_in.at[0]),
        pltpu.make_async_copy(
            r.hidden_h, r.hext.at[:, pl.ds(NEAR * width, band)], r.l_in.at[1]
        ),
        pltpu.make_async_copy(r.corr_h, r.corr_in, r.l_in.at[2]),
        pltpu.make_async_copy(r.jac_h, r.jac_in, r.l_in.at[3]),
        pltpu.make_async_copy(r.conf_h, r.conf_in, r.l_in.at[4]),
    ]
    first, second = pl.ds(0, 128), pl.ds(128, 128)
    fills = [
        pltpu.make_async_copy(r.gate_w.at[:, :, first], r.wh, r.l_w.at[0]),
        pltpu.make_async_copy(r.gate_w.at[:, :, second], r.wm, r.l_w.at[1]),
    ]
    for part, at in enumerate((first, second)):
        for b in range(3):
            fills.append(
                pltpu.make_async_copy(
                    r.cand_w.at[:, b, at], r.wc.at[part, :, :, pl.ds(b * 128, 128)], r.l_w.at[2]
                )
            )
    filled = fills[:2] + [pltpu.make_async_copy(r.wc, r.wc, r.l_w.at[2])]
    for load in ints + loads + fills:
        load.start()

    barrier = pltpu.get_barrier_semaphore()
    for rel in range(1, n_edge):
        pl.semaphore_signal(
            barrier, inc=1, device_id=((me + rel) % n_edge, tile), device_id_type=MESH
        )
    for rel in range(1, n_tile):
        pl.semaphore_signal(
            barrier, inc=1, device_id=(me, (tile + rel) % n_tile), device_id_type=MESH
        )

    pl.semaphore_wait(barrier, n_edge + n_tile - 2)

    def remote(src, dst, send_sem, recv_sem, edge_id, tile_id):
        return pltpu.make_async_remote_copy(
            src_ref=src,
            dst_ref=dst,
            send_sem=send_sem,
            recv_sem=recv_sem,
            device_id=(edge_id, tile_id),
            device_id_type=MESH,
        )

    def meta_copy(rel):
        return remote(
            r.row_v, r.meta_s.at[me], r.s_meta.at[rel - 1], r.r_meta.at[rel - 1],
            (me + rel) % n_edge, tile,
        )

    others = n_edge - 1
    raws = (r.owner_h, r.target_h)

    def raw_copy(k, rel):
        return remote(
            raws[k], r.raw_s.at[k, me], r.s_raw.at[k, rel - 1], r.r_raw.at[k, rel - 1],
            (me + rel) % n_edge, tile,
        )

    for rel in range(1, n_edge):
        for k in range(2):
            raw_copy(k, rel).start()

    class Halo:
        def __init__(self, halo, lot, buf, source, sems):
            self.halo, self.lot, self.buf, self.source, self.sems = halo, lot, buf, source, sems
            self.counts = reach(halo, rows)

        def copies(self, i, lot):
            which = pl.ds(i * lot, lot)
            for d, count in enumerate(self.counts):
                far, lines = d + 1, count * width
                s_up, r_up, s_dn, r_dn = self.sems
                up = remote(
                    self.source(which, 0, lines),
                    self.buf.at[which, pl.ds((self.halo + far * rows) * width, lines)],
                    s_up.at[d], r_up.at[d, i], me, tile - far,
                )
                dn = remote(
                    self.source(which, band - lines, lines),
                    self.buf.at[which, pl.ds((self.halo - d * rows - count) * width, lines)],
                    s_dn.at[d], r_dn.at[d, i], me, tile + far,
                )
                yield tile >= far, tile + far < n_tile, up, dn

        def start(self, i):
            for above, below, up, dn in self.copies(i, self.lot):
                pl.when(above)(up.start)
                pl.when(below)(dn.start)

        def received(self, i):
            for above, below, up, dn in self.copies(i, self.lot):
                pl.when(below)(up.wait_recv)
                pl.when(above)(dn.wait_recv)

        def sent(self):
            for above, below, up, dn in self.copies(0, edges):
                pl.when(above)(up.wait_send)
                pl.when(below)(dn.wait_send)

        def clear(self):
            for d, count in enumerate(self.counts):
                far, lines = d + 1, count * width
                zero = jnp.zeros((lines, 128), BF)
                top = (self.halo - d * rows - count) * width
                low = (self.halo + far * rows) * width

                @pl.when(tile < far)
                def _():
                    def clear_top(e):
                        self.buf[e, pl.ds(top, lines)] = zero

                    each(edges, clear_top)

                @pl.when(tile + far >= n_tile)
                def _():
                    def clear_low(e):
                        self.buf[e, pl.ds(low, lines)] = zero

                    each(edges, clear_low)

            used = (rows + 2 * self.halo) * width
            spare = self.buf.shape[1] - used
            if spare:

                def clear_pad(e):
                    self.buf[e, pl.ds(used, spare)] = jnp.zeros((spare, 128), BF)

                each(edges, clear_pad)

    def inner(buf, halo):
        return lambda which, at, lines: buf.at[which, pl.ds(halo * width + at, lines)]

    hid = Halo(
        NEAR, edges, r.hext, lambda which, at, lines: r.hidden_h.at[which, pl.ds(at, lines)],
        (r.s_hup, r.r_hup, r.s_hdn, r.r_hdn),
    )
    src = Halo(
        NEAR, edges, r.sext, inner(r.sext, NEAR), (r.s_sup, r.r_sup, r.s_sdn, r.r_sdn)
    )
    txt = Halo(FAR, 1, r.text, inner(r.text, FAR), (r.s_tup, r.r_tup, r.s_tdn, r.r_tdn))

    hid.start(0)
    for rel in range(1, n_edge):
        for k in range(2):
            remote(
                raws[k], r.raw_s.at[k, (me - rel + n_edge) % n_edge], r.s_raw.at[k, rel - 1],
                r.r_raw.at[k, rel - 1], (me + rel) % n_edge, tile,
            ).wait_recv()
    loads[0].wait()

    def asked(peer):
        picks, count = [jnp.int32(0)] * slots, jnp.int32(0)
        for k in range(edges):
            hit = (r.raw_s[0, peer, k] == me).astype(jnp.int32)
            goal = r.raw_s[1, peer, k]
            for s in range(slots):
                picks[s] = jnp.where((hit == 1) & (count == s), goal, picks[s])
            count = count + hit
        return picks

    asks = [asked((me - rel + n_edge) % n_edge) for rel in range(1, n_edge)]

    def feat_copy(rel, s):
        return remote(
            r.send.at[s * others + rel - 1], texts[s].at[rel - 1],
            r.s_feat, r.r_feat.at[s], (me - rel + n_edge) % n_edge, tile,
        )

    def feat_group(s):
        return remote(
            r.send.at[pl.ds(s * others, others)], texts[s],
            r.s_feat, r.r_feat.at[s], (me + 1) % n_edge, tile,
        )

    for s in range(slots):
        for rel in range(1, n_edge):
            r.send[s * others + rel - 1] = r.feat[asks[rel - 1][s]]
        for rel in range(1, n_edge):
            feat_copy(rel, s).start()

    for load in ints:
        load.wait()
    owner = [r.owner_s[e] for e in range(edges)]
    rel_of = [(owner[e] - me + n_edge) % n_edge for e in range(edges)]
    rank, group = [], []
    for e in range(edges):
        before = jnp.int32(0)
        for k in range(e):
            before = before + (owner[k] == owner[e]).astype(jnp.int32)
        rank.append(jnp.minimum(before, slots - 1))
        group.append(jnp.where(rel_of[e] == 0, 0, rank[e] + 1))
    lane = iota((1, 128), 1)
    row = jnp.zeros((1, 128), jnp.int32)
    for e in range(edges):
        spot = jnp.int32(0)
        for k in range(edges):
            if k < e:
                spot = spot + (group[k] <= group[e]).astype(jnp.int32)
            elif k > e:
                spot = spot + (group[k] < group[e]).astype(jnp.int32)
        goal = r.target_s[e]
        fields = (
            (OWNER, owner[e]),
            (TARGET, goal),
            (SOURCE, r.source_s[e]),
            (PLACE, jnp.int32(e)),
            (GROUP, group[e]),
            (REL, rel_of[e]),
        )
        for base, value in fields:
            row = jnp.where(lane == base + spot, value, row)
        row = jnp.where(lane == SPOT + e, spot, row)
    r.row_v[...] = row
    mine = pltpu.make_async_copy(r.row_v, r.row_s, r.l_row)
    mine.start()
    for rel in range(1, n_edge):
        meta_copy(rel).start()
    own_row = pltpu.make_async_copy(r.row_v, r.meta_s.at[me], r.l_own)
    own_row.start()
    mine.wait()

    def take_source(e):
        r.sext[e, pl.ds(NEAR * width, band)] = r.feat[r.row_s[0, SOURCE + e]]

    each(edges, take_source)
    src.start(0)
    for halo in (hid, src, txt):
        halo.clear()

    for load in loads[2:]:
        load.wait()

    spot = (iota((128, 64), 0) + 4) & 127
    along = ((spot >> 3) & 3) * 2 + (spot >> 6) - ((spot >> 5) & 1)
    across = WINDOW - 1 - (spot & 7)
    fits = (across >= 0) & (along >= 0) & (along < WINDOW)
    pick = (iota((128, 64), 1) == along * WINDOW + across) & fits
    lookup = jnp.concatenate(
        [r.corr_in[...].astype(F32), jnp.zeros((64 - WINDOW * WINDOW, 128), F32)], axis=0
    ).astype(BF)
    r.corr_w[...] = nn(one_hot(pick), lookup).astype(BF)

    place12 = iota((32, 64), 0)
    which = place12 >> 4
    within = place12 & 15
    name12 = iota((32, 64), 1)
    pick_j = (within < 12) & (name12 == which * 12 + within)
    padded_jac = jnp.concatenate(
        [r.jac_in[...].astype(F32), jnp.zeros((40, 128), F32)], axis=0
    ).astype(BF)
    conf_wide = r.conf_in[...].astype(F32)
    tall = iota((32, 128), 0)
    conf_rows = jnp.where(
        tall < 16,
        jnp.broadcast_to(conf_wide[0:1], (32, 128)),
        jnp.broadcast_to(conf_wide[1:2], (32, 128)),
    )
    r.head_w[...] = jnp.concatenate(
        [nn(one_hot(pick_j), padded_jac), jnp.where((tall & 15) < 12, conf_rows, 0.0)], axis=0
    ).astype(BF)

    def nudge(wide, by):
        lines = wide.shape[0]
        column = iota((lines, 128), 0) & (width - 1)
        edge = 0 if by == 1 else width - 1
        return jnp.where(column == edge, 0.0, pltpu.roll(wide, by % lines, 0))

    def spread(value, out):
        lines = value.shape[0]
        wide = value.astype(F32)
        out[0:lines, 0:128] = nudge(wide, 1).astype(BF)
        out[0:lines, 128:256] = value.astype(BF)
        out[0:lines, 256:384] = nudge(wide, -1).astype(BF)

    def windows(x3, q, out_rows):
        size = out_rows * width
        return jnp.concatenate([x3[q, a * width : a * width + size] for a in range(3)], axis=1)

    wide_band = (rows + 2) * width

    def state_part(p):
        for q in range(per):
            e = p * per + q
            spread(r.hext[r.row_s[0, PLACE + e]], r.x3.at[q])
            r.gpre[e] = nn(windows(r.x3, q, rows + 2), r.wh[...].reshape(9 * 128, 256))

    loads[1].wait()
    for fill in filled:
        fill.wait()
    flip_row, flip_col = iota((2 * width, 2 * width), 0), iota((2 * width, 2 * width), 1)
    flip = one_hot(
        (flip_row // width == flip_col // width)
        & ((flip_row & (width - 1)) + (flip_col & (width - 1)) == width - 1)
    )

    def take_target(e, upto):
        value = r.feat[r.row_s[0, TARGET + e]]
        at = jnp.maximum(r.row_s[0, REL + e] - 1, 0)
        for s in range(upto + 1):
            value = jnp.where(r.row_s[0, GROUP + e] == s + 1, texts[s][at], value)
        for first in range(0, band, 2 * width):
            count = min(2 * width, band - first)
            r.text[e, pl.ds(FAR * width + first, count)] = nn(
                flip[0:count, 0:count], value[first : first + count]
            ).astype(BF)
        txt.start(e)

    def take(s):
        feat_group(s).wait_recv()
        for q in range(per):
            take_target(s * per + q, s)

    hid.received(0)
    each(slots // 2, state_part)
    take(0)
    each(slots - slots // 2, lambda p: state_part(p + slots // 2))
    src.received(0)

    own_row.wait()
    for rel in range(1, n_edge):
        remote(
            r.row_v, r.meta_s.at[(me - rel + n_edge) % n_edge], r.s_meta.at[rel - 1],
            r.r_meta.at[rel - 1], (me + rel) % n_edge, tile,
        ).wait_recv()
    cam_cols = frames * 6
    cam_rows = r.where_v.shape[1] - cam_cols
    part = iota((cam_rows + cam_cols, 128), 0)
    index = jnp.where(part < cam_rows, part + tile * cam_rows, part - cam_rows + me * cam_cols)
    inside = lane & 15
    digit = jnp.where(inside < 6, inside, inside - 6)

    def place(j):
        spots = jnp.full((1, 128), -1, jnp.int32)
        for e in range(edges):
            source = (j * frames + r.meta_s[j, 0, SOURCE + e]) * 6
            target = (r.meta_s[j, 0, OWNER + e] * frames + r.meta_s[j, 0, TARGET + e]) * 6
            here = jnp.where(inside < 6, source, target) + digit
            spots = jnp.where(((lane >> 4) == e) & (inside < 12), here, spots)
        r.where_v[j] = one_hot(index == spots)

    each(n_edge, place)
    tables = pltpu.make_async_copy(r.where_v, r.where_h, r.l_meta)
    tables.start()

    lane_w = (iota((width, 128), 1) + 4) & 127
    col_w = iota((width, 128), 0) + RADIUS - (lane_w & 7)
    in_map = (col_w >= 0) & (col_w < width) & ((lane_w & 7) < WINDOW)
    scaled = [
        jnp.where(in_map & (((lane_w >> 5) & 1) == par), 128.0 ** (-0.5), 0.0) for par in range(2)
    ]
    slot_w = (lane_w >> 3) & 3
    pairs_of = (rows + 2 * NEAR + 1) // 2
    quads_of = r.text.shape[1] // (4 * width)
    used_rows = (rows + 2 * NEAR) * width

    def motion_of(e, q):
        tables, starts = [], []
        for m in range(quads_of):
            first, last = max(0, 2 * m - 3), min(pairs_of - 1, 2 * m + 1)
            starts.append(first)
            tables.append(
                nt(
                    r.sext[e, pl.ds(2 * first * width, 2 * (last - first + 1) * width)],
                    r.text[e, pl.ds(4 * m * width, 4 * width)],
                )
            )
        lines = []
        for k in range(pairs_of):
            for par in range(2):
                found = None
                for g in range(4):
                    m, h = divmod(k + g, 2)
                    at = (2 * (k - starts[m]) + par) * width
                    piece = tables[m][at : at + width, h * 128 : (h + 1) * 128]
                    moved = pltpu.roll(
                        piece, width + 8 * g + 32 * par, 1, stride=1, stride_axis=0
                    )
                    found = moved if g == 0 else jnp.where(slot_w == g, moved, found)
                lines.append((found * scaled[par]).astype(BF))
        value = nn(jnp.concatenate(lines, axis=0), r.corr_w[...])
        spread(jnp.maximum(value[0:used_rows], 0.0), r.x3.at[q])

    def update(p):
        for q in range(per):
            txt.received(p * per + q)
            motion_of(p * per + q, q)
        for q in range(per):
            e = p * per + q
            before = r.gpre[e] + nn(windows(r.x3, q, rows + 2), r.wm[...].reshape(9 * 128, 256))
            r.upd[q] = 0.5 * jnp.tanh(0.5 * before[width : width + band, 0:128]) + 0.5
            reset = 0.5 * jnp.tanh(0.5 * before[:, 128:256]) + 0.5
            state = r.hext[r.row_s[0, PLACE + e], pl.ds(width, wide_band)].astype(F32)
            r.rext[q] = (reset * state).astype(BF)
        for q in range(per):
            e = p * per + q
            part = nn(
                jnp.concatenate(
                    [r.rext[q, a * width : a * width + band] for a in range(3)]
                    + [
                        r.x3[q, (a + 1) * width : (a + 1) * width + band, 128:256]
                        for a in range(3)
                    ],
                    axis=1,
                ),
                r.wc[...].reshape(6 * 128, 384),
            )
            candidate = jnp.tanh(
                nudge(part[:, 0:128], 1) + part[:, 128:256] + nudge(part[:, 256:384], -1)
            )
            gate = r.upd[q]
            place = r.row_s[0, PLACE + e]
            state = r.hext[place, pl.ds(NEAR * width, band)]
            fresh = ((1.0 - gate) * state.astype(F32) + gate * candidate).astype(BF)
            used = (place < r.count_s[0]).astype(F32)
            live = jnp.full((band, 128), used) > 0.5
            r.held[e] = jnp.where(live, fresh, state)
            heads = nt(r.head_w[...], fresh)
            jac = heads[0:32]
            weighted = jac * jax.nn.softplus(heads[32:64])
            at16 = pl.ds(pl.multiple_of(e * 16, 16), 16)
            r.jall[at16] = jnp.concatenate([jac[0:16], jac[16:32]], axis=1).astype(BF)
            r.wall[at16] = jnp.concatenate([weighted[0:16], weighted[16:32]], axis=1).astype(BF)

    def stage(p):
        for s in range(1, slots):

            @pl.when(p == s - 1)
            def _():
                take(s)

        update(p)

    each(slots, stage)
    same = (iota((128, 128), 0) >> 4) == (iota((128, 128), 1) >> 4)
    square = jnp.where(same, nt(r.wall[...], r.jall[...]), 0.0)
    blocks = square[0:16]
    for e in range(1, edges):
        blocks = blocks + square[e * 16 : (e + 1) * 16]
    blocks = blocks * (1.0 / (MAPH * width))
    of = iota((16, 128), 1) >> 4
    for e in range(edges):
        used = (r.row_s[0, PLACE + e] < r.count_s[0]).astype(jnp.int32)
        blocks = jnp.where((of == e) & (jnp.full((16, 128), used) == 0), 0.0, blocks)
    r.gpart[...] = blocks

    def tile_copy(rel):
        return remote(
            r.gpart, r.gtile.at[tile], r.s_gt, r.r_gt, me, (tile + rel) % n_tile
        )

    def all_tiles():
        some = r.gtile.at[pl.ds(0, n_tile - 1)]
        return remote(some, some, r.s_gt, r.r_gt, me, (tile + 1) % n_tile)

    for rel in range(1, n_tile):
        tile_copy(rel).start()
    r.gtile[tile] = r.gpart[...]

    def put_back(e):
        r.ready[e] = r.held[r.row_s[0, SPOT + e]]

    each(edges, put_back)
    store = pltpu.make_async_copy(r.ready, r.out_hidden, r.l_out)
    store.start()
    all_tiles().wait_recv()
    total = r.gtile[0]
    for k in range(1, n_tile):
        total = total + r.gtile[k]
    r.gsum[...] = total

    def edge_copy(rel):
        return remote(r.gsum, r.gall.at[me], r.s_ge, r.r_ge, (me + rel) % n_edge, tile)

    def all_edges():
        some = r.gall.at[pl.ds(0, others)]
        return remote(some, some, r.s_ge, r.r_ge, (me + 1) % n_edge, tile)

    for rel in range(1, n_edge):
        edge_copy(rel).start()
    r.gall[me] = total
    all_edges().wait_recv()

    store.wait()
    tables.wait()
    for rel in range(1, n_edge):
        meta_copy(rel).wait_send()
        for k in range(2):
            raw_copy(k, rel).wait_send()
    for s in range(slots):
        feat_group(s).wait_send()
    all_tiles().wait_send()
    all_edges().wait_send()
    for halo in (hid, src, txt):
        halo.sent()


def halves(value):
    high = value.astype(BF)
    return high, (value - high.astype(F32)).astype(BF)


def assemble(dims, where_v, gall, hidden_h, out_hidden, out_cam, out_diag, held, sem):
    n_edge, n_tile, edges, frames, rows, width, slots = dims
    me = lax.axis_index("edge")
    tile = lax.axis_index("tile")
    fetch = pltpu.make_async_copy(hidden_h, held, sem.at[0])
    fetch.start()
    cam_rows, cam_cols = out_cam.shape
    same = (iota((128, 128), 0) >> 4) == (iota((128, 128), 1) >> 4)
    lefts, lows, rights = [], [], []
    for j in range(n_edge):
        left = where_v[j]
        stack = jnp.where(same, jnp.concatenate([gall[j]] * 8, axis=0), 0.0)
        picked = nn(
            jnp.concatenate([left, left], axis=1), jnp.concatenate(halves(stack), axis=0)
        )
        high, low = halves(picked)
        lefts.append(high)
        lows.append(low)
        rights.append(left[cam_rows:])
    placed = nt(jnp.concatenate(lefts + lows, axis=1), jnp.concatenate(rights + rights, axis=1))
    fetch.wait()
    store = pltpu.make_async_copy(held, out_hidden, sem.at[1])
    store.start()
    cam = placed[0:cam_rows]
    row_frame = sixth(iota((cam_rows, cam_cols), 0) + tile * cam_rows)
    col_frame = sixth(iota((cam_rows, cam_cols), 1) + me * cam_cols)
    out_cam[...] = jnp.where(row_frame == col_frame, 0.0, cam)
    own = placed[cam_rows:]
    own_row = sixth(iota((cam_cols, cam_cols), 0))
    own_col = sixth(iota((cam_cols, cam_cols), 1))
    own = jnp.where(own_row == own_col, own, 0.0)
    wide_row = iota((cam_cols, 128), 0)
    wide_lane = iota((cam_cols, 128), 1)
    row_in = wide_row.astype(F32) - 6.0 * sixth(wide_row)
    lane_of = sixth(wide_lane)
    lane_in = wide_lane.astype(F32) - 6.0 * lane_of
    gather = one_hot(row_in == lane_in)
    high, low = halves(own)
    spread = jnp.where(row_in == lane_of, nn(high, gather) + nn(low, gather), 0.0)
    fold = one_hot(
        sixth(iota((frames, cam_cols), 1)) == iota((frames, cam_cols), 0).astype(F32)
    )
    high, low = halves(spread)
    out_diag[...] = (nn(fold, high) + nn(fold, low))[:, 0:36]
    store.wait()


def per_device(
    features,
    hidden_state,
    edge_source,
    edge_owner,
    edge_target,
    edge_counts,
    corr_weight,
    gate_weight,
    candidate_weight,
    jacobian_weight,
    confidence_weight,
):
    n_edge, n_tile = lax.axis_size("edge"), lax.axis_size("tile")
    edges = hidden_state.shape[0]
    frames, rows, width, chan = features.shape
    slots = max(2, (2 * edges + n_edge - 1) // n_edge)
    assert edges % slots == 0 and edges <= 8
    per = edges // slots
    band = rows * width

    dims = (n_edge, n_tile, edges, frames, rows, width, slots)
    even = (rows + 2 * NEAR + 1) // 2 * 2
    dma = pltpu.SemaphoreType.DMA
    vmem = pl.BlockSpec(memory_space=pltpu.VMEM)
    hbm = pl.BlockSpec(memory_space=pl.ANY)

    inputs = (
        ("owner_h", edge_owner[:, 0], hbm),
        ("target_h", edge_target, hbm),
        ("source_h", edge_source, hbm),
        ("count_h", edge_counts, hbm),
        ("feat_h", features.reshape(frames, band, chan), hbm),
        ("hidden_h", hidden_state.reshape(edges, band, chan), hbm),
        ("corr_h", corr_weight, hbm),
        ("gate_w", gate_weight, hbm),
        ("cand_w", candidate_weight, hbm),
        ("jac_h", jacobian_weight.T, hbm),
        ("conf_h", confidence_weight.T, hbm),
    )
    cam_rows, cam_cols = frames * n_edge * 6 // n_tile, frames * 6
    places = (n_edge, cam_rows + cam_cols, 128)
    outputs = (
        ("out_hidden", (edges, band, chan), BF, hbm),
        ("gall", (n_edge, 16, 128), F32, vmem),
        ("where_h", places, BF, hbm),
    )
    near, far = len(reach(NEAR, rows)), len(reach(FAR, rows))
    scratch = {
        "owner_s": pltpu.SMEM((edges,), jnp.int32),
        "target_s": pltpu.SMEM((edges,), jnp.int32),
        "source_s": pltpu.SMEM((edges,), jnp.int32),
        "count_s": pltpu.SMEM((1,), jnp.int32),
        "corr_in": pltpu.VMEM(corr_weight.shape, BF),
        "jac_in": pltpu.VMEM(jacobian_weight.shape[::-1], BF),
        "conf_in": pltpu.VMEM(confidence_weight.shape[::-1], BF),
        "row_v": pltpu.VMEM((1, 128), jnp.int32),
        "row_s": pltpu.SMEM((1, 128), jnp.int32),
        "meta_s": pltpu.SMEM((n_edge, 1, 128), jnp.int32),
        "feat": pltpu.VMEM((frames, band, chan), BF),
        "held": pltpu.VMEM((edges, band, chan), BF),
        "ready": pltpu.VMEM((edges, band, chan), BF),
        "where_v": pltpu.VMEM(places, BF),
        "raw_s": pltpu.SMEM((2, n_edge, edges), jnp.int32),
        "s_raw": pltpu.SemaphoreType.DMA((2, n_edge - 1)),
        "r_raw": pltpu.SemaphoreType.DMA((2, n_edge - 1)),
        "send": pltpu.VMEM(((n_edge - 1) * slots, band, chan), BF),
        "text": pltpu.VMEM((edges, (even + 2 * RADIUS + 3) // 4 * 4 * width, chan), BF),
        "sext": pltpu.VMEM((edges, even * width, chan), BF),
        "hext": pltpu.VMEM((edges, (rows + 2 * NEAR) * width, chan), BF),
        "rext": pltpu.VMEM((per, (rows + 2) * width, chan), BF),
        "x3": pltpu.VMEM((per, (rows + 2 * NEAR) * width, 3 * chan), BF),
        "wh": pltpu.VMEM((3, 3, chan, 2 * chan), BF),
        "wm": pltpu.VMEM((3, 3, chan, 2 * chan), BF),
        "wc": pltpu.VMEM((2, 3, chan, 3 * chan), BF),
        "corr_w": pltpu.VMEM((128, chan), BF),
        "head_w": pltpu.VMEM((64, chan), BF),
        "gpre": pltpu.VMEM((edges, (rows + 2) * width, 2 * chan), F32),
        "upd": pltpu.VMEM((per, band, chan), F32),
        "jall": pltpu.VMEM((128, 2 * band), BF),
        "wall": pltpu.VMEM((128, 2 * band), BF),
        "gpart": pltpu.VMEM((16, 128), F32),
        "gtile": pltpu.VMEM((n_tile, 16, 128), F32),
        "gsum": pltpu.VMEM((16, 128), F32),
        "l_in": dma((5,)),
        "l_w": dma((3,)),
        "l_ints": dma((4,)),
        "l_row": dma,
        "l_meta": dma,
        "l_own": dma,
        "l_out": dma,
        "s_meta": dma((n_edge - 1,)),
        "r_meta": dma((n_edge - 1,)),
        "s_feat": dma,
        "r_feat": dma((slots,)),
        "s_gt": dma,
        "r_gt": dma,
        "s_ge": dma,
        "r_ge": dma,
    }
    for s in range(slots):
        scratch[f"text{s}"] = pltpu.VMEM((n_edge - 1, band, chan), BF)
    for key, count, lots in (("h", near, 1), ("s", near, 1), ("t", far, edges)):
        for way in ("up", "dn"):
            scratch[f"s_{key}{way}"] = dma((count,))
            scratch[f"r_{key}{way}"] = dma((count, lots))
    names = [i[0] for i in inputs] + [o[0] for o in outputs] + list(scratch)
    state, gall, where = pl.pallas_call(
        functools.partial(kernel, dims, names),
        out_shape=tuple(jax.ShapeDtypeStruct(shape, kind) for _, shape, kind, _ in outputs),
        in_specs=[spec for _, _, spec in inputs],
        out_specs=tuple(spec for _, _, _, spec in outputs),
        scratch_shapes=list(scratch.values()),
        compiler_params=pltpu.CompilerParams(
            collective_id=0, has_side_effects=True, vmem_limit_bytes=56 * 1024 * 1024
        ),
    )(*[value for _, value, _ in inputs])
    hidden_next, cam, diag = pl.pallas_call(
        functools.partial(assemble, dims),
        out_shape=(
            jax.ShapeDtypeStruct((edges, band, chan), BF),
            jax.ShapeDtypeStruct((cam_rows, cam_cols), F32),
            jax.ShapeDtypeStruct((frames, 36), F32),
        ),
        in_specs=[vmem, vmem, hbm],
        out_specs=(hbm, vmem, vmem),
        scratch_shapes=[pltpu.VMEM((edges, band, chan), BF), dma((2,))],
    )(where, gall, state)
    return hidden_next.reshape(hidden_state.shape), cam, diag


def solution(mesh):
    placed = (
        P("edge", "tile", None, None),
        P("edge", "tile", None, None),
        P("edge"),
        P("edge", None),
        P("edge"),
        P("edge"),
        P(),
        P(),
        P(),
        P(),
        P(),
    )
    return jax.shard_map(
        per_device,
        mesh=mesh,
        in_specs=placed,
        out_specs=(P("edge", "tile", None, None), P("tile", "edge"), P("edge", None)),
        check_vma=False,
    )
```

```python
import functools
import types

import jax
import jax.numpy as jnp
from jax import lax
from jax.experimental import pallas as pl
from jax.experimental.pallas import tpu as pltpu
from jax.sharding import PartitionSpec as P

MAPH = 48
WINDOW = 7
RADIUS = WINDOW // 2
NEAR = 2
FAR = RADIUS + NEAR
OWNER, TARGET, SOURCE, SPOT, PLACE, GROUP, REL, ASKS = 0, 8, 16, 24, 32, 40, 48, 64
PIECES = 4
MESH = pl.DeviceIdType.MESH
BF = jnp.bfloat16
F32 = jnp.float32


def nt(a, b):
    return lax.dot_general(a, b, (((1,), (1,)), ((), ())), preferred_element_type=F32)


def nn(a, b):
    return lax.dot_general(a, b, (((1,), (0,)), ((), ())), preferred_element_type=F32)


def iota(shape, dim):
    return lax.broadcasted_iota(jnp.int32, shape, dim)


def sixth(index):
    return jnp.floor((index.astype(F32) + 0.5) * (1.0 / 6.0))


def one_hot(cond):
    return cond.astype(F32).astype(BF)


def each(count, body):
    def step(i, carry):
        body(i)
        return carry

    lax.fori_loop(0, count, step, 0)


def reach(halo, rows):
    return [min(rows, halo - d * rows) for d in range((halo + rows - 1) // rows)]


def kernel(dims, names, *refs):
    n_edge, n_tile, edges, frames, rows, width, slots = dims
    r = types.SimpleNamespace(**dict(zip(names, refs)))
    band = rows * width
    per = edges // slots
    me = lax.axis_index("edge")
    tile = lax.axis_index("tile")
    texts = [getattr(r, f"text{s}") for s in range(slots)]

    ints = [
        pltpu.make_async_copy(r.owner_h, r.owner_s, r.l_ints.at[0]),
        pltpu.make_async_copy(r.target_h, r.target_s, r.l_ints.at[1]),
        pltpu.make_async_copy(r.source_h, r.source_s, r.l_ints.at[2]),
        pltpu.make_async_copy(r.count_h, r.count_s, r.l_ints.at[3]),
    ]
    loads = [
        pltpu.make_async_copy(r.feat_h, r.feat, r.l_in.at[0]),
        pltpu.make_async_copy(
            r.hidden_h, r.hext.at[:, pl.ds(NEAR * width, band)], r.l_in.at[1]
        ),
        pltpu.make_async_copy(r.corr_h, r.corr_in, r.l_in.at[2]),
        pltpu.make_async_copy(r.jac_h, r.jac_in, r.l_in.at[3]),
        pltpu.make_async_copy(r.conf_h, r.conf_in, r.l_in.at[4]),
    ]
    first, second = pl.ds(0, 128), pl.ds(128, 128)
    fills = [
        pltpu.make_async_copy(r.gate_w.at[:, :, first], r.wh, r.l_w.at[0]),
        pltpu.make_async_copy(r.gate_w.at[:, :, second], r.wm, r.l_w.at[1]),
    ]
    for part, at in enumerate((first, second)):
        for b in range(3):
            fills.append(
                pltpu.make_async_copy(
                    r.cand_w.at[:, b, at], r.wc.at[part, :, :, pl.ds(b * 128, 128)], r.l_w.at[2]
                )
            )
    filled = fills[:2] + [pltpu.make_async_copy(r.wc, r.wc, r.l_w.at[2])]
    for load in ints + loads + fills:
        load.start()

    barrier = pltpu.get_barrier_semaphore()
    for rel in range(1, n_edge):
        pl.semaphore_signal(
            barrier, inc=1, device_id=((me + rel) % n_edge, tile), device_id_type=MESH
        )
    for rel in range(1, n_tile):
        pl.semaphore_signal(
            barrier, inc=1, device_id=(me, (tile + rel) % n_tile), device_id_type=MESH
        )

    for load in ints:
        load.wait()
    owner = [r.owner_s[e] for e in range(edges)]
    rel_of = [(owner[e] - me + n_edge) % n_edge for e in range(edges)]
    rank, group = [], []
    for e in range(edges):
        before = jnp.int32(0)
        for k in range(e):
            before = before + (owner[k] == owner[e]).astype(jnp.int32)
        rank.append(jnp.minimum(before, slots - 1))
        group.append(jnp.where(rel_of[e] == 0, 0, rank[e] + 1))
    lane = iota((1, 128), 1)
    row = jnp.zeros((1, 128), jnp.int32)
    for e in range(edges):
        spot = jnp.int32(0)
        for k in range(edges):
            if k < e:
                spot = spot + (group[k] <= group[e]).astype(jnp.int32)
            elif k > e:
                spot = spot + (group[k] < group[e]).astype(jnp.int32)
        goal = r.target_s[e]
        fields = (
            (OWNER, owner[e]),
            (TARGET, goal),
            (SOURCE, r.source_s[e]),
            (PLACE, jnp.int32(e)),
            (GROUP, group[e]),
            (REL, rel_of[e]),
        )
        for base, value in fields:
            row = jnp.where(lane == base + spot, value, row)
        row = jnp.where(lane == SPOT + e, spot, row)
        row = jnp.where(lane == ASKS + rel_of[e] * slots + rank[e], goal, row)
    r.row_v[...] = row
    mine = pltpu.make_async_copy(r.row_v, r.row_s, r.l_row)
    mine.start()

    pl.semaphore_wait(barrier, n_edge + n_tile - 2)

    def remote(src, dst, send_sem, recv_sem, edge_id, tile_id):
        return pltpu.make_async_remote_copy(
            src_ref=src,
            dst_ref=dst,
            send_sem=send_sem,
            recv_sem=recv_sem,
            device_id=(edge_id, tile_id),
            device_id_type=MESH,
        )

    def meta_copy(rel):
        return remote(
            r.row_v, r.meta_s.at[me], r.s_meta.at[rel - 1], r.r_meta.at[rel - 1],
            (me + rel) % n_edge, tile,
        )

    others = n_edge - 1
    for rel in range(1, n_edge):
        meta_copy(rel).start()
    own_row = pltpu.make_async_copy(r.row_v, r.meta_s.at[me], r.l_own)
    own_row.start()

    class Halo:
        def __init__(self, halo, lot, buf, source, sems):
            self.halo, self.lot, self.buf, self.source, self.sems = halo, lot, buf, source, sems
            self.counts = reach(halo, rows)

        def copies(self, i, lot):
            which = pl.ds(i * lot, lot)
            for d, count in enumerate(self.counts):
                far, lines = d + 1, count * width
                s_up, r_up, s_dn, r_dn = self.sems
                up = remote(
                    self.source(which, 0, lines),
                    self.buf.at[which, pl.ds((self.halo + far * rows) * width, lines)],
                    s_up.at[d], r_up.at[d, i], me, tile - far,
                )
                dn = remote(
                    self.source(which, band - lines, lines),
                    self.buf.at[which, pl.ds((self.halo - d * rows - count) * width, lines)],
                    s_dn.at[d], r_dn.at[d, i], me, tile + far,
                )
                yield tile >= far, tile + far < n_tile, up, dn

        def start(self, i):
            for above, below, up, dn in self.copies(i, self.lot):
                pl.when(above)(up.start)
                pl.when(below)(dn.start)

        def received(self, i):
            for above, below, up, dn in self.copies(i, self.lot):
                pl.when(below)(up.wait_recv)
                pl.when(above)(dn.wait_recv)

        def sent(self):
            for above, below, up, dn in self.copies(0, edges):
                pl.when(above)(up.wait_send)
                pl.when(below)(dn.wait_send)

        def clear(self):
            for d, count in enumerate(self.counts):
                far, lines = d + 1, count * width
                zero = jnp.zeros((lines, 128), BF)
                top = (self.halo - d * rows - count) * width
                low = (self.halo + far * rows) * width

                @pl.when(tile < far)
                def _():
                    def clear_top(e):
                        self.buf[e, pl.ds(top, lines)] = zero

                    each(edges, clear_top)

                @pl.when(tile + far >= n_tile)
                def _():
                    def clear_low(e):
                        self.buf[e, pl.ds(low, lines)] = zero

                    each(edges, clear_low)

            used = (rows + 2 * self.halo) * width
            spare = self.buf.shape[1] - used
            if spare:

                def clear_pad(e):
                    self.buf[e, pl.ds(used, spare)] = jnp.zeros((spare, 128), BF)

                each(edges, clear_pad)

    def inner(buf, halo):
        return lambda which, at, lines: buf.at[which, pl.ds(halo * width + at, lines)]

    hid = Halo(
        NEAR, edges, r.hext, lambda which, at, lines: r.hidden_h.at[which, pl.ds(at, lines)],
        (r.s_hup, r.r_hup, r.s_hdn, r.r_hdn),
    )
    src = Halo(
        NEAR, edges, r.sext, inner(r.sext, NEAR), (r.s_sup, r.r_sup, r.s_sdn, r.r_sdn)
    )
    txt = Halo(FAR, 1, r.text, inner(r.text, FAR), (r.s_tup, r.r_tup, r.s_tdn, r.r_tdn))

    hid.start(0)
    for rel in range(1, n_edge):
        remote(
            r.row_v, r.meta_s.at[(me - rel + n_edge) % n_edge], r.s_meta.at[rel - 1],
            r.r_meta.at[rel - 1], (me + rel) % n_edge, tile,
        ).wait_recv()
    loads[0].wait()

    def feat_copy(rel, s):
        return remote(
            r.send.at[s * others + rel - 1], texts[s].at[rel - 1],
            r.s_feat, r.r_feat.at[s], (me - rel + n_edge) % n_edge, tile,
        )

    def feat_group(s):
        return remote(
            r.send.at[pl.ds(s * others, others)], texts[s],
            r.s_feat, r.r_feat.at[s], (me + 1) % n_edge, tile,
        )

    for s in range(slots):
        for rel in range(1, n_edge):
            peer = (me - rel + n_edge) % n_edge
            r.send[s * others + rel - 1] = r.feat[r.meta_s[peer, 0, ASKS + rel * slots + s]]
        for rel in range(1, n_edge):
            feat_copy(rel, s).start()

    mine.wait()

    def take_source(e):
        r.sext[e, pl.ds(NEAR * width, band)] = r.feat[r.row_s[0, SOURCE + e]]

    each(edges, take_source)
    src.start(0)
    for halo in (hid, src, txt):
        halo.clear()

    for load in loads[2:]:
        load.wait()

    spot = (iota((128, 64), 0) + 4) & 127
    along = ((spot >> 3) & 3) * 2 + (spot >> 6) - ((spot >> 5) & 1)
    across = WINDOW - 1 - (spot & 7)
    fits = (across >= 0) & (along >= 0) & (along < WINDOW)
    pick = (iota((128, 64), 1) == along * WINDOW + across) & fits
    lookup = jnp.concatenate(
        [r.corr_in[...].astype(F32), jnp.zeros((64 - WINDOW * WINDOW, 128), F32)], axis=0
    ).astype(BF)
    r.corr_w[...] = nn(one_hot(pick), lookup).astype(BF)

    place12 = iota((32, 64), 0)
    which = place12 >> 4
    within = place12 & 15
    name12 = iota((32, 64), 1)
    pick_j = (within < 12) & (name12 == which * 12 + within)
    padded_jac = jnp.concatenate(
        [r.jac_in[...].astype(F32), jnp.zeros((40, 128), F32)], axis=0
    ).astype(BF)
    conf_wide = r.conf_in[...].astype(F32)
    tall = iota((32, 128), 0)
    conf_rows = jnp.where(
        tall < 16,
        jnp.broadcast_to(conf_wide[0:1], (32, 128)),
        jnp.broadcast_to(conf_wide[1:2], (32, 128)),
    )
    r.head_w[...] = jnp.concatenate(
        [nn(one_hot(pick_j), padded_jac), jnp.where((tall & 15) < 12, conf_rows, 0.0)], axis=0
    ).astype(BF)

    def nudge(wide, by):
        lines = wide.shape[0]
        column = iota((lines, 128), 0) & (width - 1)
        edge = 0 if by == 1 else width - 1
        return jnp.where(column == edge, 0.0, pltpu.roll(wide, by % lines, 0))

    def spread(value, out):
        lines = value.shape[0]
        wide = value.astype(F32)
        out[0:lines, 0:128] = nudge(wide, 1).astype(BF)
        out[0:lines, 128:256] = value.astype(BF)
        out[0:lines, 256:384] = nudge(wide, -1).astype(BF)

    def windows(x3, q, out_rows):
        size = out_rows * width
        return jnp.concatenate([x3[q, a * width : a * width + size] for a in range(3)], axis=1)

    wide_band = (rows + 2) * width

    def state_part(p):
        for q in range(per):
            e = p * per + q
            spread(r.hext[r.row_s[0, PLACE + e]], r.x3.at[q])
            r.gpre[e] = nn(windows(r.x3, q, rows + 2), r.wh[...].reshape(9 * 128, 256))

    loads[1].wait()
    for fill in filled:
        fill.wait()
    flip_row, flip_col = iota((2 * width, 2 * width), 0), iota((2 * width, 2 * width), 1)
    flip = one_hot(
        (flip_row // width == flip_col // width)
        & ((flip_row & (width - 1)) + (flip_col & (width - 1)) == width - 1)
    )

    def take_target(e, upto):
        value = r.feat[r.row_s[0, TARGET + e]]
        at = jnp.maximum(r.row_s[0, REL + e] - 1, 0)
        for s in range(upto + 1):
            value = jnp.where(r.row_s[0, GROUP + e] == s + 1, texts[s][at], value)
        for first in range(0, band, 2 * width):
            count = min(2 * width, band - first)
            r.text[e, pl.ds(FAR * width + first, count)] = nn(
                flip[0:count, 0:count], value[first : first + count]
            ).astype(BF)
        txt.start(e)

    def take(s):
        feat_group(s).wait_recv()
        for q in range(per):
            take_target(s * per + q, s)

    hid.received(0)
    each(slots // 2, state_part)
    take(0)
    each(slots - slots // 2, lambda p: state_part(p + slots // 2))
    src.received(0)

    own_row.wait()
    cam_cols = frames * 6
    cam_rows = r.where_v.shape[1] - cam_cols
    part = iota((cam_rows + cam_cols, 128), 0)
    index = jnp.where(part < cam_rows, part + tile * cam_rows, part - cam_rows + me * cam_cols)
    inside = lane & 15
    digit = jnp.where(inside < 6, inside, inside - 6)

    def place(j):
        spots = jnp.full((1, 128), -1, jnp.int32)
        for e in range(edges):
            source = (j * frames + r.meta_s[j, 0, SOURCE + e]) * 6
            target = (r.meta_s[j, 0, OWNER + e] * frames + r.meta_s[j, 0, TARGET + e]) * 6
            here = jnp.where(inside < 6, source, target) + digit
            spots = jnp.where(((lane >> 4) == e) & (inside < 12), here, spots)
        r.where_v[j] = one_hot(index == spots)

    each(n_edge, place)
    tables = pltpu.make_async_copy(r.where_v, r.where_h, r.l_meta)
    tables.start()

    lane_w = (iota((width, 128), 1) + 4) & 127
    col_w = iota((width, 128), 0) + RADIUS - (lane_w & 7)
    in_map = (col_w >= 0) & (col_w < width) & ((lane_w & 7) < WINDOW)
    scaled = [
        jnp.where(in_map & (((lane_w >> 5) & 1) == par), 128.0 ** (-0.5), 0.0) for par in range(2)
    ]
    slot_w = (lane_w >> 3) & 3
    pairs_of = (rows + 2 * NEAR + 1) // 2
    quads_of = r.text.shape[1] // (4 * width)
    used_rows = (rows + 2 * NEAR) * width

    def motion_of(e, q):
        tables, starts = [], []
        for m in range(quads_of):
            first, last = max(0, 2 * m - 3), min(pairs_of - 1, 2 * m + 1)
            starts.append(first)
            tables.append(
                nt(
                    r.sext[e, pl.ds(2 * first * width, 2 * (last - first + 1) * width)],
                    r.text[e, pl.ds(4 * m * width, 4 * width)],
                )
            )
        lines = []
        for k in range(pairs_of):
            for par in range(2):
                found = None
                for g in range(4):
                    m, h = divmod(k + g, 2)
                    at = (2 * (k - starts[m]) + par) * width
                    piece = tables[m][at : at + width, h * 128 : (h + 1) * 128]
                    moved = pltpu.roll(
                        piece, width + 8 * g + 32 * par, 1, stride=1, stride_axis=0
                    )
                    found = moved if g == 0 else jnp.where(slot_w == g, moved, found)
                lines.append((found * scaled[par]).astype(BF))
        value = nn(jnp.concatenate(lines, axis=0), r.corr_w[...])
        spread(jnp.maximum(value[0:used_rows], 0.0), r.x3.at[q])

    def update(p):
        for q in range(per):
            txt.received(p * per + q)
            motion_of(p * per + q, q)
        for q in range(per):
            e = p * per + q
            before = r.gpre[e] + nn(windows(r.x3, q, rows + 2), r.wm[...].reshape(9 * 128, 256))
            r.upd[q] = 0.5 * jnp.tanh(0.5 * before[width : width + band, 0:128]) + 0.5
            reset = 0.5 * jnp.tanh(0.5 * before[:, 128:256]) + 0.5
            state = r.hext[r.row_s[0, PLACE + e], pl.ds(width, wide_band)].astype(F32)
            r.rext[q] = (reset * state).astype(BF)
        for q in range(per):
            e = p * per + q
            part = nn(
                jnp.concatenate(
                    [r.rext[q, a * width : a * width + band] for a in range(3)]
                    + [
                        r.x3[q, (a + 1) * width : (a + 1) * width + band, 128:256]
                        for a in range(3)
                    ],
                    axis=1,
                ),
                r.wc[...].reshape(6 * 128, 384),
            )
            candidate = jnp.tanh(
                nudge(part[:, 0:128], 1) + part[:, 128:256] + nudge(part[:, 256:384], -1)
            )
            gate = r.upd[q]
            place = r.row_s[0, PLACE + e]
            state = r.hext[place, pl.ds(NEAR * width, band)]
            fresh = ((1.0 - gate) * state.astype(F32) + gate * candidate).astype(BF)
            used = (place < r.count_s[0]).astype(F32)
            live = jnp.full((band, 128), used) > 0.5
            r.held[e] = jnp.where(live, fresh, state)
            heads = nt(r.head_w[...], fresh)
            jac = heads[0:32]
            weighted = jac * jax.nn.softplus(heads[32:64])
            at16 = pl.ds(pl.multiple_of(e * 16, 16), 16)
            r.jall[at16] = jnp.concatenate([jac[0:16], jac[16:32]], axis=1).astype(BF)
            r.wall[at16] = jnp.concatenate([weighted[0:16], weighted[16:32]], axis=1).astype(BF)

    def stage(p):
        for s in range(1, slots):

            @pl.when(p == s - 1)
            def _():
                take(s)

        update(p)

    each(slots, stage)
    same = (iota((128, 128), 0) >> 4) == (iota((128, 128), 1) >> 4)
    square = jnp.where(same, nt(r.wall[...], r.jall[...]), 0.0)
    blocks = square[0:16]
    for e in range(1, edges):
        blocks = blocks + square[e * 16 : (e + 1) * 16]
    blocks = blocks * (1.0 / (MAPH * width))
    of = iota((16, 128), 1) >> 4
    for e in range(edges):
        used = (r.row_s[0, PLACE + e] < r.count_s[0]).astype(jnp.int32)
        blocks = jnp.where((of == e) & (jnp.full((16, 128), used) == 0), 0.0, blocks)
    r.gpart[...] = blocks

    def tile_copy(rel):
        return remote(
            r.gpart, r.gtile.at[tile], r.s_gt, r.r_gt, me, (tile + rel) % n_tile
        )

    def all_tiles():
        some = r.gtile.at[pl.ds(0, n_tile - 1)]
        return remote(some, some, r.s_gt, r.r_gt, me, (tile + 1) % n_tile)

    for rel in range(1, n_tile):
        tile_copy(rel).start()
    r.gtile[tile] = r.gpart[...]

    def put_back(e):
        r.ready[e] = r.held[r.row_s[0, SPOT + e]]

    each(edges, put_back)
    store = pltpu.make_async_copy(r.ready, r.out_hidden, r.l_out)
    store.start()
    all_tiles().wait_recv()
    total = r.gtile[0]
    for k in range(1, n_tile):
        total = total + r.gtile[k]
    r.gsum[...] = total

    def edge_copy(rel):
        return remote(r.gsum, r.gall_h.at[me], r.s_ge, r.r_ge, (me + rel) % n_edge, tile)

    def all_edges():
        some = r.gall_h.at[pl.ds(0, others)]
        return remote(some, some, r.s_ge, r.r_ge, (me + 1) % n_edge, tile)

    for rel in range(1, n_edge):
        edge_copy(rel).start()
    own_sum = pltpu.make_async_copy(r.gsum, r.gall_h.at[me], r.l_sum)
    own_sum.start()
    all_edges().wait_recv()

    own_sum.wait()
    store.wait()
    tables.wait()
    for rel in range(1, n_edge):
        meta_copy(rel).wait_send()
    for s in range(slots):
        feat_group(s).wait_send()
    all_tiles().wait_send()
    all_edges().wait_send()
    for halo in (hid, src, txt):
        halo.sent()


def halves(value):
    high = value.astype(BF)
    return high, (value - high.astype(F32)).astype(BF)


def assemble(
    dims, where_h, gall_h, hidden_h, out_hidden, cam_h, diag_h, where_v, gall, out_cam, out_diag, held,
    sem, held_sem,
):
    n_edge, n_tile, edges, frames, rows, width, slots = dims
    me = lax.axis_index("edge")
    tile = lax.axis_index("tile")
    loads = [
        pltpu.make_async_copy(gall_h, gall, sem.at[0]),
        pltpu.make_async_copy(where_h, where_v, sem.at[1]),
    ]
    pieces = [pl.ds(i * (edges // PIECES), edges // PIECES) for i in range(PIECES)]
    fetches = [
        pltpu.make_async_copy(hidden_h.at[p], held.at[p], held_sem.at[i])
        for i, p in enumerate(pieces)
    ]
    stores = [
        pltpu.make_async_copy(held.at[p], out_hidden.at[p], held_sem.at[i])
        for i, p in enumerate(pieces)
    ]
    for load in loads + fetches:
        load.start()
    cam_rows, cam_cols = out_cam.shape
    same = (iota((128, 128), 0) >> 4) == (iota((128, 128), 1) >> 4)
    for load in loads:
        load.wait()
    for fetch, store in zip(fetches, stores):
        fetch.wait()
        store.start()
    lefts, lows, rights = [], [], []
    for j in range(n_edge):
        left = where_v[j]
        stack = jnp.where(same, jnp.concatenate([gall[j]] * 8, axis=0), 0.0)
        picked = nn(
            jnp.concatenate([left, left], axis=1), jnp.concatenate(halves(stack), axis=0)
        )
        high, low = halves(picked)
        lefts.append(high)
        lows.append(low)
        rights.append(left[cam_rows:])
    placed = nt(jnp.concatenate(lefts + lows, axis=1), jnp.concatenate(rights + rights, axis=1))
    cam = placed[0:cam_rows]
    row_frame = sixth(iota((cam_rows, cam_cols), 0) + tile * cam_rows)
    col_frame = sixth(iota((cam_rows, cam_cols), 1) + me * cam_cols)
    out_cam[...] = jnp.where(row_frame == col_frame, 0.0, cam)
    cam_store = pltpu.make_async_copy(out_cam, cam_h, sem.at[0])
    cam_store.start()
    own = placed[cam_rows:]
    own_row = sixth(iota((cam_cols, cam_cols), 0))
    own_col = sixth(iota((cam_cols, cam_cols), 1))
    own = jnp.where(own_row == own_col, own, 0.0)
    wide_row = iota((cam_cols, 128), 0)
    wide_lane = iota((cam_cols, 128), 1)
    row_in = wide_row.astype(F32) - 6.0 * sixth(wide_row)
    lane_of = sixth(wide_lane)
    lane_in = wide_lane.astype(F32) - 6.0 * lane_of
    gather = one_hot(row_in == lane_in)
    high, low = halves(own)
    spread = jnp.where(row_in == lane_of, nn(high, gather) + nn(low, gather), 0.0)
    fold = one_hot(
        sixth(iota((frames, cam_cols), 1)) == iota((frames, cam_cols), 0).astype(F32)
    )
    high, low = halves(spread)
    out_diag[...] = (nn(fold, high) + nn(fold, low))[:, 0:36]
    diag_store = pltpu.make_async_copy(out_diag, diag_h, sem.at[1])
    diag_store.start()
    for store in stores + [cam_store, diag_store]:
        store.wait()


def per_device(
    features,
    hidden_state,
    edge_source,
    edge_owner,
    edge_target,
    edge_counts,
    corr_weight,
    gate_weight,
    candidate_weight,
    jacobian_weight,
    confidence_weight,
):
    n_edge, n_tile = lax.axis_size("edge"), lax.axis_size("tile")
    edges = hidden_state.shape[0]
    frames, rows, width, chan = features.shape
    slots = max(2, (2 * edges + n_edge - 1) // n_edge)
    assert edges % slots == 0 and edges <= 8 and ASKS + n_edge * slots <= 128
    per = edges // slots
    band = rows * width

    dims = (n_edge, n_tile, edges, frames, rows, width, slots)
    even = (rows + 2 * NEAR + 1) // 2 * 2
    dma = pltpu.SemaphoreType.DMA
    hbm = pl.BlockSpec(memory_space=pl.ANY)

    inputs = (
        ("owner_h", edge_owner[:, 0], hbm),
        ("target_h", edge_target, hbm),
        ("source_h", edge_source, hbm),
        ("count_h", edge_counts, hbm),
        ("feat_h", features.reshape(frames, band, chan), hbm),
        ("hidden_h", hidden_state.reshape(edges, band, chan), hbm),
        ("corr_h", corr_weight, hbm),
        ("gate_w", gate_weight, hbm),
        ("cand_w", candidate_weight, hbm),
        ("jac_h", jacobian_weight.T, hbm),
        ("conf_h", confidence_weight.T, hbm),
    )
    cam_rows, cam_cols = frames * n_edge * 6 // n_tile, frames * 6
    places = (n_edge, cam_rows + cam_cols, 128)
    outputs = (
        ("out_hidden", (edges, band, chan), BF, hbm),
        ("gall_h", (n_edge, 16, 128), F32, hbm),
        ("where_h", places, BF, hbm),
    )
    near, far = len(reach(NEAR, rows)), len(reach(FAR, rows))
    scratch = {
        "owner_s": pltpu.SMEM((edges,), jnp.int32),
        "target_s": pltpu.SMEM((edges,), jnp.int32),
        "source_s": pltpu.SMEM((edges,), jnp.int32),
        "count_s": pltpu.SMEM((1,), jnp.int32),
        "corr_in": pltpu.VMEM(corr_weight.shape, BF),
        "jac_in": pltpu.VMEM(jacobian_weight.shape[::-1], BF),
        "conf_in": pltpu.VMEM(confidence_weight.shape[::-1], BF),
        "row_v": pltpu.VMEM((1, 128), jnp.int32),
        "row_s": pltpu.SMEM((1, 128), jnp.int32),
        "meta_s": pltpu.SMEM((n_edge, 1, 128), jnp.int32),
        "feat": pltpu.VMEM((frames, band, chan), BF),
        "held": pltpu.VMEM((edges, band, chan), BF),
        "ready": pltpu.VMEM((edges, band, chan), BF),
        "where_v": pltpu.VMEM(places, BF),
        "send": pltpu.VMEM(((n_edge - 1) * slots, band, chan), BF),
        "text": pltpu.VMEM((edges, (even + 2 * RADIUS + 3) // 4 * 4 * width, chan), BF),
        "sext": pltpu.VMEM((edges, even * width, chan), BF),
        "hext": pltpu.VMEM((edges, (rows + 2 * NEAR) * width, chan), BF),
        "rext": pltpu.VMEM((per, (rows + 2) * width, chan), BF),
        "x3": pltpu.VMEM((per, (rows + 2 * NEAR) * width, 3 * chan), BF),
        "wh": pltpu.VMEM((3, 3, chan, 2 * chan), BF),
        "wm": pltpu.VMEM((3, 3, chan, 2 * chan), BF),
        "wc": pltpu.VMEM((2, 3, chan, 3 * chan), BF),
        "corr_w": pltpu.VMEM((128, chan), BF),
        "head_w": pltpu.VMEM((64, chan), BF),
        "gpre": pltpu.VMEM((edges, (rows + 2) * width, 2 * chan), F32),
        "upd": pltpu.VMEM((per, band, chan), F32),
        "jall": pltpu.VMEM((128, 2 * band), BF),
        "wall": pltpu.VMEM((128, 2 * band), BF),
        "gpart": pltpu.VMEM((16, 128), F32),
        "gtile": pltpu.VMEM((n_tile, 16, 128), F32),
        "gsum": pltpu.VMEM((16, 128), F32),
        "l_in": dma((5,)),
        "l_w": dma((3,)),
        "l_ints": dma((4,)),
        "l_row": dma,
        "l_meta": dma,
        "l_own": dma,
        "l_sum": dma,
        "l_out": dma,
        "s_meta": dma((n_edge - 1,)),
        "r_meta": dma((n_edge - 1,)),
        "s_feat": dma,
        "r_feat": dma((slots,)),
        "s_gt": dma,
        "r_gt": dma,
        "s_ge": dma,
        "r_ge": dma,
    }
    for s in range(slots):
        scratch[f"text{s}"] = pltpu.VMEM((n_edge - 1, band, chan), BF)
    for key, count, lots in (("h", near, 1), ("s", near, 1), ("t", far, edges)):
        for way in ("up", "dn"):
            scratch[f"s_{key}{way}"] = dma((count,))
            scratch[f"r_{key}{way}"] = dma((count, lots))
    names = [i[0] for i in inputs] + [o[0] for o in outputs] + list(scratch)
    state, gall, where = pl.pallas_call(
        functools.partial(kernel, dims, names),
        out_shape=tuple(jax.ShapeDtypeStruct(shape, kind) for _, shape, kind, _ in outputs),
        in_specs=[spec for _, _, spec in inputs],
        out_specs=tuple(spec for _, _, _, spec in outputs),
        scratch_shapes=list(scratch.values()),
        compiler_params=pltpu.CompilerParams(
            collective_id=0, has_side_effects=True, vmem_limit_bytes=56 * 1024 * 1024
        ),
    )(*[value for _, value, _ in inputs])
    hidden_next, cam, diag = pl.pallas_call(
        functools.partial(assemble, dims),
        out_shape=(
            jax.ShapeDtypeStruct((edges, band, chan), BF),
            jax.ShapeDtypeStruct((cam_rows, cam_cols), F32),
            jax.ShapeDtypeStruct((frames, 36), F32),
        ),
        in_specs=[hbm] * 3,
        out_specs=(hbm,) * 3,
        scratch_shapes=[
            pltpu.VMEM(places, BF),
            pltpu.VMEM((n_edge, 16, 128), F32),
            pltpu.VMEM((cam_rows, cam_cols), F32),
            pltpu.VMEM((frames, 36), F32),
            pltpu.VMEM((edges, band, chan), BF),
            dma((2,)),
            dma((PIECES,)),
        ],
    )(where, gall, state)
    return hidden_next.reshape(hidden_state.shape), cam, diag


def solution(mesh):
    placed = (
        P("edge", "tile", None, None),
        P("edge", "tile", None, None),
        P("edge"),
        P("edge", None),
        P("edge"),
        P("edge"),
        P(),
        P(),
        P(),
        P(),
        P(),
    )
    return jax.shard_map(
        per_device,
        mesh=mesh,
        in_specs=placed,
        out_specs=(P("edge", "tile", None, None), P("tile", "edge"), P("edge", None)),
        check_vma=False,
    )
```

```python
import functools
import types

import jax
import jax.numpy as jnp
from jax import lax
from jax.experimental import pallas as pl
from jax.experimental.pallas import tpu as pltpu
from jax.sharding import PartitionSpec as P

MAPH = 48
WINDOW = 7
RADIUS = WINDOW // 2
NEAR = 2
FAR = RADIUS + NEAR
OWNER, TARGET, SOURCE, SPOT, PLACE, GROUP, REL, ASKS = 0, 8, 16, 24, 32, 40, 48, 64
PIECES = 4
MESH = pl.DeviceIdType.MESH
BF = jnp.bfloat16
F32 = jnp.float32


def nt(a, b):
    return lax.dot_general(a, b, (((1,), (1,)), ((), ())), preferred_element_type=F32)


def nn(a, b):
    return lax.dot_general(a, b, (((1,), (0,)), ((), ())), preferred_element_type=F32)


def iota(shape, dim):
    return lax.broadcasted_iota(jnp.int32, shape, dim)


def sixth(index):
    return jnp.floor((index.astype(F32) + 0.5) * (1.0 / 6.0))


def one_hot(cond):
    return cond.astype(F32).astype(BF)


def each(count, body):
    def step(i, carry):
        body(i)
        return carry

    lax.fori_loop(0, count, step, 0)


def reach(halo, rows):
    return [min(rows, halo - d * rows) for d in range((halo + rows - 1) // rows)]


def kernel(dims, names, *refs):
    n_edge, n_tile, edges, frames, rows, width, slots = dims
    r = types.SimpleNamespace(**dict(zip(names, refs)))
    band = rows * width
    per = edges // slots
    me = lax.axis_index("edge")
    tile = lax.axis_index("tile")
    texts = [getattr(r, f"text{s}") for s in range(slots)]

    ints = [
        pltpu.make_async_copy(r.owner_h, r.owner_s, r.l_ints.at[0]),
        pltpu.make_async_copy(r.target_h, r.target_s, r.l_ints.at[1]),
        pltpu.make_async_copy(r.source_h, r.source_s, r.l_ints.at[2]),
        pltpu.make_async_copy(r.count_h, r.count_s, r.l_ints.at[3]),
    ]
    loads = [
        pltpu.make_async_copy(r.feat_h, r.feat, r.l_in.at[0]),
        pltpu.make_async_copy(
            r.hidden_h, r.hext.at[:, pl.ds(NEAR * width, band)], r.l_in.at[1]
        ),
        pltpu.make_async_copy(r.corr_h, r.corr_in, r.l_in.at[2]),
        pltpu.make_async_copy(r.jac_h, r.jac_in, r.l_in.at[3]),
        pltpu.make_async_copy(r.conf_h, r.conf_in, r.l_in.at[4]),
    ]
    first, second = pl.ds(0, 128), pl.ds(128, 128)
    fills = [
        pltpu.make_async_copy(r.gate_w.at[:, :, first], r.wh, r.l_w.at[0]),
        pltpu.make_async_copy(r.gate_w.at[:, :, second], r.wm, r.l_w.at[1]),
    ]
    for part, at in enumerate((first, second)):
        for b in range(3):
            fills.append(
                pltpu.make_async_copy(
                    r.cand_w.at[:, b, at], r.wc.at[part, :, :, pl.ds(b * 128, 128)], r.l_w.at[2]
                )
            )
    filled = fills[:2] + [pltpu.make_async_copy(r.wc, r.wc, r.l_w.at[2])]
    for load in ints:
        load.start()

    barrier = pltpu.get_barrier_semaphore()
    for rel in range(1, n_edge):
        pl.semaphore_signal(
            barrier, inc=1, device_id=((me + rel) % n_edge, tile), device_id_type=MESH
        )
    for rel in range(1, n_tile):
        pl.semaphore_signal(
            barrier, inc=1, device_id=(me, (tile + rel) % n_tile), device_id_type=MESH
        )

    for load in loads + fills:
        load.start()

    for load in ints:
        load.wait()
    owner = [r.owner_s[e] for e in range(edges)]
    rel_of = [(owner[e] - me + n_edge) % n_edge for e in range(edges)]
    rank, group = [], []
    for e in range(edges):
        before = jnp.int32(0)
        for k in range(e):
            before = before + (owner[k] == owner[e]).astype(jnp.int32)
        rank.append(jnp.minimum(before, slots - 1))
        group.append(jnp.where(rel_of[e] == 0, 0, rank[e] + 1))
    lane = iota((1, 128), 1)
    row = jnp.zeros((1, 128), jnp.int32)
    for e in range(edges):
        spot = jnp.int32(0)
        for k in range(edges):
            if k < e:
                spot = spot + (group[k] <= group[e]).astype(jnp.int32)
            elif k > e:
                spot = spot + (group[k] < group[e]).astype(jnp.int32)
        goal = r.target_s[e]
        fields = (
            (OWNER, owner[e]),
            (TARGET, goal),
            (SOURCE, r.source_s[e]),
            (PLACE, jnp.int32(e)),
            (GROUP, group[e]),
            (REL, rel_of[e]),
        )
        for base, value in fields:
            row = jnp.where(lane == base + spot, value, row)
        row = jnp.where(lane == SPOT + e, spot, row)
        row = jnp.where(lane == ASKS + rel_of[e] * slots + rank[e], goal, row)
    r.row_v[...] = row
    mine = pltpu.make_async_copy(r.row_v, r.row_s, r.l_row)
    mine.start()

    pl.semaphore_wait(barrier, n_edge + n_tile - 2)

    def remote(src, dst, send_sem, recv_sem, edge_id, tile_id):
        return pltpu.make_async_remote_copy(
            src_ref=src,
            dst_ref=dst,
            send_sem=send_sem,
            recv_sem=recv_sem,
            device_id=(edge_id, tile_id),
            device_id_type=MESH,
        )

    def meta_copy(rel):
        return remote(
            r.row_v, r.meta_s.at[me], r.s_meta.at[rel - 1], r.r_meta.at[rel - 1],
            (me + rel) % n_edge, tile,
        )

    others = n_edge - 1
    for rel in range(1, n_edge):
        meta_copy(rel).start()
    own_row = pltpu.make_async_copy(r.row_v, r.meta_s.at[me], r.l_own)
    own_row.start()

    class Halo:
        def __init__(self, halo, lot, buf, source, sems):
            self.halo, self.lot, self.buf, self.source, self.sems = halo, lot, buf, source, sems
            self.counts = reach(halo, rows)

        def copies(self, i, lot):
            which = pl.ds(i * lot, lot)
            for d, count in enumerate(self.counts):
                far, lines = d + 1, count * width
                s_up, r_up, s_dn, r_dn = self.sems
                up = remote(
                    self.source(which, 0, lines),
                    self.buf.at[which, pl.ds((self.halo + far * rows) * width, lines)],
                    s_up.at[d], r_up.at[d, i], me, tile - far,
                )
                dn = remote(
                    self.source(which, band - lines, lines),
                    self.buf.at[which, pl.ds((self.halo - d * rows - count) * width, lines)],
                    s_dn.at[d], r_dn.at[d, i], me, tile + far,
                )
                yield tile >= far, tile + far < n_tile, up, dn

        def start(self, i):
            for above, below, up, dn in self.copies(i, self.lot):
                pl.when(above)(up.start)
                pl.when(below)(dn.start)

        def received(self, i):
            for above, below, up, dn in self.copies(i, self.lot):
                pl.when(below)(up.wait_recv)
                pl.when(above)(dn.wait_recv)

        def sent(self):
            for above, below, up, dn in self.copies(0, edges):
                pl.when(above)(up.wait_send)
                pl.when(below)(dn.wait_send)

        def clear(self):
            for d, count in enumerate(self.counts):
                far, lines = d + 1, count * width
                zero = jnp.zeros((lines, 128), BF)
                top = (self.halo - d * rows - count) * width
                low = (self.halo + far * rows) * width

                @pl.when(tile < far)
                def _():
                    def clear_top(e):
                        self.buf[e, pl.ds(top, lines)] = zero

                    each(edges, clear_top)

                @pl.when(tile + far >= n_tile)
                def _():
                    def clear_low(e):
                        self.buf[e, pl.ds(low, lines)] = zero

                    each(edges, clear_low)

            used = (rows + 2 * self.halo) * width
            spare = self.buf.shape[1] - used
            if spare:

                def clear_pad(e):
                    self.buf[e, pl.ds(used, spare)] = jnp.zeros((spare, 128), BF)

                each(edges, clear_pad)

    def inner(buf, halo):
        return lambda which, at, lines: buf.at[which, pl.ds(halo * width + at, lines)]

    hid = Halo(
        NEAR, edges, r.hext, lambda which, at, lines: r.hidden_h.at[which, pl.ds(at, lines)],
        (r.s_hup, r.r_hup, r.s_hdn, r.r_hdn),
    )
    src = Halo(
        NEAR, edges, r.sext, inner(r.sext, NEAR), (r.s_sup, r.r_sup, r.s_sdn, r.r_sdn)
    )
    txt = Halo(FAR, per, r.text, inner(r.text, FAR), (r.s_tup, r.r_tup, r.s_tdn, r.r_tdn))

    loads[0].wait()

    turns = [n_edge // 2]
    turns += [n_edge - k - (n_edge - 2 * k) * (me % 2) for k in range(1, (n_edge + 1) // 2)]
    turns += [k + (n_edge - 2 * k) * (me % 2) for k in range(1, (n_edge + 1) // 2)]

    def feat_copy(rel, s):
        return remote(
            r.send.at[s * others + rel - 1], texts[s].at[rel - 1],
            r.s_feat, r.r_feat.at[s], (me - rel + n_edge) % n_edge, tile,
        )

    def feat_group(s):
        return remote(
            r.send.at[pl.ds(s * others, others)], texts[s],
            r.s_feat, r.r_feat.at[s], (me + 1) % n_edge, tile,
        )

    for s in range(slots):
        for rel in turns:
            peer = (me - rel + n_edge) % n_edge
            if s == 0:
                remote(
                    r.row_v, r.meta_s.at[peer], r.s_meta.at[rel - 1], r.r_meta.at[rel - 1],
                    (me + rel) % n_edge, tile,
                ).wait_recv()
            r.send[s * others + rel - 1] = r.feat[r.meta_s[peer, 0, ASKS + rel * slots + s]]
            feat_copy(rel, s).start()

    hid.start(0)
    mine.wait()

    def take_source(e):
        r.sext[e, pl.ds(NEAR * width, band)] = r.feat[r.row_s[0, SOURCE + e]]

    each(edges, take_source)
    src.start(0)
    for halo in (hid, src, txt):
        halo.clear()

    for load in loads[2:]:
        load.wait()

    spot = (iota((128, 64), 0) + 4) & 127
    along = ((spot >> 3) & 3) * 2 + (spot >> 6) - ((spot >> 5) & 1)
    across = WINDOW - 1 - (spot & 7)
    fits = (across >= 0) & (along >= 0) & (along < WINDOW)
    pick = (iota((128, 64), 1) == along * WINDOW + across) & fits
    lookup = jnp.concatenate(
        [r.corr_in[...].astype(F32), jnp.zeros((64 - WINDOW * WINDOW, 128), F32)], axis=0
    ).astype(BF)
    r.corr_w[...] = nn(one_hot(pick), lookup).astype(BF)

    place12 = iota((32, 64), 0)
    which = place12 >> 4
    within = place12 & 15
    name12 = iota((32, 64), 1)
    pick_j = (within < 12) & (name12 == which * 12 + within)
    padded_jac = jnp.concatenate(
        [r.jac_in[...].astype(F32), jnp.zeros((40, 128), F32)], axis=0
    ).astype(BF)
    conf_wide = r.conf_in[...].astype(F32)
    tall = iota((32, 128), 0)
    conf_rows = jnp.where(
        tall < 16,
        jnp.broadcast_to(conf_wide[0:1], (32, 128)),
        jnp.broadcast_to(conf_wide[1:2], (32, 128)),
    )
    r.head_w[...] = jnp.concatenate(
        [nn(one_hot(pick_j), padded_jac), jnp.where((tall & 15) < 12, conf_rows, 0.0)], axis=0
    ).astype(BF)

    def nudge(wide, by):
        lines = wide.shape[0]
        column = iota((lines, 128), 0) & (width - 1)
        edge = 0 if by == 1 else width - 1
        return jnp.where(column == edge, 0.0, pltpu.roll(wide, by % lines, 0))

    def spread(value, out):
        lines = value.shape[0]
        wide = value.astype(F32)
        out[0:lines, 0:128] = nudge(wide, 1).astype(BF)
        out[0:lines, 128:256] = value.astype(BF)
        out[0:lines, 256:384] = nudge(wide, -1).astype(BF)

    def windows(x3, q, out_rows):
        size = out_rows * width
        return jnp.concatenate([x3[q, a * width : a * width + size] for a in range(3)], axis=1)

    wide_band = (rows + 2) * width

    def state_part(p):
        for q in range(per):
            e = p * per + q
            spread(r.hext[r.row_s[0, PLACE + e]], r.x3.at[q])
            r.gpre[e] = nn(windows(r.x3, q, rows + 2), r.wh[...].reshape(9 * 128, 256))

    loads[1].wait()
    for fill in filled:
        fill.wait()
    flip_row, flip_col = iota((2 * width, 2 * width), 0), iota((2 * width, 2 * width), 1)
    flip = one_hot(
        (flip_row // width == flip_col // width)
        & ((flip_row & (width - 1)) + (flip_col & (width - 1)) == width - 1)
    )

    def take_target(e, upto):
        value = r.feat[r.row_s[0, TARGET + e]]
        at = jnp.maximum(r.row_s[0, REL + e] - 1, 0)
        for s in range(upto + 1):
            value = jnp.where(r.row_s[0, GROUP + e] == s + 1, texts[s][at], value)
        for first in range(0, band, 2 * width):
            count = min(2 * width, band - first)
            r.text[e, pl.ds(FAR * width + first, count)] = nn(
                flip[0:count, 0:count], value[first : first + count]
            ).astype(BF)

    def take(s):
        feat_group(s).wait_recv()
        for q in range(per):
            take_target(s * per + q, s)
        txt.start(s)

    hid.received(0)
    each(slots // 2, state_part)
    take(0)
    each(slots - slots // 2, lambda p: state_part(p + slots // 2))
    src.received(0)

    own_row.wait()
    cam_cols = frames * 6
    cam_rows = r.where_v.shape[1] - cam_cols
    part = iota((cam_rows + cam_cols, 128), 0)
    index = jnp.where(part < cam_rows, part + tile * cam_rows, part - cam_rows + me * cam_cols)
    inside = lane & 15
    digit = jnp.where(inside < 6, inside, inside - 6)

    def place(j):
        spots = jnp.full((1, 128), -1, jnp.int32)
        for e in range(edges):
            source = (j * frames + r.meta_s[j, 0, SOURCE + e]) * 6
            target = (r.meta_s[j, 0, OWNER + e] * frames + r.meta_s[j, 0, TARGET + e]) * 6
            here = jnp.where(inside < 6, source, target) + digit
            spots = jnp.where(((lane >> 4) == e) & (inside < 12), here, spots)
        r.where_v[j] = one_hot(index == spots)

    each(n_edge, place)
    tables = pltpu.make_async_copy(r.where_v, r.where_h, r.l_meta)
    tables.start()

    lane_w = (iota((width, 128), 1) + 4) & 127
    col_w = iota((width, 128), 0) + RADIUS - (lane_w & 7)
    in_map = (col_w >= 0) & (col_w < width) & ((lane_w & 7) < WINDOW)
    scaled = [
        jnp.where(in_map & (((lane_w >> 5) & 1) == par), 128.0 ** (-0.5), 0.0) for par in range(2)
    ]
    slot_w = (lane_w >> 3) & 3
    pairs_of = (rows + 2 * NEAR + 1) // 2
    quads_of = r.text.shape[1] // (4 * width)
    used_rows = (rows + 2 * NEAR) * width

    def motion_of(e, q):
        tables, starts = [], []
        for m in range(quads_of):
            first, last = max(0, 2 * m - 3), min(pairs_of - 1, 2 * m + 1)
            starts.append(first)
            tables.append(
                nt(
                    r.sext[e, pl.ds(2 * first * width, 2 * (last - first + 1) * width)],
                    r.text[e, pl.ds(4 * m * width, 4 * width)],
                )
            )
        lines = []
        for k in range(pairs_of):
            for par in range(2):
                found = None
                for g in range(4):
                    m, h = divmod(k + g, 2)
                    at = (2 * (k - starts[m]) + par) * width
                    piece = tables[m][at : at + width, h * 128 : (h + 1) * 128]
                    moved = pltpu.roll(
                        piece, width + 8 * g + 32 * par, 1, stride=1, stride_axis=0
                    )
                    found = moved if g == 0 else jnp.where(slot_w == g, moved, found)
                lines.append((found * scaled[par]).astype(BF))
        value = nn(jnp.concatenate(lines, axis=0), r.corr_w[...])
        spread(jnp.maximum(value[0:used_rows], 0.0), r.x3.at[q])

    def update(p):
        txt.received(p)
        for q in range(per):
            motion_of(p * per + q, q)
        for q in range(per):
            e = p * per + q
            before = r.gpre[e] + nn(windows(r.x3, q, rows + 2), r.wm[...].reshape(9 * 128, 256))
            r.upd[q] = 0.5 * jnp.tanh(0.5 * before[width : width + band, 0:128]) + 0.5
            reset = 0.5 * jnp.tanh(0.5 * before[:, 128:256]) + 0.5
            state = r.hext[r.row_s[0, PLACE + e], pl.ds(width, wide_band)].astype(F32)
            r.rext[q] = (reset * state).astype(BF)
        for q in range(per):
            e = p * per + q
            part = nn(
                jnp.concatenate(
                    [r.rext[q, a * width : a * width + band] for a in range(3)]
                    + [
                        r.x3[q, (a + 1) * width : (a + 1) * width + band, 128:256]
                        for a in range(3)
                    ],
                    axis=1,
                ),
                r.wc[...].reshape(6 * 128, 384),
            )
            candidate = jnp.tanh(
                nudge(part[:, 0:128], 1) + part[:, 128:256] + nudge(part[:, 256:384], -1)
            )
            gate = r.upd[q]
            place = r.row_s[0, PLACE + e]
            state = r.hext[place, pl.ds(NEAR * width, band)]
            fresh = ((1.0 - gate) * state.astype(F32) + gate * candidate).astype(BF)
            used = (place < r.count_s[0]).astype(F32)
            live = jnp.full((band, 128), used) > 0.5
            r.held[e] = jnp.where(live, fresh, state)
            heads = nt(r.head_w[...], fresh)
            jac = heads[0:32]
            weighted = jac * jax.nn.softplus(heads[32:64])
            at16 = pl.ds(pl.multiple_of(e * 16, 16), 16)
            r.jall[at16] = jnp.concatenate([jac[0:16], jac[16:32]], axis=1).astype(BF)
            r.wall[at16] = jnp.concatenate([weighted[0:16], weighted[16:32]], axis=1).astype(BF)

    def stage(p):
        for s in range(1, slots):

            @pl.when(p == s - 1)
            def _():
                take(s)

        update(p)

    each(slots, stage)
    same = (iota((128, 128), 0) >> 4) == (iota((128, 128), 1) >> 4)
    square = jnp.where(same, nt(r.wall[...], r.jall[...]), 0.0)
    blocks = square[0:16]
    for e in range(1, edges):
        blocks = blocks + square[e * 16 : (e + 1) * 16]
    blocks = blocks * (1.0 / (MAPH * width))
    of = iota((16, 128), 1) >> 4
    for e in range(edges):
        used = (r.row_s[0, PLACE + e] < r.count_s[0]).astype(jnp.int32)
        blocks = jnp.where((of == e) & (jnp.full((16, 128), used) == 0), 0.0, blocks)
    r.gpart[...] = blocks

    def tile_copy(rel):
        return remote(
            r.gpart, r.gtile.at[tile], r.s_gt, r.r_gt, me, (tile + rel) % n_tile
        )

    def all_tiles():
        some = r.gtile.at[pl.ds(0, n_tile - 1)]
        return remote(some, some, r.s_gt, r.r_gt, me, (tile + 1) % n_tile)

    for rel in range(1, n_tile):
        tile_copy(rel).start()
    r.gtile[tile] = r.gpart[...]

    def put_back(e):
        r.ready[e] = r.held[r.row_s[0, SPOT + e]]

    each(edges, put_back)
    store = pltpu.make_async_copy(r.ready, r.out_hidden, r.l_out)
    store.start()
    all_tiles().wait_recv()
    total = r.gtile[0]
    for k in range(1, n_tile):
        total = total + r.gtile[k]
    r.gsum[...] = total

    def edge_copy(rel):
        return remote(r.gsum, r.gall_h.at[me], r.s_ge, r.r_ge, (me + rel) % n_edge, tile)

    def all_edges():
        some = r.gall_h.at[pl.ds(0, others)]
        return remote(some, some, r.s_ge, r.r_ge, (me + 1) % n_edge, tile)

    for rel in range(1, n_edge):
        edge_copy(rel).start()
    own_sum = pltpu.make_async_copy(r.gsum, r.gall_h.at[me], r.l_sum)
    own_sum.start()
    all_edges().wait_recv()

    own_sum.wait()
    store.wait()
    tables.wait()
    for rel in range(1, n_edge):
        meta_copy(rel).wait_send()
    for s in range(slots):
        feat_group(s).wait_send()
    all_tiles().wait_send()
    all_edges().wait_send()
    for halo in (hid, src, txt):
        halo.sent()


def halves(value):
    high = value.astype(BF)
    return high, (value - high.astype(F32)).astype(BF)


def assemble(
    dims, where_h, gall_h, hidden_h, out_hidden, cam_h, diag_h, where_v, gall, out_cam, out_diag, held,
    sem, held_sem,
):
    n_edge, n_tile, edges, frames, rows, width, slots = dims
    me = lax.axis_index("edge")
    tile = lax.axis_index("tile")
    loads = [
        pltpu.make_async_copy(gall_h, gall, sem.at[0]),
        pltpu.make_async_copy(where_h, where_v, sem.at[1]),
    ]
    pieces = [pl.ds(i * (edges // PIECES), edges // PIECES) for i in range(PIECES)]
    fetches = [
        pltpu.make_async_copy(hidden_h.at[p], held.at[p], held_sem.at[i])
        for i, p in enumerate(pieces)
    ]
    stores = [
        pltpu.make_async_copy(held.at[p], out_hidden.at[p], held_sem.at[i])
        for i, p in enumerate(pieces)
    ]
    for load in loads + fetches:
        load.start()
    cam_rows, cam_cols = out_cam.shape
    same = (iota((128, 128), 0) >> 4) == (iota((128, 128), 1) >> 4)
    for load in loads:
        load.wait()
    for fetch, store in zip(fetches, stores):
        fetch.wait()
        store.start()
    lefts, lows, rights = [], [], []
    for j in range(n_edge):
        left = where_v[j]
        stack = jnp.where(same, jnp.concatenate([gall[j]] * 8, axis=0), 0.0)
        picked = nn(
            jnp.concatenate([left, left], axis=1), jnp.concatenate(halves(stack), axis=0)
        )
        high, low = halves(picked)
        lefts.append(high)
        lows.append(low)
        rights.append(left[cam_rows:])
    placed = nt(jnp.concatenate(lefts + lows, axis=1), jnp.concatenate(rights + rights, axis=1))
    cam = placed[0:cam_rows]
    row_frame = sixth(iota((cam_rows, cam_cols), 0) + tile * cam_rows)
    col_frame = sixth(iota((cam_rows, cam_cols), 1) + me * cam_cols)
    out_cam[...] = jnp.where(row_frame == col_frame, 0.0, cam)
    cam_store = pltpu.make_async_copy(out_cam, cam_h, sem.at[0])
    cam_store.start()
    own = placed[cam_rows:]
    own_row = sixth(iota((cam_cols, cam_cols), 0))
    own_col = sixth(iota((cam_cols, cam_cols), 1))
    own = jnp.where(own_row == own_col, own, 0.0)
    wide_row = iota((cam_cols, 128), 0)
    wide_lane = iota((cam_cols, 128), 1)
    row_in = wide_row.astype(F32) - 6.0 * sixth(wide_row)
    lane_of = sixth(wide_lane)
    lane_in = wide_lane.astype(F32) - 6.0 * lane_of
    gather = one_hot(row_in == lane_in)
    high, low = halves(own)
    spread = jnp.where(row_in == lane_of, nn(high, gather) + nn(low, gather), 0.0)
    fold = one_hot(
        sixth(iota((frames, cam_cols), 1)) == iota((frames, cam_cols), 0).astype(F32)
    )
    high, low = halves(spread)
    out_diag[...] = (nn(fold, high) + nn(fold, low))[:, 0:36]
    diag_store = pltpu.make_async_copy(out_diag, diag_h, sem.at[1])
    diag_store.start()
    for store in stores + [cam_store, diag_store]:
        store.wait()


def per_device(
    features,
    hidden_state,
    edge_source,
    edge_owner,
    edge_target,
    edge_counts,
    corr_weight,
    gate_weight,
    candidate_weight,
    jacobian_weight,
    confidence_weight,
):
    n_edge, n_tile = lax.axis_size("edge"), lax.axis_size("tile")
    edges = hidden_state.shape[0]
    frames, rows, width, chan = features.shape
    slots = max(2, (2 * edges + n_edge - 1) // n_edge)
    assert edges % slots == 0 and edges <= 8 and ASKS + n_edge * slots <= 128
    per = edges // slots
    band = rows * width

    dims = (n_edge, n_tile, edges, frames, rows, width, slots)
    even = (rows + 2 * NEAR + 1) // 2 * 2
    dma = pltpu.SemaphoreType.DMA
    hbm = pl.BlockSpec(memory_space=pl.ANY)

    inputs = (
        ("owner_h", edge_owner[:, 0], hbm),
        ("target_h", edge_target, hbm),
        ("source_h", edge_source, hbm),
        ("count_h", edge_counts, hbm),
        ("feat_h", features.reshape(frames, band, chan), hbm),
        ("hidden_h", hidden_state.reshape(edges, band, chan), hbm),
        ("corr_h", corr_weight, hbm),
        ("gate_w", gate_weight, hbm),
        ("cand_w", candidate_weight, hbm),
        ("jac_h", jacobian_weight.T, hbm),
        ("conf_h", confidence_weight.T, hbm),
    )
    cam_rows, cam_cols = frames * n_edge * 6 // n_tile, frames * 6
    places = (n_edge, cam_rows + cam_cols, 128)
    outputs = (
        ("out_hidden", (edges, band, chan), BF, hbm),
        ("gall_h", (n_edge, 16, 128), F32, hbm),
        ("where_h", places, BF, hbm),
    )
    near, far = len(reach(NEAR, rows)), len(reach(FAR, rows))
    scratch = {
        "owner_s": pltpu.SMEM((edges,), jnp.int32),
        "target_s": pltpu.SMEM((edges,), jnp.int32),
        "source_s": pltpu.SMEM((edges,), jnp.int32),
        "count_s": pltpu.SMEM((1,), jnp.int32),
        "corr_in": pltpu.VMEM(corr_weight.shape, BF),
        "jac_in": pltpu.VMEM(jacobian_weight.shape[::-1], BF),
        "conf_in": pltpu.VMEM(confidence_weight.shape[::-1], BF),
        "row_v": pltpu.VMEM((1, 128), jnp.int32),
        "row_s": pltpu.SMEM((1, 128), jnp.int32),
        "meta_s": pltpu.SMEM((n_edge, 1, 128), jnp.int32),
        "feat": pltpu.VMEM((frames, band, chan), BF),
        "held": pltpu.VMEM((edges, band, chan), BF),
        "ready": pltpu.VMEM((edges, band, chan), BF),
        "where_v": pltpu.VMEM(places, BF),
        "send": pltpu.VMEM(((n_edge - 1) * slots, band, chan), BF),
        "text": pltpu.VMEM((edges, (even + 2 * RADIUS + 3) // 4 * 4 * width, chan), BF),
        "sext": pltpu.VMEM((edges, even * width, chan), BF),
        "hext": pltpu.VMEM((edges, (rows + 2 * NEAR) * width, chan), BF),
        "rext": pltpu.VMEM((per, (rows + 2) * width, chan), BF),
        "x3": pltpu.VMEM((per, (rows + 2 * NEAR) * width, 3 * chan), BF),
        "wh": pltpu.VMEM((3, 3, chan, 2 * chan), BF),
        "wm": pltpu.VMEM((3, 3, chan, 2 * chan), BF),
        "wc": pltpu.VMEM((2, 3, chan, 3 * chan), BF),
        "corr_w": pltpu.VMEM((128, chan), BF),
        "head_w": pltpu.VMEM((64, chan), BF),
        "gpre": pltpu.VMEM((edges, (rows + 2) * width, 2 * chan), F32),
        "upd": pltpu.VMEM((per, band, chan), F32),
        "jall": pltpu.VMEM((128, 2 * band), BF),
        "wall": pltpu.VMEM((128, 2 * band), BF),
        "gpart": pltpu.VMEM((16, 128), F32),
        "gtile": pltpu.VMEM((n_tile, 16, 128), F32),
        "gsum": pltpu.VMEM((16, 128), F32),
        "l_in": dma((5,)),
        "l_w": dma((3,)),
        "l_ints": dma((4,)),
        "l_row": dma,
        "l_meta": dma,
        "l_own": dma,
        "l_sum": dma,
        "l_out": dma,
        "s_meta": dma((n_edge - 1,)),
        "r_meta": dma((n_edge - 1,)),
        "s_feat": dma,
        "r_feat": dma((slots,)),
        "s_gt": dma,
        "r_gt": dma,
        "s_ge": dma,
        "r_ge": dma,
    }
    for s in range(slots):
        scratch[f"text{s}"] = pltpu.VMEM((n_edge - 1, band, chan), BF)
    for key, count, lots in (("h", near, 1), ("s", near, 1), ("t", far, slots)):
        for way in ("up", "dn"):
            scratch[f"s_{key}{way}"] = dma((count,))
            scratch[f"r_{key}{way}"] = dma((count, lots))
    names = [i[0] for i in inputs] + [o[0] for o in outputs] + list(scratch)
    state, gall, where = pl.pallas_call(
        functools.partial(kernel, dims, names),
        out_shape=tuple(jax.ShapeDtypeStruct(shape, kind) for _, shape, kind, _ in outputs),
        in_specs=[spec for _, _, spec in inputs],
        out_specs=tuple(spec for _, _, _, spec in outputs),
        scratch_shapes=list(scratch.values()),
        compiler_params=pltpu.CompilerParams(
            collective_id=0, has_side_effects=True, vmem_limit_bytes=56 * 1024 * 1024
        ),
    )(*[value for _, value, _ in inputs])
    hidden_next, cam, diag = pl.pallas_call(
        functools.partial(assemble, dims),
        out_shape=(
            jax.ShapeDtypeStruct((edges, band, chan), BF),
            jax.ShapeDtypeStruct((cam_rows, cam_cols), F32),
            jax.ShapeDtypeStruct((frames, 36), F32),
        ),
        in_specs=[hbm] * 3,
        out_specs=(hbm,) * 3,
        scratch_shapes=[
            pltpu.VMEM(places, BF),
            pltpu.VMEM((n_edge, 16, 128), F32),
            pltpu.VMEM((cam_rows, cam_cols), F32),
            pltpu.VMEM((frames, 36), F32),
            pltpu.VMEM((edges, band, chan), BF),
            dma((2,)),
            dma((PIECES,)),
        ],
    )(where, gall, state)
    return hidden_next.reshape(hidden_state.shape), cam, diag


def solution(mesh):
    placed = (
        P("edge", "tile", None, None),
        P("edge", "tile", None, None),
        P("edge"),
        P("edge", None),
        P("edge"),
        P("edge"),
        P(),
        P(),
        P(),
        P(),
        P(),
    )
    return jax.shard_map(
        per_device,
        mesh=mesh,
        in_specs=placed,
        out_specs=(P("edge", "tile", None, None), P("tile", "edge"), P("edge", None)),
        check_vma=False,
    )
```

```python
import functools
import types

import jax
import jax.numpy as jnp
from jax import lax
from jax.experimental import pallas as pl
from jax.experimental.pallas import tpu as pltpu
from jax.sharding import PartitionSpec as P

MAPH = 48
WINDOW = 7
RADIUS = WINDOW // 2
NEAR = 2
FAR = RADIUS + NEAR
OWNER, TARGET, SOURCE, SPOT, PLACE, GROUP, REL, ASKS = 0, 8, 16, 24, 32, 40, 48, 64
PIECES = 4
MESH = pl.DeviceIdType.MESH
BF = jnp.bfloat16
F32 = jnp.float32


def nt(a, b):
    return lax.dot_general(a, b, (((1,), (1,)), ((), ())), preferred_element_type=F32)


def nn(a, b):
    return lax.dot_general(a, b, (((1,), (0,)), ((), ())), preferred_element_type=F32)


def iota(shape, dim):
    return lax.broadcasted_iota(jnp.int32, shape, dim)


def sixth(index):
    return jnp.floor((index.astype(F32) + 0.5) * (1.0 / 6.0))


def one_hot(cond):
    return cond.astype(F32).astype(BF)


def each(count, body):
    def step(i, carry):
        body(i)
        return carry

    lax.fori_loop(0, count, step, 0)


def reach(halo, rows):
    return [min(rows, halo - d * rows) for d in range((halo + rows - 1) // rows)]


def kernel(dims, names, *refs):
    n_edge, n_tile, edges, frames, rows, width, slots = dims
    r = types.SimpleNamespace(**dict(zip(names, refs)))
    band = rows * width
    per = edges // slots
    me = lax.axis_index("edge")
    tile = lax.axis_index("tile")
    texts = [getattr(r, f"text{s}") for s in range(slots)]

    ints = [
        pltpu.make_async_copy(r.owner_h, r.owner_s, r.l_ints.at[0]),
        pltpu.make_async_copy(r.target_h, r.target_s, r.l_ints.at[1]),
        pltpu.make_async_copy(r.source_h, r.source_s, r.l_ints.at[2]),
        pltpu.make_async_copy(r.count_h, r.count_s, r.l_ints.at[3]),
    ]
    loads = [
        pltpu.make_async_copy(r.feat_h, r.feat, r.l_in.at[0]),
        pltpu.make_async_copy(
            r.hidden_h, r.hext.at[:, pl.ds(NEAR * width, band)], r.l_in.at[1]
        ),
        pltpu.make_async_copy(r.corr_h, r.corr_in, r.l_in.at[2]),
        pltpu.make_async_copy(r.jac_h, r.jac_in, r.l_in.at[3]),
        pltpu.make_async_copy(r.conf_h, r.conf_in, r.l_in.at[4]),
    ]
    first, second = pl.ds(0, 128), pl.ds(128, 128)
    fills = [
        pltpu.make_async_copy(r.gate_w.at[:, :, first], r.wh, r.l_w.at[0]),
        pltpu.make_async_copy(r.gate_w.at[:, :, second], r.wm, r.l_w.at[1]),
    ]
    for part, at in enumerate((first, second)):
        for b in range(3):
            fills.append(
                pltpu.make_async_copy(
                    r.cand_w.at[:, b, at], r.wc.at[part, :, :, pl.ds(b * 128, 128)], r.l_w.at[2]
                )
            )
    filled = fills[:2] + [pltpu.make_async_copy(r.wc, r.wc, r.l_w.at[2])]
    for load in ints:
        load.start()

    barrier = pltpu.get_barrier_semaphore()
    for rel in range(1, n_edge):
        pl.semaphore_signal(
            barrier, inc=1, device_id=((me + rel) % n_edge, tile), device_id_type=MESH
        )
    for rel in range(1, n_tile):
        pl.semaphore_signal(
            barrier, inc=1, device_id=(me, (tile + rel) % n_tile), device_id_type=MESH
        )

    for load in loads + fills:
        load.start()

    for load in ints:
        load.wait()
    owner = [r.owner_s[e] for e in range(edges)]
    rel_of = [(owner[e] - me + n_edge) % n_edge for e in range(edges)]
    rank, group = [], []
    for e in range(edges):
        before = jnp.int32(0)
        for k in range(e):
            before = before + (owner[k] == owner[e]).astype(jnp.int32)
        rank.append(jnp.minimum(before, slots - 1))
        group.append(jnp.where(rel_of[e] == 0, 0, rank[e] + 1))
    lane = iota((1, 128), 1)
    row = jnp.zeros((1, 128), jnp.int32)
    for e in range(edges):
        spot = jnp.int32(0)
        for k in range(edges):
            if k < e:
                spot = spot + (group[k] <= group[e]).astype(jnp.int32)
            elif k > e:
                spot = spot + (group[k] < group[e]).astype(jnp.int32)
        goal = r.target_s[e]
        fields = (
            (OWNER, owner[e]),
            (TARGET, goal),
            (SOURCE, r.source_s[e]),
            (PLACE, jnp.int32(e)),
            (GROUP, group[e]),
            (REL, rel_of[e]),
        )
        for base, value in fields:
            row = jnp.where(lane == base + spot, value, row)
        row = jnp.where(lane == SPOT + e, spot, row)
        row = jnp.where(lane == ASKS + rel_of[e] * slots + rank[e], goal, row)
    r.row_v[...] = row
    mine = pltpu.make_async_copy(r.row_v, r.row_s, r.l_row)
    mine.start()

    pl.semaphore_wait(barrier, n_edge + n_tile - 2)

    def remote(src, dst, send_sem, recv_sem, edge_id, tile_id):
        return pltpu.make_async_remote_copy(
            src_ref=src,
            dst_ref=dst,
            send_sem=send_sem,
            recv_sem=recv_sem,
            device_id=(edge_id, tile_id),
            device_id_type=MESH,
        )

    def meta_copy(rel):
        return remote(
            r.row_v, r.meta_s.at[me], r.s_meta.at[rel - 1], r.r_meta.at[rel - 1],
            (me + rel) % n_edge, tile,
        )

    others = n_edge - 1
    for rel in range(1, n_edge):
        meta_copy(rel).start()
    own_row = pltpu.make_async_copy(r.row_v, r.meta_s.at[me], r.l_own)
    own_row.start()

    class Halo:
        def __init__(self, halo, lot, buf, source, sems):
            self.halo, self.lot, self.buf, self.source, self.sems = halo, lot, buf, source, sems
            self.counts = reach(halo, rows)

        def copies(self, i, lot):
            which = pl.ds(i * lot, lot)
            for d, count in enumerate(self.counts):
                far, lines = d + 1, count * width
                s_up, r_up, s_dn, r_dn = self.sems
                up = remote(
                    self.source(which, 0, lines),
                    self.buf.at[which, pl.ds((self.halo + far * rows) * width, lines)],
                    s_up.at[d], r_up.at[d, i], me, tile - far,
                )
                dn = remote(
                    self.source(which, band - lines, lines),
                    self.buf.at[which, pl.ds((self.halo - d * rows - count) * width, lines)],
                    s_dn.at[d], r_dn.at[d, i], me, tile + far,
                )
                yield tile >= far, tile + far < n_tile, up, dn

        def start(self, i):
            for above, below, up, dn in self.copies(i, self.lot):
                pl.when(above)(up.start)
                pl.when(below)(dn.start)

        def received(self, i):
            for above, below, up, dn in self.copies(i, self.lot):
                pl.when(below)(up.wait_recv)
                pl.when(above)(dn.wait_recv)

        def sent(self):
            for above, below, up, dn in self.copies(0, edges):
                pl.when(above)(up.wait_send)
                pl.when(below)(dn.wait_send)

        def clear(self):
            for d, count in enumerate(self.counts):
                far, lines = d + 1, count * width
                zero = jnp.zeros((lines, 128), BF)
                top = (self.halo - d * rows - count) * width
                low = (self.halo + far * rows) * width

                @pl.when(tile < far)
                def _():
                    def clear_top(e):
                        self.buf[e, pl.ds(top, lines)] = zero

                    each(edges, clear_top)

                @pl.when(tile + far >= n_tile)
                def _():
                    def clear_low(e):
                        self.buf[e, pl.ds(low, lines)] = zero

                    each(edges, clear_low)

            used = (rows + 2 * self.halo) * width
            spare = self.buf.shape[1] - used
            if spare:

                def clear_pad(e):
                    self.buf[e, pl.ds(used, spare)] = jnp.zeros((spare, 128), BF)

                each(edges, clear_pad)

    def inner(buf, halo):
        return lambda which, at, lines: buf.at[which, pl.ds(halo * width + at, lines)]

    hid = Halo(
        NEAR, edges, r.hext, lambda which, at, lines: r.hidden_h.at[which, pl.ds(at, lines)],
        (r.s_hup, r.r_hup, r.s_hdn, r.r_hdn),
    )
    src = Halo(
        NEAR, edges, r.sext, inner(r.sext, NEAR), (r.s_sup, r.r_sup, r.s_sdn, r.r_sdn)
    )
    txt = Halo(FAR, per, r.text, inner(r.text, FAR), (r.s_tup, r.r_tup, r.s_tdn, r.r_tdn))

    loads[0].wait()

    turns = [n_edge // 2]
    turns += [n_edge - k - (n_edge - 2 * k) * (me % 2) for k in range(1, (n_edge + 1) // 2)]
    turns += [k + (n_edge - 2 * k) * (me % 2) for k in range(1, (n_edge + 1) // 2)]

    def feat_copy(rel, s):
        return remote(
            r.send.at[s * others + rel - 1], texts[s].at[rel - 1],
            r.s_feat, r.r_feat.at[s], (me - rel + n_edge) % n_edge, tile,
        )

    def feat_group(s):
        return remote(
            r.send.at[pl.ds(s * others, others)], texts[s],
            r.s_feat, r.r_feat.at[s], (me + 1) % n_edge, tile,
        )

    for s in range(slots):
        for rel in turns:
            peer = (me - rel + n_edge) % n_edge
            if s == 0:
                remote(
                    r.row_v, r.meta_s.at[peer], r.s_meta.at[rel - 1], r.r_meta.at[rel - 1],
                    (me + rel) % n_edge, tile,
                ).wait_recv()
            r.send[s * others + rel - 1] = r.feat[r.meta_s[peer, 0, ASKS + rel * slots + s]]
            feat_copy(rel, s).start()

    hid.start(0)
    mine.wait()

    def take_source(e):
        r.sext[e, pl.ds(NEAR * width, band)] = r.feat[r.row_s[0, SOURCE + e]]

    each(edges, take_source)
    src.start(0)
    for halo in (hid, src, txt):
        halo.clear()

    for load in loads[2:]:
        load.wait()

    spot = (iota((128, 64), 0) + 4) & 127
    along = ((spot >> 3) & 3) * 2 + (spot >> 6) - ((spot >> 5) & 1)
    across = WINDOW - 1 - (spot & 7)
    fits = (across >= 0) & (along >= 0) & (along < WINDOW)
    pick = (iota((128, 64), 1) == along * WINDOW + across) & fits
    lookup = jnp.concatenate(
        [r.corr_in[...].astype(F32), jnp.zeros((64 - WINDOW * WINDOW, 128), F32)], axis=0
    ).astype(BF)
    r.corr_w[...] = nn(one_hot(pick), lookup).astype(BF)

    place12 = iota((32, 64), 0)
    which = place12 >> 4
    within = place12 & 15
    name12 = iota((32, 64), 1)
    pick_j = (within < 12) & (name12 == which * 12 + within)
    padded_jac = jnp.concatenate(
        [r.jac_in[...].astype(F32), jnp.zeros((40, 128), F32)], axis=0
    ).astype(BF)
    conf_wide = r.conf_in[...].astype(F32)
    tall = iota((32, 128), 0)
    conf_rows = jnp.where(
        tall < 16,
        jnp.broadcast_to(conf_wide[0:1], (32, 128)),
        jnp.broadcast_to(conf_wide[1:2], (32, 128)),
    )
    r.head_w[...] = jnp.concatenate(
        [nn(one_hot(pick_j), padded_jac), jnp.where((tall & 15) < 12, conf_rows, 0.0)], axis=0
    ).astype(BF)

    def nudge(wide, by):
        lines = wide.shape[0]
        column = iota((lines, 128), 0) & (width - 1)
        edge = 0 if by == 1 else width - 1
        return jnp.where(column == edge, 0.0, pltpu.roll(wide, by % lines, 0))

    def spread(value, out):
        lines = value.shape[0]
        wide = value.astype(F32)
        out[0:lines, 0:128] = nudge(wide, 1).astype(BF)
        out[0:lines, 128:256] = value.astype(BF)
        out[0:lines, 256:384] = nudge(wide, -1).astype(BF)

    def windows(x3, q, out_rows):
        size = out_rows * width
        return jnp.concatenate([x3[q, a * width : a * width + size] for a in range(3)], axis=1)

    wide_band = (rows + 2) * width

    def state_part(p):
        for q in range(per):
            e = p * per + q
            spread(r.hext[r.row_s[0, PLACE + e]], r.x3.at[q])
            r.gpre[e] = nn(windows(r.x3, q, rows + 2), r.wh[...].reshape(9 * 128, 256))

    loads[1].wait()
    for fill in filled:
        fill.wait()
    flip_row, flip_col = iota((2 * width, 2 * width), 0), iota((2 * width, 2 * width), 1)
    flip = one_hot(
        (flip_row // width == flip_col // width)
        & ((flip_row & (width - 1)) + (flip_col & (width - 1)) == width - 1)
    )

    def take_target(e, upto):
        value = r.feat[r.row_s[0, TARGET + e]]
        at = jnp.maximum(r.row_s[0, REL + e] - 1, 0)
        for s in range(upto + 1):
            value = jnp.where(r.row_s[0, GROUP + e] == s + 1, texts[s][at], value)
        for first in range(0, band, 2 * width):
            count = min(2 * width, band - first)
            r.text[e, pl.ds(FAR * width + first, count)] = nn(
                flip[0:count, 0:count], value[first : first + count]
            ).astype(BF)

    def take(s):
        feat_group(s).wait_recv()
        for q in range(per):
            take_target(s * per + q, s)
        txt.start(s)

    hid.received(0)
    each(slots // 2, state_part)
    take(0)
    each(slots - slots // 2, lambda p: state_part(p + slots // 2))
    src.received(0)

    own_row.wait()
    cam_cols = frames * 6
    cam_rows = r.where_v.shape[1] - cam_cols
    part = iota((cam_rows + cam_cols, 128), 0)
    index = jnp.where(part < cam_rows, part + tile * cam_rows, part - cam_rows + me * cam_cols)
    inside = lane & 15
    digit = jnp.where(inside < 6, inside, inside - 6)

    def place(j):
        spots = jnp.full((1, 128), -1, jnp.int32)
        for e in range(edges):
            source = (j * frames + r.meta_s[j, 0, SOURCE + e]) * 6
            target = (r.meta_s[j, 0, OWNER + e] * frames + r.meta_s[j, 0, TARGET + e]) * 6
            here = jnp.where(inside < 6, source, target) + digit
            spots = jnp.where(((lane >> 4) == e) & (inside < 12), here, spots)
        r.where_v[j] = one_hot(index == spots)

    each(n_edge, place)
    tables = pltpu.make_async_copy(r.where_v, r.where_h, r.l_meta)
    tables.start()

    lane_w = (iota((width, 128), 1) + 4) & 127
    col_w = iota((width, 128), 0) + RADIUS - (lane_w & 7)
    in_map = (col_w >= 0) & (col_w < width) & ((lane_w & 7) < WINDOW)
    scaled = [
        jnp.where(in_map & (((lane_w >> 5) & 1) == par), 128.0 ** (-0.5), 0.0) for par in range(2)
    ]
    slot_w = (lane_w >> 3) & 3
    pairs_of = (rows + 2 * NEAR + 1) // 2
    quads_of = r.text.shape[1] // (4 * width)
    used_rows = (rows + 2 * NEAR) * width

    def motion_of(e, q):
        tables, starts = [], []
        for m in range(quads_of):
            first, last = max(0, 2 * m - 3), min(pairs_of - 1, 2 * m + 1)
            starts.append(first)
            tables.append(
                nt(
                    r.sext[e, pl.ds(2 * first * width, 2 * (last - first + 1) * width)],
                    r.text[e, pl.ds(4 * m * width, 4 * width)],
                )
            )
        lines = []
        for k in range(pairs_of):
            for par in range(2):
                found = None
                for g in range(4):
                    m, h = divmod(k + g, 2)
                    at = (2 * (k - starts[m]) + par) * width
                    piece = tables[m][at : at + width, h * 128 : (h + 1) * 128]
                    moved = pltpu.roll(
                        piece, width + 8 * g + 32 * par, 1, stride=1, stride_axis=0
                    )
                    found = moved if g == 0 else jnp.where(slot_w == g, moved, found)
                lines.append((found * scaled[par]).astype(BF))
        value = nn(jnp.concatenate(lines, axis=0), r.corr_w[...])
        spread(jnp.maximum(value[0:used_rows], 0.0), r.x3.at[q])

    def update(p):
        txt.received(p)
        for q in range(per):
            motion_of(p * per + q, q)
            e = p * per + q
            before = r.gpre[e] + nn(windows(r.x3, q, rows + 2), r.wm[...].reshape(9 * 128, 256))
            r.upd[q] = 0.5 * jnp.tanh(0.5 * before[width : width + band, 0:128]) + 0.5
            reset = 0.5 * jnp.tanh(0.5 * before[:, 128:256]) + 0.5
            state = r.hext[r.row_s[0, PLACE + e], pl.ds(width, wide_band)].astype(F32)
            r.rext[q] = (reset * state).astype(BF)
        for q in range(per):
            e = p * per + q
            part = nn(
                jnp.concatenate(
                    [r.rext[q, a * width : a * width + band] for a in range(3)]
                    + [
                        r.x3[q, (a + 1) * width : (a + 1) * width + band, 128:256]
                        for a in range(3)
                    ],
                    axis=1,
                ),
                r.wc[...].reshape(6 * 128, 384),
            )
            candidate = jnp.tanh(
                nudge(part[:, 0:128], 1) + part[:, 128:256] + nudge(part[:, 256:384], -1)
            )
            gate = r.upd[q]
            place = r.row_s[0, PLACE + e]
            state = r.hext[place, pl.ds(NEAR * width, band)]
            fresh = ((1.0 - gate) * state.astype(F32) + gate * candidate).astype(BF)
            used = (place < r.count_s[0]).astype(F32)
            live = jnp.full((band, 128), used) > 0.5
            r.held[e] = jnp.where(live, fresh, state)
            heads = nt(r.head_w[...], fresh)
            jac = heads[0:32]
            weighted = jac * jax.nn.softplus(heads[32:64])
            at16 = pl.ds(pl.multiple_of(e * 16, 16), 16)
            r.jall[at16] = jnp.concatenate([jac[0:16], jac[16:32]], axis=1).astype(BF)
            r.wall[at16] = jnp.concatenate([weighted[0:16], weighted[16:32]], axis=1).astype(BF)

    def stage(p):
        for s in range(1, slots):

            @pl.when(p == s - 1)
            def _():
                take(s)

        update(p)

    each(slots, stage)
    same = (iota((128, 128), 0) >> 4) == (iota((128, 128), 1) >> 4)
    square = jnp.where(same, nt(r.wall[...], r.jall[...]), 0.0)
    blocks = square[0:16]
    for e in range(1, edges):
        blocks = blocks + square[e * 16 : (e + 1) * 16]
    blocks = blocks * (1.0 / (MAPH * width))
    of = iota((16, 128), 1) >> 4
    for e in range(edges):
        used = (r.row_s[0, PLACE + e] < r.count_s[0]).astype(jnp.int32)
        blocks = jnp.where((of == e) & (jnp.full((16, 128), used) == 0), 0.0, blocks)
    r.gpart[...] = blocks

    def tile_copy(rel):
        return remote(
            r.gpart, r.gtile.at[tile], r.s_gt, r.r_gt, me, (tile + rel) % n_tile
        )

    def all_tiles():
        some = r.gtile.at[pl.ds(0, n_tile - 1)]
        return remote(some, some, r.s_gt, r.r_gt, me, (tile + 1) % n_tile)

    for rel in range(1, n_tile):
        tile_copy(rel).start()
    r.gtile[tile] = r.gpart[...]

    def put_back(e):
        r.ready[e] = r.held[r.row_s[0, SPOT + e]]

    each(edges, put_back)
    store = pltpu.make_async_copy(r.ready, r.out_hidden, r.l_out)
    store.start()
    all_tiles().wait_recv()
    total = r.gtile[0]
    for k in range(1, n_tile):
        total = total + r.gtile[k]
    r.gsum[...] = total

    def edge_copy(rel):
        return remote(r.gsum, r.gall_h.at[me], r.s_ge, r.r_ge, (me + rel) % n_edge, tile)

    def all_edges():
        some = r.gall_h.at[pl.ds(0, others)]
        return remote(some, some, r.s_ge, r.r_ge, (me + 1) % n_edge, tile)

    for rel in range(1, n_edge):
        edge_copy(rel).start()
    own_sum = pltpu.make_async_copy(r.gsum, r.gall_h.at[me], r.l_sum)
    own_sum.start()
    all_edges().wait_recv()

    own_sum.wait()
    store.wait()
    tables.wait()
    for rel in range(1, n_edge):
        meta_copy(rel).wait_send()
    for s in range(slots):
        feat_group(s).wait_send()
    all_tiles().wait_send()
    all_edges().wait_send()
    for halo in (hid, src, txt):
        halo.sent()


def halves(value):
    high = value.astype(BF)
    return high, (value - high.astype(F32)).astype(BF)


def assemble(
    dims, where_h, gall_h, hidden_h, out_hidden, cam_h, diag_h, where_v, gall, out_cam, out_diag, held,
    sem, held_sem,
):
    n_edge, n_tile, edges, frames, rows, width, slots = dims
    me = lax.axis_index("edge")
    tile = lax.axis_index("tile")
    loads = [
        pltpu.make_async_copy(gall_h, gall, sem.at[0]),
        pltpu.make_async_copy(where_h, where_v, sem.at[1]),
    ]
    pieces = [pl.ds(i * (edges // PIECES), edges // PIECES) for i in range(PIECES)]
    fetches = [
        pltpu.make_async_copy(hidden_h.at[p], held.at[p], held_sem.at[i])
        for i, p in enumerate(pieces)
    ]
    stores = [
        pltpu.make_async_copy(held.at[p], out_hidden.at[p], held_sem.at[i])
        for i, p in enumerate(pieces)
    ]
    for load in loads + fetches:
        load.start()
    cam_rows, cam_cols = out_cam.shape
    same = (iota((128, 128), 0) >> 4) == (iota((128, 128), 1) >> 4)
    for load in loads:
        load.wait()
    for fetch, store in zip(fetches, stores):
        fetch.wait()
        store.start()
    lefts, lows, rights = [], [], []
    for j in range(n_edge):
        left = where_v[j]
        stack = jnp.where(same, jnp.concatenate([gall[j]] * 8, axis=0), 0.0)
        picked = nn(
            jnp.concatenate([left, left], axis=1), jnp.concatenate(halves(stack), axis=0)
        )
        high, low = halves(picked)
        lefts.append(high)
        lows.append(low)
        rights.append(left[cam_rows:])
    placed = nt(jnp.concatenate(lefts + lows, axis=1), jnp.concatenate(rights + rights, axis=1))
    cam = placed[0:cam_rows]
    row_frame = sixth(iota((cam_rows, cam_cols), 0) + tile * cam_rows)
    col_frame = sixth(iota((cam_rows, cam_cols), 1) + me * cam_cols)
    out_cam[...] = jnp.where(row_frame == col_frame, 0.0, cam)
    cam_store = pltpu.make_async_copy(out_cam, cam_h, sem.at[0])
    cam_store.start()
    own = placed[cam_rows:]
    own_row = sixth(iota((cam_cols, cam_cols), 0))
    own_col = sixth(iota((cam_cols, cam_cols), 1))
    own = jnp.where(own_row == own_col, own, 0.0)
    wide_row = iota((cam_cols, 128), 0)
    wide_lane = iota((cam_cols, 128), 1)
    row_in = wide_row.astype(F32) - 6.0 * sixth(wide_row)
    lane_of = sixth(wide_lane)
    lane_in = wide_lane.astype(F32) - 6.0 * lane_of
    gather = one_hot(row_in == lane_in)
    high, low = halves(own)
    spread = jnp.where(row_in == lane_of, nn(high, gather) + nn(low, gather), 0.0)
    fold = one_hot(
        sixth(iota((frames, cam_cols), 1)) == iota((frames, cam_cols), 0).astype(F32)
    )
    high, low = halves(spread)
    out_diag[...] = (nn(fold, high) + nn(fold, low))[:, 0:36]
    diag_store = pltpu.make_async_copy(out_diag, diag_h, sem.at[1])
    diag_store.start()
    for store in stores + [cam_store, diag_store]:
        store.wait()


def per_device(
    features,
    hidden_state,
    edge_source,
    edge_owner,
    edge_target,
    edge_counts,
    corr_weight,
    gate_weight,
    candidate_weight,
    jacobian_weight,
    confidence_weight,
):
    n_edge, n_tile = lax.axis_size("edge"), lax.axis_size("tile")
    edges = hidden_state.shape[0]
    frames, rows, width, chan = features.shape
    slots = max(2, (2 * edges + n_edge - 1) // n_edge)
    assert edges % slots == 0 and edges <= 8 and ASKS + n_edge * slots <= 128
    per = edges // slots
    band = rows * width

    dims = (n_edge, n_tile, edges, frames, rows, width, slots)
    even = (rows + 2 * NEAR + 1) // 2 * 2
    dma = pltpu.SemaphoreType.DMA
    hbm = pl.BlockSpec(memory_space=pl.ANY)

    inputs = (
        ("owner_h", edge_owner[:, 0], hbm),
        ("target_h", edge_target, hbm),
        ("source_h", edge_source, hbm),
        ("count_h", edge_counts, hbm),
        ("feat_h", features.reshape(frames, band, chan), hbm),
        ("hidden_h", hidden_state.reshape(edges, band, chan), hbm),
        ("corr_h", corr_weight, hbm),
        ("gate_w", gate_weight, hbm),
        ("cand_w", candidate_weight, hbm),
        ("jac_h", jacobian_weight.T, hbm),
        ("conf_h", confidence_weight.T, hbm),
    )
    cam_rows, cam_cols = frames * n_edge * 6 // n_tile, frames * 6
    places = (n_edge, cam_rows + cam_cols, 128)
    outputs = (
        ("out_hidden", (edges, band, chan), BF, hbm),
        ("gall_h", (n_edge, 16, 128), F32, hbm),
        ("where_h", places, BF, hbm),
    )
    near, far = len(reach(NEAR, rows)), len(reach(FAR, rows))
    scratch = {
        "owner_s": pltpu.SMEM((edges,), jnp.int32),
        "target_s": pltpu.SMEM((edges,), jnp.int32),
        "source_s": pltpu.SMEM((edges,), jnp.int32),
        "count_s": pltpu.SMEM((1,), jnp.int32),
        "corr_in": pltpu.VMEM(corr_weight.shape, BF),
        "jac_in": pltpu.VMEM(jacobian_weight.shape[::-1], BF),
        "conf_in": pltpu.VMEM(confidence_weight.shape[::-1], BF),
        "row_v": pltpu.VMEM((1, 128), jnp.int32),
        "row_s": pltpu.SMEM((1, 128), jnp.int32),
        "meta_s": pltpu.SMEM((n_edge, 1, 128), jnp.int32),
        "feat": pltpu.VMEM((frames, band, chan), BF),
        "held": pltpu.VMEM((edges, band, chan), BF),
        "ready": pltpu.VMEM((edges, band, chan), BF),
        "where_v": pltpu.VMEM(places, BF),
        "send": pltpu.VMEM(((n_edge - 1) * slots, band, chan), BF),
        "text": pltpu.VMEM((edges, (even + 2 * RADIUS + 3) // 4 * 4 * width, chan), BF),
        "sext": pltpu.VMEM((edges, even * width, chan), BF),
        "hext": pltpu.VMEM((edges, (rows + 2 * NEAR) * width, chan), BF),
        "rext": pltpu.VMEM((per, (rows + 2) * width, chan), BF),
        "x3": pltpu.VMEM((per, (rows + 2 * NEAR) * width, 3 * chan), BF),
        "wh": pltpu.VMEM((3, 3, chan, 2 * chan), BF),
        "wm": pltpu.VMEM((3, 3, chan, 2 * chan), BF),
        "wc": pltpu.VMEM((2, 3, chan, 3 * chan), BF),
        "corr_w": pltpu.VMEM((128, chan), BF),
        "head_w": pltpu.VMEM((64, chan), BF),
        "gpre": pltpu.VMEM((edges, (rows + 2) * width, 2 * chan), F32),
        "upd": pltpu.VMEM((per, band, chan), F32),
        "jall": pltpu.VMEM((128, 2 * band), BF),
        "wall": pltpu.VMEM((128, 2 * band), BF),
        "gpart": pltpu.VMEM((16, 128), F32),
        "gtile": pltpu.VMEM((n_tile, 16, 128), F32),
        "gsum": pltpu.VMEM((16, 128), F32),
        "l_in": dma((5,)),
        "l_w": dma((3,)),
        "l_ints": dma((4,)),
        "l_row": dma,
        "l_meta": dma,
        "l_own": dma,
        "l_sum": dma,
        "l_out": dma,
        "s_meta": dma((n_edge - 1,)),
        "r_meta": dma((n_edge - 1,)),
        "s_feat": dma,
        "r_feat": dma((slots,)),
        "s_gt": dma,
        "r_gt": dma,
        "s_ge": dma,
        "r_ge": dma,
    }
    for s in range(slots):
        scratch[f"text{s}"] = pltpu.VMEM((n_edge - 1, band, chan), BF)
    for key, count, lots in (("h", near, 1), ("s", near, 1), ("t", far, slots)):
        for way in ("up", "dn"):
            scratch[f"s_{key}{way}"] = dma((count,))
            scratch[f"r_{key}{way}"] = dma((count, lots))
    names = [i[0] for i in inputs] + [o[0] for o in outputs] + list(scratch)
    state, gall, where = pl.pallas_call(
        functools.partial(kernel, dims, names),
        out_shape=tuple(jax.ShapeDtypeStruct(shape, kind) for _, shape, kind, _ in outputs),
        in_specs=[spec for _, _, spec in inputs],
        out_specs=tuple(spec for _, _, _, spec in outputs),
        scratch_shapes=list(scratch.values()),
        compiler_params=pltpu.CompilerParams(
            collective_id=0, has_side_effects=True, vmem_limit_bytes=56 * 1024 * 1024
        ),
    )(*[value for _, value, _ in inputs])
    hidden_next, cam, diag = pl.pallas_call(
        functools.partial(assemble, dims),
        out_shape=(
            jax.ShapeDtypeStruct((edges, band, chan), BF),
            jax.ShapeDtypeStruct((cam_rows, cam_cols), F32),
            jax.ShapeDtypeStruct((frames, 36), F32),
        ),
        in_specs=[hbm] * 3,
        out_specs=(hbm,) * 3,
        scratch_shapes=[
            pltpu.VMEM(places, BF),
            pltpu.VMEM((n_edge, 16, 128), F32),
            pltpu.VMEM((cam_rows, cam_cols), F32),
            pltpu.VMEM((frames, 36), F32),
            pltpu.VMEM((edges, band, chan), BF),
            dma((2,)),
            dma((PIECES,)),
        ],
    )(where, gall, state)
    return hidden_next.reshape(hidden_state.shape), cam, diag


def solution(mesh):
    placed = (
        P("edge", "tile", None, None),
        P("edge", "tile", None, None),
        P("edge"),
        P("edge", None),
        P("edge"),
        P("edge"),
        P(),
        P(),
        P(),
        P(),
        P(),
    )
    return jax.shard_map(
        per_device,
        mesh=mesh,
        in_specs=placed,
        out_specs=(P("edge", "tile", None, None), P("tile", "edge"), P("edge", None)),
        check_vma=False,
    )
```

```python
import functools
import types

import jax
import jax.numpy as jnp
from jax import lax
from jax.experimental import pallas as pl
from jax.experimental.pallas import tpu as pltpu
from jax.sharding import PartitionSpec as P

MAPH = 48
WINDOW = 7
RADIUS = WINDOW // 2
NEAR = 2
FAR = RADIUS + NEAR
OWNER, TARGET, SOURCE, SPOT, PLACE, GROUP, REL, ASKS = 0, 8, 16, 24, 32, 40, 48, 64
PIECES = 4
MESH = pl.DeviceIdType.MESH
BF = jnp.bfloat16
F32 = jnp.float32


def nt(a, b):
    return lax.dot_general(a, b, (((1,), (1,)), ((), ())), preferred_element_type=F32)


def nn(a, b):
    return lax.dot_general(a, b, (((1,), (0,)), ((), ())), preferred_element_type=F32)


def iota(shape, dim):
    return lax.broadcasted_iota(jnp.int32, shape, dim)


def sixth(index):
    return jnp.floor((index.astype(F32) + 0.5) * (1.0 / 6.0))


def one_hot(cond):
    return cond.astype(F32).astype(BF)


def each(count, body):
    def step(i, carry):
        body(i)
        return carry

    lax.fori_loop(0, count, step, 0)


def reach(halo, rows):
    return [min(rows, halo - d * rows) for d in range((halo + rows - 1) // rows)]


def kernel(dims, names, *refs):
    n_edge, n_tile, edges, frames, rows, width, slots = dims
    r = types.SimpleNamespace(**dict(zip(names, refs)))
    band = rows * width
    per = edges // slots
    me = lax.axis_index("edge")
    tile = lax.axis_index("tile")
    texts = [getattr(r, f"text{s}") for s in range(slots)]

    ints = [
        pltpu.make_async_copy(r.owner_h, r.owner_s, r.l_ints.at[0]),
        pltpu.make_async_copy(r.target_h, r.target_s, r.l_ints.at[1]),
        pltpu.make_async_copy(r.source_h, r.source_s, r.l_ints.at[2]),
        pltpu.make_async_copy(r.count_h, r.count_s, r.l_ints.at[3]),
    ]
    loads = [
        pltpu.make_async_copy(r.feat_h, r.feat, r.l_in.at[0]),
        pltpu.make_async_copy(
            r.hidden_h, r.hext.at[:, pl.ds(NEAR * width, band)], r.l_in.at[1]
        ),
        pltpu.make_async_copy(r.corr_h, r.corr_in, r.l_in.at[2]),
        pltpu.make_async_copy(r.jac_h, r.jac_in, r.l_in.at[3]),
        pltpu.make_async_copy(r.conf_h, r.conf_in, r.l_in.at[4]),
    ]
    first, second = pl.ds(0, 128), pl.ds(128, 128)
    fills = [
        pltpu.make_async_copy(r.gate_w.at[:, :, first], r.wh, r.l_w.at[0]),
        pltpu.make_async_copy(r.gate_w.at[:, :, second], r.wm, r.l_w.at[1]),
    ]
    for part, at in enumerate((first, second)):
        for b in range(3):
            fills.append(
                pltpu.make_async_copy(
                    r.cand_w.at[:, b, at], r.wc.at[part, :, :, pl.ds(b * 128, 128)], r.l_w.at[2]
                )
            )
    filled = fills[:2] + [pltpu.make_async_copy(r.wc, r.wc, r.l_w.at[2])]
    for load in ints:
        load.start()

    barrier = pltpu.get_barrier_semaphore()
    for rel in range(1, n_edge):
        pl.semaphore_signal(
            barrier, inc=1, device_id=((me + rel) % n_edge, tile), device_id_type=MESH
        )
    for rel in range(1, n_tile):
        pl.semaphore_signal(
            barrier, inc=1, device_id=(me, (tile + rel) % n_tile), device_id_type=MESH
        )

    for load in loads + fills:
        load.start()

    for load in ints:
        load.wait()
    owner = [r.owner_s[e] for e in range(edges)]
    rel_of = [(owner[e] - me + n_edge) % n_edge for e in range(edges)]
    rank, group = [], []
    for e in range(edges):
        before = jnp.int32(0)
        for k in range(e):
            before = before + (owner[k] == owner[e]).astype(jnp.int32)
        rank.append(jnp.minimum(before, slots - 1))
        group.append(jnp.where(rel_of[e] == 0, 0, rank[e] + 1))
    lane = iota((1, 128), 1)
    row = jnp.zeros((1, 128), jnp.int32)
    for e in range(edges):
        spot = jnp.int32(0)
        for k in range(edges):
            if k < e:
                spot = spot + (group[k] <= group[e]).astype(jnp.int32)
            elif k > e:
                spot = spot + (group[k] < group[e]).astype(jnp.int32)
        goal = r.target_s[e]
        fields = (
            (OWNER, owner[e]),
            (TARGET, goal),
            (SOURCE, r.source_s[e]),
            (PLACE, jnp.int32(e)),
            (GROUP, group[e]),
            (REL, rel_of[e]),
        )
        for base, value in fields:
            row = jnp.where(lane == base + spot, value, row)
        row = jnp.where(lane == SPOT + e, spot, row)
        row = jnp.where(lane == ASKS + rel_of[e] * slots + rank[e], goal, row)
    r.row_v[...] = row
    mine = pltpu.make_async_copy(r.row_v, r.row_s, r.l_row)
    mine.start()

    pl.semaphore_wait(barrier, n_edge + n_tile - 2)

    def remote(src, dst, send_sem, recv_sem, edge_id, tile_id):
        return pltpu.make_async_remote_copy(
            src_ref=src,
            dst_ref=dst,
            send_sem=send_sem,
            recv_sem=recv_sem,
            device_id=(edge_id, tile_id),
            device_id_type=MESH,
        )

    def meta_copy(rel):
        return remote(
            r.row_v, r.meta_s.at[me], r.s_meta.at[rel - 1], r.r_meta.at[rel - 1],
            (me + rel) % n_edge, tile,
        )

    others = n_edge - 1
    for rel in range(1, n_edge):
        meta_copy(rel).start()
    own_row = pltpu.make_async_copy(r.row_v, r.meta_s.at[me], r.l_own)
    own_row.start()

    class Halo:
        def __init__(self, halo, lot, buf, source, sems):
            self.halo, self.lot, self.buf, self.source, self.sems = halo, lot, buf, source, sems
            self.counts = reach(halo, rows)

        def copies(self, i, lot):
            which = pl.ds(i * lot, lot)
            for d, count in enumerate(self.counts):
                far, lines = d + 1, count * width
                s_up, r_up, s_dn, r_dn = self.sems
                up = remote(
                    self.source(which, 0, lines),
                    self.buf.at[which, pl.ds((self.halo + far * rows) * width, lines)],
                    s_up.at[d], r_up.at[d, i], me, tile - far,
                )
                dn = remote(
                    self.source(which, band - lines, lines),
                    self.buf.at[which, pl.ds((self.halo - d * rows - count) * width, lines)],
                    s_dn.at[d], r_dn.at[d, i], me, tile + far,
                )
                yield tile >= far, tile + far < n_tile, up, dn

        def start(self, i):
            for above, below, up, dn in self.copies(i, self.lot):
                pl.when(above)(up.start)
                pl.when(below)(dn.start)

        def received(self, i):
            for above, below, up, dn in self.copies(i, self.lot):
                pl.when(below)(up.wait_recv)
                pl.when(above)(dn.wait_recv)

        def sent(self):
            for above, below, up, dn in self.copies(0, edges):
                pl.when(above)(up.wait_send)
                pl.when(below)(dn.wait_send)

        def clear(self):
            for d, count in enumerate(self.counts):
                far, lines = d + 1, count * width
                zero = jnp.zeros((lines, 128), BF)
                top = (self.halo - d * rows - count) * width
                low = (self.halo + far * rows) * width

                @pl.when(tile < far)
                def _():
                    def clear_top(e):
                        self.buf[e, pl.ds(top, lines)] = zero

                    each(edges, clear_top)

                @pl.when(tile + far >= n_tile)
                def _():
                    def clear_low(e):
                        self.buf[e, pl.ds(low, lines)] = zero

                    each(edges, clear_low)

            used = (rows + 2 * self.halo) * width
            spare = self.buf.shape[1] - used
            if spare:

                def clear_pad(e):
                    self.buf[e, pl.ds(used, spare)] = jnp.zeros((spare, 128), BF)

                each(edges, clear_pad)

    def inner(buf, halo):
        return lambda which, at, lines: buf.at[which, pl.ds(halo * width + at, lines)]

    hid = Halo(
        NEAR, edges, r.hext, lambda which, at, lines: r.hidden_h.at[which, pl.ds(at, lines)],
        (r.s_hup, r.r_hup, r.s_hdn, r.r_hdn),
    )
    src = Halo(
        NEAR, edges, r.sext, inner(r.sext, NEAR), (r.s_sup, r.r_sup, r.s_sdn, r.r_sdn)
    )
    txt = Halo(FAR, per, r.text, inner(r.text, FAR), (r.s_tup, r.r_tup, r.s_tdn, r.r_tdn))

    loads[0].wait()

    turns = [n_edge // 2]
    turns += [n_edge - k - (n_edge - 2 * k) * (me % 2) for k in range(1, (n_edge + 1) // 2)]
    turns += [k + (n_edge - 2 * k) * (me % 2) for k in range(1, (n_edge + 1) // 2)]

    def feat_copy(rel, s):
        return remote(
            r.send.at[s * others + rel - 1], texts[s].at[rel - 1],
            r.s_feat, r.r_feat.at[s], (me - rel + n_edge) % n_edge, tile,
        )

    def feat_group(s):
        return remote(
            r.send.at[pl.ds(s * others, others)], texts[s],
            r.s_feat, r.r_feat.at[s], (me + 1) % n_edge, tile,
        )

    for s in range(slots):
        for rel in turns:
            peer = (me - rel + n_edge) % n_edge
            if s == 0:
                remote(
                    r.row_v, r.meta_s.at[peer], r.s_meta.at[rel - 1], r.r_meta.at[rel - 1],
                    (me + rel) % n_edge, tile,
                ).wait_recv()
            r.send[s * others + rel - 1] = r.feat[r.meta_s[peer, 0, ASKS + rel * slots + s]]
            feat_copy(rel, s).start()

    hid.start(0)
    mine.wait()

    def take_source(e):
        r.sext[e, pl.ds(NEAR * width, band)] = r.feat[r.row_s[0, SOURCE + e]]

    each(edges, take_source)
    src.start(0)
    for halo in (hid, src, txt):
        halo.clear()

    for load in loads[2:]:
        load.wait()

    spot = (iota((128, 64), 0) + 4) & 127
    along = ((spot >> 3) & 3) * 2 + (spot >> 6) - ((spot >> 5) & 1)
    across = WINDOW - 1 - (spot & 7)
    fits = (across >= 0) & (along >= 0) & (along < WINDOW)
    pick = (iota((128, 64), 1) == along * WINDOW + across) & fits
    lookup = jnp.concatenate(
        [r.corr_in[...].astype(F32), jnp.zeros((64 - WINDOW * WINDOW, 128), F32)], axis=0
    ).astype(BF)
    r.corr_w[...] = nn(one_hot(pick), lookup).astype(BF)

    place12 = iota((32, 64), 0)
    which = place12 >> 4
    within = place12 & 15
    name12 = iota((32, 64), 1)
    pick_j = (within < 12) & (name12 == which * 12 + within)
    padded_jac = jnp.concatenate(
        [r.jac_in[...].astype(F32), jnp.zeros((40, 128), F32)], axis=0
    ).astype(BF)
    conf_wide = r.conf_in[...].astype(F32)
    tall = iota((32, 128), 0)
    conf_rows = jnp.where(
        tall < 16,
        jnp.broadcast_to(conf_wide[0:1], (32, 128)),
        jnp.broadcast_to(conf_wide[1:2], (32, 128)),
    )
    r.head_w[...] = jnp.concatenate(
        [nn(one_hot(pick_j), padded_jac), jnp.where((tall & 15) < 12, conf_rows, 0.0)], axis=0
    ).astype(BF)

    def nudge(wide, by):
        lines = wide.shape[0]
        column = iota((lines, 128), 0) & (width - 1)
        edge = 0 if by == 1 else width - 1
        return jnp.where(column == edge, 0.0, pltpu.roll(wide, by % lines, 0))

    def spread(value, out):
        lines = value.shape[0]
        wide = value.astype(F32)
        out[0:lines, 0:128] = nudge(wide, 1).astype(BF)
        out[0:lines, 128:256] = value.astype(BF)
        out[0:lines, 256:384] = nudge(wide, -1).astype(BF)

    def windows(x3, q, out_rows):
        size = out_rows * width
        return jnp.concatenate([x3[q, a * width : a * width + size] for a in range(3)], axis=1)

    wide_band = (rows + 2) * width

    def state_part(p):
        for q in range(per):
            e = p * per + q
            spread(r.hext[r.row_s[0, PLACE + e]], r.x3.at[q])
            r.gpre[e] = nn(windows(r.x3, q, rows + 2), r.wh[...].reshape(9 * 128, 256))

    loads[1].wait()
    for fill in filled:
        fill.wait()
    flip_row, flip_col = iota((2 * width, 2 * width), 0), iota((2 * width, 2 * width), 1)
    flip = one_hot(
        (flip_row // width == flip_col // width)
        & ((flip_row & (width - 1)) + (flip_col & (width - 1)) == width - 1)
    )

    def take_target(e, upto):
        value = r.feat[r.row_s[0, TARGET + e]]
        at = jnp.maximum(r.row_s[0, REL + e] - 1, 0)
        for s in range(upto + 1):
            value = jnp.where(r.row_s[0, GROUP + e] == s + 1, texts[s][at], value)
        for first in range(0, band, 2 * width):
            count = min(2 * width, band - first)
            r.text[e, pl.ds(FAR * width + first, count)] = nn(
                flip[0:count, 0:count], value[first : first + count]
            ).astype(BF)

    def take(s):
        feat_group(s).wait_recv()
        for q in range(per):
            take_target(s * per + q, s)
        txt.start(s)

    hid.received(0)
    each(slots // 2, state_part)
    take(0)
    each(slots - slots // 2, lambda p: state_part(p + slots // 2))
    src.received(0)

    own_row.wait()
    cam_cols = frames * 6
    cam_rows = r.where_v.shape[1] - cam_cols
    part = iota((cam_rows + cam_cols, 128), 0)
    index = jnp.where(part < cam_rows, part + tile * cam_rows, part - cam_rows + me * cam_cols)
    inside = lane & 15
    digit = jnp.where(inside < 6, inside, inside - 6)

    def place(j):
        spots = jnp.full((1, 128), -1, jnp.int32)
        for e in range(edges):
            source = (j * frames + r.meta_s[j, 0, SOURCE + e]) * 6
            target = (r.meta_s[j, 0, OWNER + e] * frames + r.meta_s[j, 0, TARGET + e]) * 6
            here = jnp.where(inside < 6, source, target) + digit
            spots = jnp.where(((lane >> 4) == e) & (inside < 12), here, spots)
        r.where_v[j] = one_hot(index == spots)

    each(n_edge, place)
    tables = pltpu.make_async_copy(r.where_v, r.where_h, r.l_meta)
    tables.start()

    lane_w = (iota((width, 128), 1) + 4) & 127
    col_w = iota((width, 128), 0) + RADIUS - (lane_w & 7)
    in_map = (col_w >= 0) & (col_w < width) & ((lane_w & 7) < WINDOW)
    scaled = [
        jnp.where(in_map & (((lane_w >> 5) & 1) == par), 128.0 ** (-0.5), 0.0) for par in range(2)
    ]
    slot_w = (lane_w >> 3) & 3
    pairs_of = (rows + 2 * NEAR + 1) // 2
    quads_of = r.text.shape[1] // (4 * width)
    used_rows = (rows + 2 * NEAR) * width

    def motion_of(e, q):
        tables, starts = [], []
        for m in range(quads_of):
            first, last = max(0, 2 * m - 3), min(pairs_of - 1, 2 * m + 1)
            starts.append(first)
            tables.append(
                nt(
                    r.sext[e, pl.ds(2 * first * width, 2 * (last - first + 1) * width)],
                    r.text[e, pl.ds(4 * m * width, 4 * width)],
                )
            )
        lines = []
        for k in range(pairs_of):
            for par in range(2):
                found = None
                for g in range(4):
                    m, h = divmod(k + g, 2)
                    at = (2 * (k - starts[m]) + par) * width
                    piece = tables[m][at : at + width, h * 128 : (h + 1) * 128]
                    moved = pltpu.roll(
                        piece, width + 8 * g + 32 * par, 1, stride=1, stride_axis=0
                    )
                    found = moved if g == 0 else jnp.where(slot_w == g, moved, found)
                lines.append((found * scaled[par]).astype(BF))
        value = nn(jnp.concatenate(lines, axis=0), r.corr_w[...])
        spread(jnp.maximum(value[0:used_rows], 0.0), r.x3.at[q])

    def update(p):
        txt.received(p)
        for q in range(per):
            motion_of(p * per + q, q)
        for q in range(per):
            e = p * per + q
            before = r.gpre[e] + nn(windows(r.x3, q, rows + 2), r.wm[...].reshape(9 * 128, 256))
            r.upd[q] = 0.5 * jnp.tanh(0.5 * before[width : width + band, 0:128]) + 0.5
            reset = 0.5 * jnp.tanh(0.5 * before[:, 128:256]) + 0.5
            state = r.hext[r.row_s[0, PLACE + e], pl.ds(width, wide_band)].astype(F32)
            r.rext[q] = (reset * state).astype(BF)
        for q in range(per):
            e = p * per + q
            part = nn(
                jnp.concatenate(
                    [r.rext[q, a * width : a * width + band] for a in range(3)]
                    + [
                        r.x3[q, (a + 1) * width : (a + 1) * width + band, 128:256]
                        for a in range(3)
                    ],
                    axis=1,
                ),
                r.wc[...].reshape(6 * 128, 384),
            )
            candidate = jnp.tanh(
                nudge(part[:, 0:128], 1) + part[:, 128:256] + nudge(part[:, 256:384], -1)
            )
            gate = r.upd[q]
            place = r.row_s[0, PLACE + e]
            state = r.hext[place, pl.ds(NEAR * width, band)]
            fresh = ((1.0 - gate) * state.astype(F32) + gate * candidate).astype(BF)
            used = (place < r.count_s[0]).astype(F32)
            live = jnp.full((band, 128), used) > 0.5
            r.held[e] = jnp.where(live, fresh, state)
            heads = nt(r.head_w[...], fresh)
            jac = heads[0:32]
            weighted = jac * jax.nn.softplus(heads[32:64])
            at16 = pl.ds(pl.multiple_of(e * 16, 16), 16)
            r.jall[at16] = jnp.concatenate([jac[0:16], jac[16:32]], axis=1).astype(BF)
            r.wall[at16] = jnp.concatenate([weighted[0:16], weighted[16:32]], axis=1).astype(BF)

    def stage(p):
        for s in range(1, slots):

            @pl.when(p == s - 1)
            def _():
                take(s)

        update(p)

    each(slots, stage)
    same = (iota((128, 128), 0) >> 4) == (iota((128, 128), 1) >> 4)
    square = jnp.where(same, nt(r.wall[...], r.jall[...]), 0.0)
    blocks = square[0:16]
    for e in range(1, edges):
        blocks = blocks + square[e * 16 : (e + 1) * 16]
    blocks = blocks * (1.0 / (MAPH * width))
    of = iota((16, 128), 1) >> 4
    for e in range(edges):
        used = (r.row_s[0, PLACE + e] < r.count_s[0]).astype(jnp.int32)
        blocks = jnp.where((of == e) & (jnp.full((16, 128), used) == 0), 0.0, blocks)
    r.gpart[...] = blocks.astype(BF)

    def tile_copy(rel):
        return remote(
            r.gpart, r.gtile.at[tile], r.s_gt, r.r_gt, me, (tile + rel) % n_tile
        )

    def all_tiles():
        some = r.gtile.at[pl.ds(0, n_tile - 1)]
        return remote(some, some, r.s_gt, r.r_gt, me, (tile + 1) % n_tile)

    for rel in range(1, n_tile):
        tile_copy(rel).start()
    r.gtile[tile] = r.gpart[...]

    def put_back(e):
        r.ready[e] = r.held[r.row_s[0, SPOT + e]]

    each(edges, put_back)
    store = pltpu.make_async_copy(r.ready, r.out_hidden, r.l_out)
    store.start()
    all_tiles().wait_recv()
    total = r.gtile[0].astype(F32)
    for k in range(1, n_tile):
        total = total + r.gtile[k].astype(F32)
    r.gsum[...] = total

    def edge_copy(rel):
        return remote(r.gsum, r.gall_h.at[me], r.s_ge, r.r_ge, (me + rel) % n_edge, tile)

    def all_edges():
        some = r.gall_h.at[pl.ds(0, others)]
        return remote(some, some, r.s_ge, r.r_ge, (me + 1) % n_edge, tile)

    for rel in range(1, n_edge):
        edge_copy(rel).start()
    own_sum = pltpu.make_async_copy(r.gsum, r.gall_h.at[me], r.l_sum)
    own_sum.start()
    all_edges().wait_recv()

    own_sum.wait()
    store.wait()
    tables.wait()
    for rel in range(1, n_edge):
        meta_copy(rel).wait_send()
    for s in range(slots):
        feat_group(s).wait_send()
    all_tiles().wait_send()
    all_edges().wait_send()
    for halo in (hid, src, txt):
        halo.sent()


def halves(value):
    high = value.astype(BF)
    return high, (value - high.astype(F32)).astype(BF)


def assemble(
    dims, where_h, gall_h, hidden_h, out_hidden, cam_h, diag_h, where_v, gall, out_cam, out_diag, held,
    sem, held_sem,
):
    n_edge, n_tile, edges, frames, rows, width, slots = dims
    me = lax.axis_index("edge")
    tile = lax.axis_index("tile")
    loads = [
        pltpu.make_async_copy(gall_h, gall, sem.at[0]),
        pltpu.make_async_copy(where_h, where_v, sem.at[1]),
    ]
    pieces = [pl.ds(i * (edges // PIECES), edges // PIECES) for i in range(PIECES)]
    fetches = [
        pltpu.make_async_copy(hidden_h.at[p], held.at[p], held_sem.at[i])
        for i, p in enumerate(pieces)
    ]
    stores = [
        pltpu.make_async_copy(held.at[p], out_hidden.at[p], held_sem.at[i])
        for i, p in enumerate(pieces)
    ]
    for load in loads + fetches:
        load.start()
    cam_rows, cam_cols = out_cam.shape
    same = (iota((128, 128), 0) >> 4) == (iota((128, 128), 1) >> 4)
    for load in loads:
        load.wait()
    for fetch, store in zip(fetches, stores):
        fetch.wait()
        store.start()
    lefts, lows, rights = [], [], []
    for j in range(n_edge):
        left = where_v[j]
        stack = jnp.where(same, jnp.concatenate([gall[j]] * 8, axis=0), 0.0)
        picked = nn(
            jnp.concatenate([left, left], axis=1), jnp.concatenate(halves(stack), axis=0)
        )
        high, low = halves(picked)
        lefts.append(high)
        lows.append(low)
        rights.append(left[cam_rows:])
    placed = nt(jnp.concatenate(lefts + lows, axis=1), jnp.concatenate(rights + rights, axis=1))
    cam = placed[0:cam_rows]
    row_frame = sixth(iota((cam_rows, cam_cols), 0) + tile * cam_rows)
    col_frame = sixth(iota((cam_rows, cam_cols), 1) + me * cam_cols)
    out_cam[...] = jnp.where(row_frame == col_frame, 0.0, cam)
    cam_store = pltpu.make_async_copy(out_cam, cam_h, sem.at[0])
    cam_store.start()
    own = placed[cam_rows:]
    own_row = sixth(iota((cam_cols, cam_cols), 0))
    own_col = sixth(iota((cam_cols, cam_cols), 1))
    own = jnp.where(own_row == own_col, own, 0.0)
    wide_row = iota((cam_cols, 128), 0)
    wide_lane = iota((cam_cols, 128), 1)
    row_in = wide_row.astype(F32) - 6.0 * sixth(wide_row)
    lane_of = sixth(wide_lane)
    lane_in = wide_lane.astype(F32) - 6.0 * lane_of
    gather = one_hot(row_in == lane_in)
    high, low = halves(own)
    spread = jnp.where(row_in == lane_of, nn(high, gather) + nn(low, gather), 0.0)
    fold = one_hot(
        sixth(iota((frames, cam_cols), 1)) == iota((frames, cam_cols), 0).astype(F32)
    )
    high, low = halves(spread)
    out_diag[...] = (nn(fold, high) + nn(fold, low))[:, 0:36]
    diag_store = pltpu.make_async_copy(out_diag, diag_h, sem.at[1])
    diag_store.start()
    for store in stores + [cam_store, diag_store]:
        store.wait()


def per_device(
    features,
    hidden_state,
    edge_source,
    edge_owner,
    edge_target,
    edge_counts,
    corr_weight,
    gate_weight,
    candidate_weight,
    jacobian_weight,
    confidence_weight,
):
    n_edge, n_tile = lax.axis_size("edge"), lax.axis_size("tile")
    edges = hidden_state.shape[0]
    frames, rows, width, chan = features.shape
    slots = max(2, (2 * edges + n_edge - 1) // n_edge)
    assert edges % slots == 0 and edges <= 8 and ASKS + n_edge * slots <= 128
    per = edges // slots
    band = rows * width

    dims = (n_edge, n_tile, edges, frames, rows, width, slots)
    even = (rows + 2 * NEAR + 1) // 2 * 2
    dma = pltpu.SemaphoreType.DMA
    hbm = pl.BlockSpec(memory_space=pl.ANY)

    inputs = (
        ("owner_h", edge_owner[:, 0], hbm),
        ("target_h", edge_target, hbm),
        ("source_h", edge_source, hbm),
        ("count_h", edge_counts, hbm),
        ("feat_h", features.reshape(frames, band, chan), hbm),
        ("hidden_h", hidden_state.reshape(edges, band, chan), hbm),
        ("corr_h", corr_weight, hbm),
        ("gate_w", gate_weight, hbm),
        ("cand_w", candidate_weight, hbm),
        ("jac_h", jacobian_weight.T, hbm),
        ("conf_h", confidence_weight.T, hbm),
    )
    cam_rows, cam_cols = frames * n_edge * 6 // n_tile, frames * 6
    places = (n_edge, cam_rows + cam_cols, 128)
    outputs = (
        ("out_hidden", (edges, band, chan), BF, hbm),
        ("gall_h", (n_edge, 16, 128), F32, hbm),
        ("where_h", places, BF, hbm),
    )
    near, far = len(reach(NEAR, rows)), len(reach(FAR, rows))
    scratch = {
        "owner_s": pltpu.SMEM((edges,), jnp.int32),
        "target_s": pltpu.SMEM((edges,), jnp.int32),
        "source_s": pltpu.SMEM((edges,), jnp.int32),
        "count_s": pltpu.SMEM((1,), jnp.int32),
        "corr_in": pltpu.VMEM(corr_weight.shape, BF),
        "jac_in": pltpu.VMEM(jacobian_weight.shape[::-1], BF),
        "conf_in": pltpu.VMEM(confidence_weight.shape[::-1], BF),
        "row_v": pltpu.VMEM((1, 128), jnp.int32),
        "row_s": pltpu.SMEM((1, 128), jnp.int32),
        "meta_s": pltpu.SMEM((n_edge, 1, 128), jnp.int32),
        "feat": pltpu.VMEM((frames, band, chan), BF),
        "held": pltpu.VMEM((edges, band, chan), BF),
        "ready": pltpu.VMEM((edges, band, chan), BF),
        "where_v": pltpu.VMEM(places, BF),
        "send": pltpu.VMEM(((n_edge - 1) * slots, band, chan), BF),
        "text": pltpu.VMEM((edges, (even + 2 * RADIUS + 3) // 4 * 4 * width, chan), BF),
        "sext": pltpu.VMEM((edges, even * width, chan), BF),
        "hext": pltpu.VMEM((edges, (rows + 2 * NEAR) * width, chan), BF),
        "rext": pltpu.VMEM((per, (rows + 2) * width, chan), BF),
        "x3": pltpu.VMEM((per, (rows + 2 * NEAR) * width, 3 * chan), BF),
        "wh": pltpu.VMEM((3, 3, chan, 2 * chan), BF),
        "wm": pltpu.VMEM((3, 3, chan, 2 * chan), BF),
        "wc": pltpu.VMEM((2, 3, chan, 3 * chan), BF),
        "corr_w": pltpu.VMEM((128, chan), BF),
        "head_w": pltpu.VMEM((64, chan), BF),
        "gpre": pltpu.VMEM((edges, (rows + 2) * width, 2 * chan), F32),
        "upd": pltpu.VMEM((per, band, chan), F32),
        "jall": pltpu.VMEM((128, 2 * band), BF),
        "wall": pltpu.VMEM((128, 2 * band), BF),
        "gpart": pltpu.VMEM((16, 128), BF),
        "gtile": pltpu.VMEM((n_tile, 16, 128), BF),
        "gsum": pltpu.VMEM((16, 128), F32),
        "l_in": dma((5,)),
        "l_w": dma((3,)),
        "l_ints": dma((4,)),
        "l_row": dma,
        "l_meta": dma,
        "l_own": dma,
        "l_sum": dma,
        "l_out": dma,
        "s_meta": dma((n_edge - 1,)),
        "r_meta": dma((n_edge - 1,)),
        "s_feat": dma,
        "r_feat": dma((slots,)),
        "s_gt": dma,
        "r_gt": dma,
        "s_ge": dma,
        "r_ge": dma,
    }
    for s in range(slots):
        scratch[f"text{s}"] = pltpu.VMEM((n_edge - 1, band, chan), BF)
    for key, count, lots in (("h", near, 1), ("s", near, 1), ("t", far, slots)):
        for way in ("up", "dn"):
            scratch[f"s_{key}{way}"] = dma((count,))
            scratch[f"r_{key}{way}"] = dma((count, lots))
    names = [i[0] for i in inputs] + [o[0] for o in outputs] + list(scratch)
    state, gall, where = pl.pallas_call(
        functools.partial(kernel, dims, names),
        out_shape=tuple(jax.ShapeDtypeStruct(shape, kind) for _, shape, kind, _ in outputs),
        in_specs=[spec for _, _, spec in inputs],
        out_specs=tuple(spec for _, _, _, spec in outputs),
        scratch_shapes=list(scratch.values()),
        compiler_params=pltpu.CompilerParams(
            collective_id=0, has_side_effects=True, vmem_limit_bytes=56 * 1024 * 1024
        ),
    )(*[value for _, value, _ in inputs])
    hidden_next, cam, diag = pl.pallas_call(
        functools.partial(assemble, dims),
        out_shape=(
            jax.ShapeDtypeStruct((edges, band, chan), BF),
            jax.ShapeDtypeStruct((cam_rows, cam_cols), F32),
            jax.ShapeDtypeStruct((frames, 36), F32),
        ),
        in_specs=[hbm] * 3,
        out_specs=(hbm,) * 3,
        scratch_shapes=[
            pltpu.VMEM(places, BF),
            pltpu.VMEM((n_edge, 16, 128), F32),
            pltpu.VMEM((cam_rows, cam_cols), F32),
            pltpu.VMEM((frames, 36), F32),
            pltpu.VMEM((edges, band, chan), BF),
            dma((2,)),
            dma((PIECES,)),
        ],
    )(where, gall, state)
    return hidden_next.reshape(hidden_state.shape), cam, diag


def solution(mesh):
    placed = (
        P("edge", "tile", None, None),
        P("edge", "tile", None, None),
        P("edge"),
        P("edge", None),
        P("edge"),
        P("edge"),
        P(),
        P(),
        P(),
        P(),
        P(),
    )
    return jax.shard_map(
        per_device,
        mesh=mesh,
        in_specs=placed,
        out_specs=(P("edge", "tile", None, None), P("tile", "edge"), P("edge", None)),
        check_vma=False,
    )
```

```python
import functools
import types

import jax
import jax.numpy as jnp
from jax import lax
from jax.experimental import pallas as pl
from jax.experimental.pallas import tpu as pltpu
from jax.sharding import PartitionSpec as P

MAPH = 48
WINDOW = 7
RADIUS = WINDOW // 2
NEAR = 2
FAR = RADIUS + NEAR
OWNER, TARGET, SOURCE, SPOT, PLACE, GROUP, REL, ASKS = 0, 8, 16, 24, 32, 40, 48, 64
PIECES = 4
MESH = pl.DeviceIdType.MESH
BF = jnp.bfloat16
F32 = jnp.float32


def nt(a, b):
    return lax.dot_general(a, b, (((1,), (1,)), ((), ())), preferred_element_type=F32)


def nn(a, b):
    return lax.dot_general(a, b, (((1,), (0,)), ((), ())), preferred_element_type=F32)


def iota(shape, dim):
    return lax.broadcasted_iota(jnp.int32, shape, dim)


def sixth(index):
    return jnp.floor((index.astype(F32) + 0.5) * (1.0 / 6.0))


def one_hot(cond):
    return cond.astype(F32).astype(BF)


def each(count, body):
    def step(i, carry):
        body(i)
        return carry

    lax.fori_loop(0, count, step, 0)


def reach(halo, rows):
    return [min(rows, halo - d * rows) for d in range((halo + rows - 1) // rows)]


def kernel(dims, names, *refs):
    n_edge, n_tile, edges, frames, rows, width, slots = dims
    r = types.SimpleNamespace(**dict(zip(names, refs)))
    band = rows * width
    per = edges // slots
    me = lax.axis_index("edge")
    tile = lax.axis_index("tile")
    texts = [getattr(r, f"text{s}") for s in range(slots)]

    ints = [
        pltpu.make_async_copy(r.owner_h, r.owner_s, r.l_ints.at[0]),
        pltpu.make_async_copy(r.target_h, r.target_s, r.l_ints.at[1]),
        pltpu.make_async_copy(r.source_h, r.source_s, r.l_ints.at[2]),
        pltpu.make_async_copy(r.count_h, r.count_s, r.l_ints.at[3]),
    ]
    loads = [
        pltpu.make_async_copy(r.feat_h, r.feat, r.l_in.at[0]),
        pltpu.make_async_copy(
            r.hidden_h, r.hext.at[:, pl.ds(NEAR * width, band)], r.l_in.at[1]
        ),
        pltpu.make_async_copy(r.corr_h, r.corr_in, r.l_in.at[2]),
        pltpu.make_async_copy(r.jac_h, r.jac_in, r.l_in.at[3]),
        pltpu.make_async_copy(r.conf_h, r.conf_in, r.l_in.at[4]),
    ]
    first, second = pl.ds(0, 128), pl.ds(128, 128)
    fills = [
        pltpu.make_async_copy(r.gate_w.at[:, :, first], r.wh, r.l_w.at[0]),
        pltpu.make_async_copy(r.gate_w.at[:, :, second], r.wm, r.l_w.at[1]),
    ]
    for part, at in enumerate((first, second)):
        for b in range(3):
            fills.append(
                pltpu.make_async_copy(
                    r.cand_w.at[:, b, at], r.wc.at[part, :, :, pl.ds(b * 128, 128)], r.l_w.at[2]
                )
            )
    filled = fills[:2] + [pltpu.make_async_copy(r.wc, r.wc, r.l_w.at[2])]
    for load in ints:
        load.start()

    barrier = pltpu.get_barrier_semaphore()
    for rel in range(1, n_edge):
        pl.semaphore_signal(
            barrier, inc=1, device_id=((me + rel) % n_edge, tile), device_id_type=MESH
        )
    for rel in range(1, n_tile):
        pl.semaphore_signal(
            barrier, inc=1, device_id=(me, (tile + rel) % n_tile), device_id_type=MESH
        )

    for load in loads + fills:
        load.start()

    for load in ints:
        load.wait()
    owner = [r.owner_s[e] for e in range(edges)]
    rel_of = [(owner[e] - me + n_edge) % n_edge for e in range(edges)]
    rank, group = [], []
    for e in range(edges):
        before = jnp.int32(0)
        for k in range(e):
            before = before + (owner[k] == owner[e]).astype(jnp.int32)
        rank.append(jnp.minimum(before, slots - 1))
        group.append(jnp.where(rel_of[e] == 0, 0, rank[e] + 1))
    lane = iota((1, 128), 1)
    row = jnp.zeros((1, 128), jnp.int32)
    for e in range(edges):
        spot = jnp.int32(0)
        for k in range(edges):
            if k < e:
                spot = spot + (group[k] <= group[e]).astype(jnp.int32)
            elif k > e:
                spot = spot + (group[k] < group[e]).astype(jnp.int32)
        goal = r.target_s[e]
        fields = (
            (OWNER, owner[e]),
            (TARGET, goal),
            (SOURCE, r.source_s[e]),
            (PLACE, jnp.int32(e)),
            (GROUP, group[e]),
            (REL, rel_of[e]),
        )
        for base, value in fields:
            row = jnp.where(lane == base + spot, value, row)
        row = jnp.where(lane == SPOT + e, spot, row)
        row = jnp.where(lane == ASKS + rel_of[e] * slots + rank[e], goal, row)
    r.row_v[...] = row
    mine = pltpu.make_async_copy(r.row_v, r.row_s, r.l_row)
    mine.start()

    pl.semaphore_wait(barrier, n_edge + n_tile - 2)

    def remote(src, dst, send_sem, recv_sem, edge_id, tile_id):
        return pltpu.make_async_remote_copy(
            src_ref=src,
            dst_ref=dst,
            send_sem=send_sem,
            recv_sem=recv_sem,
            device_id=(edge_id, tile_id),
            device_id_type=MESH,
        )

    def meta_copy(rel):
        return remote(
            r.row_v, r.meta_s.at[me], r.s_meta.at[rel - 1], r.r_meta.at[rel - 1],
            (me + rel) % n_edge, tile,
        )

    others = n_edge - 1
    for rel in range(1, n_edge):
        meta_copy(rel).start()
    own_row = pltpu.make_async_copy(r.row_v, r.meta_s.at[me], r.l_own)
    own_row.start()

    class Halo:
        def __init__(self, halo, lot, buf, source, sems):
            self.halo, self.lot, self.buf, self.source, self.sems = halo, lot, buf, source, sems
            self.counts = reach(halo, rows)

        def copies(self, i, lot):
            which = pl.ds(i * lot, lot)
            for d, count in enumerate(self.counts):
                far, lines = d + 1, count * width
                s_up, r_up, s_dn, r_dn = self.sems
                up = remote(
                    self.source(which, 0, lines),
                    self.buf.at[which, pl.ds((self.halo + far * rows) * width, lines)],
                    s_up.at[d], r_up.at[d, i], me, tile - far,
                )
                dn = remote(
                    self.source(which, band - lines, lines),
                    self.buf.at[which, pl.ds((self.halo - d * rows - count) * width, lines)],
                    s_dn.at[d], r_dn.at[d, i], me, tile + far,
                )
                yield tile >= far, tile + far < n_tile, up, dn

        def start(self, i):
            for above, below, up, dn in self.copies(i, self.lot):
                pl.when(above)(up.start)
                pl.when(below)(dn.start)

        def received(self, i):
            for above, below, up, dn in self.copies(i, self.lot):
                pl.when(below)(up.wait_recv)
                pl.when(above)(dn.wait_recv)

        def sent(self):
            for above, below, up, dn in self.copies(0, edges):
                pl.when(above)(up.wait_send)
                pl.when(below)(dn.wait_send)

        def clear(self):
            for d, count in enumerate(self.counts):
                far, lines = d + 1, count * width
                zero = jnp.zeros((lines, 128), BF)
                top = (self.halo - d * rows - count) * width
                low = (self.halo + far * rows) * width

                @pl.when(tile < far)
                def _():
                    def clear_top(e):
                        self.buf[e, pl.ds(top, lines)] = zero

                    each(edges, clear_top)

                @pl.when(tile + far >= n_tile)
                def _():
                    def clear_low(e):
                        self.buf[e, pl.ds(low, lines)] = zero

                    each(edges, clear_low)

            used = (rows + 2 * self.halo) * width
            spare = self.buf.shape[1] - used
            if spare:

                def clear_pad(e):
                    self.buf[e, pl.ds(used, spare)] = jnp.zeros((spare, 128), BF)

                each(edges, clear_pad)

    def inner(buf, halo):
        return lambda which, at, lines: buf.at[which, pl.ds(halo * width + at, lines)]

    hid = Halo(
        NEAR, edges, r.hext, lambda which, at, lines: r.hidden_h.at[which, pl.ds(at, lines)],
        (r.s_hup, r.r_hup, r.s_hdn, r.r_hdn),
    )
    src = Halo(
        NEAR, edges, r.sext, inner(r.sext, NEAR), (r.s_sup, r.r_sup, r.s_sdn, r.r_sdn)
    )
    txt = Halo(FAR, per, r.text, inner(r.text, FAR), (r.s_tup, r.r_tup, r.s_tdn, r.r_tdn))

    loads[0].wait()

    turns = [n_edge // 2]
    turns += [n_edge - k - (n_edge - 2 * k) * (me % 2) for k in range(1, (n_edge + 1) // 2)]
    turns += [k + (n_edge - 2 * k) * (me % 2) for k in range(1, (n_edge + 1) // 2)]

    def feat_copy(rel, s):
        return remote(
            r.send.at[s * others + rel - 1], texts[s].at[rel - 1],
            r.s_feat, r.r_feat.at[s], (me - rel + n_edge) % n_edge, tile,
        )

    def feat_group(s):
        return remote(
            r.send.at[pl.ds(s * others, others)], texts[s],
            r.s_feat, r.r_feat.at[s], (me + 1) % n_edge, tile,
        )

    for s in range(slots):
        for rel in turns:
            peer = (me - rel + n_edge) % n_edge
            if s == 0:
                remote(
                    r.row_v, r.meta_s.at[peer], r.s_meta.at[rel - 1], r.r_meta.at[rel - 1],
                    (me + rel) % n_edge, tile,
                ).wait_recv()
            r.send[s * others + rel - 1] = r.feat[r.meta_s[peer, 0, ASKS + rel * slots + s]]
            feat_copy(rel, s).start()

    hid.start(0)
    mine.wait()

    def take_source(e):
        r.sext[e, pl.ds(NEAR * width, band)] = r.feat[r.row_s[0, SOURCE + e]]

    each(edges, take_source)
    src.start(0)
    for halo in (hid, src, txt):
        halo.clear()

    for load in loads[2:]:
        load.wait()

    spot = (iota((128, 64), 0) + 4) & 127
    along = ((spot >> 3) & 3) * 2 + (spot >> 6) - ((spot >> 5) & 1)
    across = WINDOW - 1 - (spot & 7)
    fits = (across >= 0) & (along >= 0) & (along < WINDOW)
    pick = (iota((128, 64), 1) == along * WINDOW + across) & fits
    lookup = jnp.concatenate(
        [r.corr_in[...].astype(F32), jnp.zeros((64 - WINDOW * WINDOW, 128), F32)], axis=0
    ).astype(BF)
    r.corr_w[...] = nn(one_hot(pick), lookup).astype(BF)

    place12 = iota((32, 64), 0)
    which = place12 >> 4
    within = place12 & 15
    name12 = iota((32, 64), 1)
    pick_j = (within < 12) & (name12 == which * 12 + within)
    padded_jac = jnp.concatenate(
        [r.jac_in[...].astype(F32), jnp.zeros((40, 128), F32)], axis=0
    ).astype(BF)
    conf_wide = r.conf_in[...].astype(F32)
    tall = iota((32, 128), 0)
    conf_rows = jnp.where(
        tall < 16,
        jnp.broadcast_to(conf_wide[0:1], (32, 128)),
        jnp.broadcast_to(conf_wide[1:2], (32, 128)),
    )
    r.head_w[...] = jnp.concatenate(
        [nn(one_hot(pick_j), padded_jac), jnp.where((tall & 15) < 12, conf_rows, 0.0)], axis=0
    ).astype(BF)

    def nudge(wide, by):
        lines = wide.shape[0]
        column = iota((lines, 128), 0) & (width - 1)
        edge = 0 if by == 1 else width - 1
        return jnp.where(column == edge, 0.0, pltpu.roll(wide, by % lines, 0))

    def spread(value, out):
        lines = value.shape[0]
        wide = value.astype(F32)
        out[0:lines, 0:128] = nudge(wide, 1).astype(BF)
        out[0:lines, 128:256] = value.astype(BF)
        out[0:lines, 256:384] = nudge(wide, -1).astype(BF)

    def windows(x3, q, out_rows):
        size = out_rows * width
        return jnp.concatenate([x3[q, a * width : a * width + size] for a in range(3)], axis=1)

    wide_band = (rows + 2) * width

    def state_part(p):
        for q in range(per):
            e = p * per + q
            spread(r.hext[r.row_s[0, PLACE + e]], r.x3.at[q])
            r.gpre[e] = nn(windows(r.x3, q, rows + 2), r.wh[...].reshape(9 * 128, 256))

    loads[1].wait()
    for fill in filled:
        fill.wait()
    flip_row, flip_col = iota((2 * width, 2 * width), 0), iota((2 * width, 2 * width), 1)
    flip = one_hot(
        (flip_row // width == flip_col // width)
        & ((flip_row & (width - 1)) + (flip_col & (width - 1)) == width - 1)
    )

    def take_target(e, upto):
        value = r.feat[r.row_s[0, TARGET + e]]
        at = jnp.maximum(r.row_s[0, REL + e] - 1, 0)
        for s in range(upto + 1):
            value = jnp.where(r.row_s[0, GROUP + e] == s + 1, texts[s][at], value)
        for first in range(0, band, 2 * width):
            count = min(2 * width, band - first)
            r.text[e, pl.ds(FAR * width + first, count)] = nn(
                flip[0:count, 0:count], value[first : first + count]
            ).astype(BF)

    def take(s):
        feat_group(s).wait_recv()
        for q in range(per):
            take_target(s * per + q, s)
        txt.start(s)

    hid.received(0)
    each(slots // 2, state_part)
    take(0)
    each(slots - slots // 2, lambda p: state_part(p + slots // 2))
    src.received(0)

    own_row.wait()
    cam_cols = frames * 6
    cam_rows = r.where_v.shape[1] - cam_cols
    part = iota((cam_rows + cam_cols, 128), 0)
    index = jnp.where(part < cam_rows, part + tile * cam_rows, part - cam_rows + me * cam_cols)
    inside = lane & 15
    digit = jnp.where(inside < 6, inside, inside - 6)

    def place(j):
        spots = jnp.full((1, 128), -1, jnp.int32)
        for e in range(edges):
            source = (j * frames + r.meta_s[j, 0, SOURCE + e]) * 6
            target = (r.meta_s[j, 0, OWNER + e] * frames + r.meta_s[j, 0, TARGET + e]) * 6
            here = jnp.where(inside < 6, source, target) + digit
            spots = jnp.where(((lane >> 4) == e) & (inside < 12), here, spots)
        r.where_v[j] = one_hot(index == spots)

    each(n_edge, place)
    tables = pltpu.make_async_copy(r.where_v, r.where_h, r.l_meta)
    tables.start()

    lane_w = (iota((width, 128), 1) + 4) & 127
    col_w = iota((width, 128), 0) + RADIUS - (lane_w & 7)
    in_map = (col_w >= 0) & (col_w < width) & ((lane_w & 7) < WINDOW)
    scaled = [
        jnp.where(in_map & (((lane_w >> 5) & 1) == par), 128.0 ** (-0.5), 0.0) for par in range(2)
    ]
    slot_w = (lane_w >> 3) & 3
    pairs_of = (rows + 2 * NEAR + 1) // 2
    quads_of = r.text.shape[1] // (4 * width)
    used_rows = (rows + 2 * NEAR) * width

    def motion_of(e, q):
        tables, starts = [], []
        for m in range(quads_of):
            first, last = max(0, 2 * m - 3), min(pairs_of - 1, 2 * m + 1)
            starts.append(first)
            tables.append(
                nt(
                    r.sext[e, pl.ds(2 * first * width, 2 * (last - first + 1) * width)],
                    r.text[e, pl.ds(4 * m * width, 4 * width)],
                )
            )
        lines = []
        for k in range(pairs_of):
            for par in range(2):
                found = None
                for g in range(4):
                    m, h = divmod(k + g, 2)
                    at = (2 * (k - starts[m]) + par) * width
                    piece = tables[m][at : at + width, h * 128 : (h + 1) * 128]
                    moved = pltpu.roll(
                        piece, width + 8 * g + 32 * par, 1, stride=1, stride_axis=0
                    )
                    found = moved if g == 0 else jnp.where(slot_w == g, moved, found)
                lines.append((found * scaled[par]).astype(BF))
        value = nn(jnp.concatenate(lines, axis=0), r.corr_w[...])
        spread(jnp.maximum(value[0:used_rows], 0.0), r.x3.at[q])

    def update(p):
        txt.received(p)
        for q in range(per):
            motion_of(p * per + q, q)
            e = p * per + q
            before = r.gpre[e] + nn(windows(r.x3, q, rows + 2), r.wm[...].reshape(9 * 128, 256))
            r.upd[q] = 0.5 * jnp.tanh(0.5 * before[width : width + band, 0:128]) + 0.5
            reset = 0.5 * jnp.tanh(0.5 * before[:, 128:256]) + 0.5
            state = r.hext[r.row_s[0, PLACE + e], pl.ds(width, wide_band)].astype(F32)
            r.rext[q] = (reset * state).astype(BF)
        for q in range(per):
            e = p * per + q
            part = nn(
                jnp.concatenate(
                    [r.rext[q, a * width : a * width + band] for a in range(3)]
                    + [
                        r.x3[q, (a + 1) * width : (a + 1) * width + band, 128:256]
                        for a in range(3)
                    ],
                    axis=1,
                ),
                r.wc[...].reshape(6 * 128, 384),
            )
            candidate = jnp.tanh(
                nudge(part[:, 0:128], 1) + part[:, 128:256] + nudge(part[:, 256:384], -1)
            )
            gate = r.upd[q]
            place = r.row_s[0, PLACE + e]
            state = r.hext[place, pl.ds(NEAR * width, band)]
            fresh = ((1.0 - gate) * state.astype(F32) + gate * candidate).astype(BF)
            used = (place < r.count_s[0]).astype(F32)
            live = jnp.full((band, 128), used) > 0.5
            r.held[e] = jnp.where(live, fresh, state)
            heads = nt(r.head_w[...], fresh)
            jac = heads[0:32]
            weighted = jac * jax.nn.softplus(heads[32:64])
            at16 = pl.ds(pl.multiple_of(e * 16, 16), 16)
            r.jall[at16] = jnp.concatenate([jac[0:16], jac[16:32]], axis=1).astype(BF)
            r.wall[at16] = jnp.concatenate([weighted[0:16], weighted[16:32]], axis=1).astype(BF)

    def stage(p):
        for s in range(1, slots):

            @pl.when(p == s - 1)
            def _():
                take(s)

        update(p)

    each(slots, stage)
    same = (iota((128, 128), 0) >> 4) == (iota((128, 128), 1) >> 4)
    square = jnp.where(same, nt(r.wall[...], r.jall[...]), 0.0)
    blocks = square[0:16]
    for e in range(1, edges):
        blocks = blocks + square[e * 16 : (e + 1) * 16]
    blocks = blocks * (1.0 / (MAPH * width))
    of = iota((16, 128), 1) >> 4
    for e in range(edges):
        used = (r.row_s[0, PLACE + e] < r.count_s[0]).astype(jnp.int32)
        blocks = jnp.where((of == e) & (jnp.full((16, 128), used) == 0), 0.0, blocks)
    r.gpart[...] = blocks

    def tile_copy(rel):
        return remote(
            r.gpart, r.gtile.at[tile], r.s_gt, r.r_gt, me, (tile + rel) % n_tile
        )

    def all_tiles():
        some = r.gtile.at[pl.ds(0, n_tile - 1)]
        return remote(some, some, r.s_gt, r.r_gt, me, (tile + 1) % n_tile)

    for rel in range(1, n_tile):
        tile_copy(rel).start()
    r.gtile[tile] = r.gpart[...]

    def put_back(e):
        r.ready[e] = r.held[r.row_s[0, SPOT + e]]

    each(edges, put_back)
    store = pltpu.make_async_copy(r.ready, r.out_hidden, r.l_out)
    store.start()
    all_tiles().wait_recv()
    total = r.gtile[0]
    for k in range(1, n_tile):
        total = total + r.gtile[k]
    r.gsum[...] = total

    def edge_copy(rel):
        return remote(r.gsum, r.gall_h.at[me], r.s_ge, r.r_ge, (me + rel) % n_edge, tile)

    def all_edges():
        some = r.gall_h.at[pl.ds(0, others)]
        return remote(some, some, r.s_ge, r.r_ge, (me + 1) % n_edge, tile)

    for rel in range(1, n_edge):
        edge_copy(rel).start()
    own_sum = pltpu.make_async_copy(r.gsum, r.gall_h.at[me], r.l_sum)
    own_sum.start()
    all_edges().wait_recv()

    own_sum.wait()
    store.wait()
    tables.wait()
    for rel in range(1, n_edge):
        meta_copy(rel).wait_send()
    for s in range(slots):
        feat_group(s).wait_send()
    all_tiles().wait_send()
    all_edges().wait_send()
    for halo in (hid, src, txt):
        halo.sent()


def halves(value):
    high = value.astype(BF)
    return high, (value - high.astype(F32)).astype(BF)


def assemble(
    dims, where_h, gall_h, hidden_h, out_hidden, cam_h, diag_h, where_v, gall, out_cam, out_diag, held,
    sem, held_sem,
):
    n_edge, n_tile, edges, frames, rows, width, slots = dims
    me = lax.axis_index("edge")
    tile = lax.axis_index("tile")
    loads = [
        pltpu.make_async_copy(gall_h, gall, sem.at[0]),
        pltpu.make_async_copy(where_h, where_v, sem.at[1]),
    ]
    pieces = [pl.ds(i * (edges // PIECES), edges // PIECES) for i in range(PIECES)]
    fetches = [
        pltpu.make_async_copy(hidden_h.at[p], held.at[p], held_sem.at[i])
        for i, p in enumerate(pieces)
    ]
    stores = [
        pltpu.make_async_copy(held.at[p], out_hidden.at[p], held_sem.at[i])
        for i, p in enumerate(pieces)
    ]
    for load in loads + fetches:
        load.start()
    cam_rows, cam_cols = out_cam.shape
    same = (iota((128, 128), 0) >> 4) == (iota((128, 128), 1) >> 4)
    for load in loads:
        load.wait()
    lefts, lows, rights = [], [], []
    for j in range(n_edge):
        left = where_v[j]
        stack = jnp.where(same, jnp.concatenate([gall[j]] * 8, axis=0), 0.0)
        picked = nn(
            jnp.concatenate([left, left], axis=1), jnp.concatenate(halves(stack), axis=0)
        )
        high, low = halves(picked)
        lefts.append(high)
        lows.append(low)
        rights.append(left[cam_rows:])
    placed = nt(jnp.concatenate(lefts + lows, axis=1), jnp.concatenate(rights + rights, axis=1))
    for fetch, store in zip(fetches, stores):
        fetch.wait()
        store.start()
    cam = placed[0:cam_rows]
    row_frame = sixth(iota((cam_rows, cam_cols), 0) + tile * cam_rows)
    col_frame = sixth(iota((cam_rows, cam_cols), 1) + me * cam_cols)
    out_cam[...] = jnp.where(row_frame == col_frame, 0.0, cam)
    cam_store = pltpu.make_async_copy(out_cam, cam_h, sem.at[0])
    cam_store.start()
    own = placed[cam_rows:]
    own_row = sixth(iota((cam_cols, cam_cols), 0))
    own_col = sixth(iota((cam_cols, cam_cols), 1))
    own = jnp.where(own_row == own_col, own, 0.0)
    wide_row = iota((cam_cols, 128), 0)
    wide_lane = iota((cam_cols, 128), 1)
    row_in = wide_row.astype(F32) - 6.0 * sixth(wide_row)
    lane_of = sixth(wide_lane)
    lane_in = wide_lane.astype(F32) - 6.0 * lane_of
    gather = one_hot(row_in == lane_in)
    high, low = halves(own)
    spread = jnp.where(row_in == lane_of, nn(high, gather) + nn(low, gather), 0.0)
    fold = one_hot(
        sixth(iota((frames, cam_cols), 1)) == iota((frames, cam_cols), 0).astype(F32)
    )
    high, low = halves(spread)
    out_diag[...] = (nn(fold, high) + nn(fold, low))[:, 0:36]
    diag_store = pltpu.make_async_copy(out_diag, diag_h, sem.at[1])
    diag_store.start()
    for store in stores + [cam_store, diag_store]:
        store.wait()


def per_device(
    features,
    hidden_state,
    edge_source,
    edge_owner,
    edge_target,
    edge_counts,
    corr_weight,
    gate_weight,
    candidate_weight,
    jacobian_weight,
    confidence_weight,
):
    n_edge, n_tile = lax.axis_size("edge"), lax.axis_size("tile")
    edges = hidden_state.shape[0]
    frames, rows, width, chan = features.shape
    slots = max(2, (2 * edges + n_edge - 1) // n_edge)
    assert edges % slots == 0 and edges <= 8 and ASKS + n_edge * slots <= 128
    per = edges // slots
    band = rows * width

    dims = (n_edge, n_tile, edges, frames, rows, width, slots)
    even = (rows + 2 * NEAR + 1) // 2 * 2
    dma = pltpu.SemaphoreType.DMA
    hbm = pl.BlockSpec(memory_space=pl.ANY)

    inputs = (
        ("owner_h", edge_owner[:, 0], hbm),
        ("target_h", edge_target, hbm),
        ("source_h", edge_source, hbm),
        ("count_h", edge_counts, hbm),
        ("feat_h", features.reshape(frames, band, chan), hbm),
        ("hidden_h", hidden_state.reshape(edges, band, chan), hbm),
        ("corr_h", corr_weight, hbm),
        ("gate_w", gate_weight, hbm),
        ("cand_w", candidate_weight, hbm),
        ("jac_h", jacobian_weight.T, hbm),
        ("conf_h", confidence_weight.T, hbm),
    )
    cam_rows, cam_cols = frames * n_edge * 6 // n_tile, frames * 6
    places = (n_edge, cam_rows + cam_cols, 128)
    outputs = (
        ("out_hidden", (edges, band, chan), BF, hbm),
        ("gall_h", (n_edge, 16, 128), F32, hbm),
        ("where_h", places, BF, hbm),
    )
    near, far = len(reach(NEAR, rows)), len(reach(FAR, rows))
    scratch = {
        "owner_s": pltpu.SMEM((edges,), jnp.int32),
        "target_s": pltpu.SMEM((edges,), jnp.int32),
        "source_s": pltpu.SMEM((edges,), jnp.int32),
        "count_s": pltpu.SMEM((1,), jnp.int32),
        "corr_in": pltpu.VMEM(corr_weight.shape, BF),
        "jac_in": pltpu.VMEM(jacobian_weight.shape[::-1], BF),
        "conf_in": pltpu.VMEM(confidence_weight.shape[::-1], BF),
        "row_v": pltpu.VMEM((1, 128), jnp.int32),
        "row_s": pltpu.SMEM((1, 128), jnp.int32),
        "meta_s": pltpu.SMEM((n_edge, 1, 128), jnp.int32),
        "feat": pltpu.VMEM((frames, band, chan), BF),
        "held": pltpu.VMEM((edges, band, chan), BF),
        "ready": pltpu.VMEM((edges, band, chan), BF),
        "where_v": pltpu.VMEM(places, BF),
        "send": pltpu.VMEM(((n_edge - 1) * slots, band, chan), BF),
        "text": pltpu.VMEM((edges, (even + 2 * RADIUS + 3) // 4 * 4 * width, chan), BF),
        "sext": pltpu.VMEM((edges, even * width, chan), BF),
        "hext": pltpu.VMEM((edges, (rows + 2 * NEAR) * width, chan), BF),
        "rext": pltpu.VMEM((per, (rows + 2) * width, chan), BF),
        "x3": pltpu.VMEM((per, (rows + 2 * NEAR) * width, 3 * chan), BF),
        "wh": pltpu.VMEM((3, 3, chan, 2 * chan), BF),
        "wm": pltpu.VMEM((3, 3, chan, 2 * chan), BF),
        "wc": pltpu.VMEM((2, 3, chan, 3 * chan), BF),
        "corr_w": pltpu.VMEM((128, chan), BF),
        "head_w": pltpu.VMEM((64, chan), BF),
        "gpre": pltpu.VMEM((edges, (rows + 2) * width, 2 * chan), F32),
        "upd": pltpu.VMEM((per, band, chan), F32),
        "jall": pltpu.VMEM((128, 2 * band), BF),
        "wall": pltpu.VMEM((128, 2 * band), BF),
        "gpart": pltpu.VMEM((16, 128), F32),
        "gtile": pltpu.VMEM((n_tile, 16, 128), F32),
        "gsum": pltpu.VMEM((16, 128), F32),
        "l_in": dma((5,)),
        "l_w": dma((3,)),
        "l_ints": dma((4,)),
        "l_row": dma,
        "l_meta": dma,
        "l_own": dma,
        "l_sum": dma,
        "l_out": dma,
        "s_meta": dma((n_edge - 1,)),
        "r_meta": dma((n_edge - 1,)),
        "s_feat": dma,
        "r_feat": dma((slots,)),
        "s_gt": dma,
        "r_gt": dma,
        "s_ge": dma,
        "r_ge": dma,
    }
    for s in range(slots):
        scratch[f"text{s}"] = pltpu.VMEM((n_edge - 1, band, chan), BF)
    for key, count, lots in (("h", near, 1), ("s", near, 1), ("t", far, slots)):
        for way in ("up", "dn"):
            scratch[f"s_{key}{way}"] = dma((count,))
            scratch[f"r_{key}{way}"] = dma((count, lots))
    names = [i[0] for i in inputs] + [o[0] for o in outputs] + list(scratch)
    state, gall, where = pl.pallas_call(
        functools.partial(kernel, dims, names),
        out_shape=tuple(jax.ShapeDtypeStruct(shape, kind) for _, shape, kind, _ in outputs),
        in_specs=[spec for _, _, spec in inputs],
        out_specs=tuple(spec for _, _, _, spec in outputs),
        scratch_shapes=list(scratch.values()),
        compiler_params=pltpu.CompilerParams(
            collective_id=0, has_side_effects=True, vmem_limit_bytes=56 * 1024 * 1024
        ),
    )(*[value for _, value, _ in inputs])
    hidden_next, cam, diag = pl.pallas_call(
        functools.partial(assemble, dims),
        out_shape=(
            jax.ShapeDtypeStruct((edges, band, chan), BF),
            jax.ShapeDtypeStruct((cam_rows, cam_cols), F32),
            jax.ShapeDtypeStruct((frames, 36), F32),
        ),
        in_specs=[hbm] * 3,
        out_specs=(hbm,) * 3,
        scratch_shapes=[
            pltpu.VMEM(places, BF),
            pltpu.VMEM((n_edge, 16, 128), F32),
            pltpu.VMEM((cam_rows, cam_cols), F32),
            pltpu.VMEM((frames, 36), F32),
            pltpu.VMEM((edges, band, chan), BF),
            dma((2,)),
            dma((PIECES,)),
        ],
    )(where, gall, state)
    return hidden_next.reshape(hidden_state.shape), cam, diag


def solution(mesh):
    placed = (
        P("edge", "tile", None, None),
        P("edge", "tile", None, None),
        P("edge"),
        P("edge", None),
        P("edge"),
        P("edge"),
        P(),
        P(),
        P(),
        P(),
        P(),
    )
    return jax.shard_map(
        per_device,
        mesh=mesh,
        in_specs=placed,
        out_specs=(P("edge", "tile", None, None), P("tile", "edge"), P("edge", None)),
        check_vma=False,
    )
```
